128 devices in a mesh: ctx: 8 (over y, x_lo), tp: 16 (over x_hi, z, core).
Axes of the slice: x: 4 (x_hi: 2, x_lo: 2; x = x_hi * 2 + x_lo), y: 4, z: 4, core: 2. Of those that a mesh axis runs over, the one named last changes fastest.
Arguments:
- hidden_input: bfloat16 [3072, 8192], P('ctx'), may hold values from -6 to 6
- output_cotangent: bfloat16 [3072, 8192], P('ctx', 'tp'), may hold values from -6 to 6
- query_projection: bfloat16 [8192, 4096], P(None, 'tp')
- key_value_projection: bfloat16 [8192, 2048], P(None, 'tp')
- output_projection: bfloat16 [4096, 8192], P('tp'), may hold values from -0.09375 to 0.09375
- adapter_qkv_down_store: bfloat16 [32, 8192, 192], P('ctx', 'tp'), may hold values from -0.0625 to 0.0625
- adapter_query_up: bfloat16 [32, 64, 4096], P('ctx', None, 'tp'), may hold values from -0.375 to 0.375
- adapter_key_value_up: bfloat16 [32, 64, 2048], P('ctx', None, 'tp'), may hold values from -0.375 to 0.375
- adapter_output_down: bfloat16 [32, 4096, 64], P('ctx', 'tp'), may hold values from -0.1875 to 0.1875
- adapter_output_up: bfloat16 [32, 64, 8192], P('ctx', None, 'tp'), may hold values from -0.75 to 0.75
- crop_token_length: int32 [4], replicated, may hold values from 1 to 2688, 3072 in all
- tenant_per_block: int32 [24], replicated, may hold values from 0 to 31, as said below
- tenant_store_row: int32 [32], replicated, may hold values from 0 to 31, as said below
Outputs:
- output: bfloat16 [3072, 8192], P('ctx', 'tp')
- hidden_input_gradient: bfloat16 [3072, 8192], P('ctx', 'tp')
- grad_down_qkv: float32 [32, 8192, 192], P('ctx', 'tp')
- grad_up_q: float32 [32, 64, 4096], P('ctx', None, 'tp')
- grad_up_kv: float32 [32, 64, 2048], P('ctx', None, 'tp')
- grad_down_o: float32 [32, 4096, 64], P('ctx', 'tp')
- grad_up_o: float32 [32, 64, 8192], P('ctx', None, 'tp')
The draws below stay inside these ranges and needn't reach their ends.
Inputs may be any that keep to these rules, and one draw needn't show every extreme that they name: A permutation: tenant t's adapters are at store row tenant_store_row[t]; rows j * 4 to (j + 1) * 4 - 1 belong to owner j. `tenant_per_block`: of the 3 blocks of one index of ctx, at most 1 name tenants of one owner, and some owner is named that often.
All inputs are finite; a program needn't handle non-finite values.
Results may differ from the reference program's by a relative error of at most 0.038.
Values may be sent and summed in bfloat16 or wider, within the bound.
A program may use at most 128 MiB of HBM per device.

```python
import math
import jax
import jax.numpy as jnp
import numpy as np
from jax import lax

MODEL_WIDTH = 8192
HEAD_SIZE = 128
KEY_VALUE_HEADS = 8
QUERY_HEADS = 32
ADAPTER_RANK = 64
BLK = 128
TEN_OWN = 4
NSEG = 4
TOKENS = 3072
TENANT_COUNT = 32
TB = 3
GROUP = 4
HEAD_GROUP = 2
COL_GROUP = 512
KV_GROUP = 128
SEG_MOST = 2688
N_TP = 16


def draw_hidden_input(key, part):
    base_values = jax.random.normal(jax.random.fold_in(key, 31), (TOKENS, MODEL_WIDTH), jnp.float32)
    return jnp.clip(base_values, -6.0, 6.0).astype(jnp.bfloat16)


def projection_normal(key, tag, array_shape):
    base_values = jax.random.normal(jax.random.fold_in(key, tag), array_shape, jnp.float32)
    return jnp.clip(base_values, -6.0, 6.0) * MODEL_WIDTH ** (-0.5)


def draw_query_projection(key, part):
    return projection_normal(key, 41, (MODEL_WIDTH, QUERY_HEADS * HEAD_SIZE)).astype(jnp.bfloat16)


def draw_key_value_projection(key, part):
    fresh_values = projection_normal(key, 42, (MODEL_WIDTH, KEY_VALUE_HEADS, 2, HEAD_SIZE))
    return fresh_values.reshape(MODEL_WIDTH, 2 * KEY_VALUE_HEADS * HEAD_SIZE).astype(jnp.bfloat16)


def store_order(key):
    return jax.random.permutation(jax.random.fold_in(key, 51), TENANT_COUNT).astype(jnp.int32)


def draw_tenant_store_row(key, part):
    return store_order(key)


def force_first(orders, picks, shard_no, target_row):
    target_owner = target_row // TEN_OWN
    order_row = orders[shard_no]
    moved = jnp.where(order_row == target_owner, order_row[0], order_row)
    moved = moved.at[0].set(target_owner)
    orders = orders.at[shard_no].set(moved)
    picks = picks.at[shard_no, 0].set(target_row % TEN_OWN)
    return (orders, picks)


def draw_tenant_per_block(key, part):
    rows_of = store_order(key)
    tenant_of_row = jnp.argsort(rows_of).astype(jnp.int32)
    shard_count = TENANT_COUNT // TEN_OWN
    shard_keys = jax.random.split(jax.random.fold_in(key, 52), shard_count)
    orders = jax.vmap(lambda key_one: jax.random.permutation(key_one, shard_count))(shard_keys).astype(jnp.int32)
    picks = jax.random.randint(jax.random.fold_in(key, 53), (shard_count, TB), 0, TEN_OWN).astype(jnp.int32)
    orders, picks = force_first(orders, picks, 0, rows_of[TENANT_COUNT - 1])
    orders, picks = force_first(orders, picks, 1, rows_of[0])
    slot_ids = jnp.arange(TB, dtype=jnp.int32) % shard_count
    owners = orders[:, slot_ids].astype(jnp.int32)
    store_rows = owners * TEN_OWN + picks
    return tenant_of_row[store_rows.reshape(-1)].astype(jnp.int32)


def steps_of(key, extent, pieces, smallest, top_value):
    level = 1.0
    for dim, shards_of in pieces:
        steps = jax.random.uniform(jax.random.fold_in(jax.random.fold_in(key, 6), dim), (shards_of,), jnp.float32, smallest / len(pieces), top_value / len(pieces))
        level = level * jnp.repeat(jnp.exp(steps), extent[dim] // shards_of).reshape((-1,) + (1,) * (len(extent) - 1 - dim))
    return level


def length_profile(amount, total, most, slope):
    portions = [(1 << 20) // math.isqrt(rank ** slope) + 1 for rank in range(2, amount + 1)]
    rest, counts = total - most - (amount - 1), [1] * (amount - 1)
    while rest > 0:
        free = [i for i in range(amount - 1) if counts[i] < most]
        mass, budget = sum([portions[i] for i in free]), rest
        for i in free:
            addition = min(most - counts[i], max(1, budget * portions[i] // mass), rest)
            counts[i] = counts[i] + addition
            rest = rest - addition
    return np.array([most] + counts)


def uneven_parts(stream_key, count, total, bound, skew):
    if count == 2:
        one = jax.random.randint(stream_key, (), max(1, total - bound), min(bound, total - 1) + 1)
        return jnp.stack([one, total - one])
    tallies = jnp.asarray(length_profile(count, total, bound, skew), jnp.int32)
    couples = (count - 1) // 2
    source_of, receiver = tallies[1:1 + 2 * couples:2], tallies[2:2 + 2 * couples:2]
    slack = jnp.minimum(source_of - 1, bound - receiver)
    passed = jax.random.randint(jax.random.fold_in(stream_key, 1), (couples,), 0, 1 << 20) % (slack + 1)
    tallies = tallies.at[1:1 + 2 * couples:2].set(source_of - passed).at[2:2 + 2 * couples:2].set(receiver + passed)
    return tallies[jax.random.permutation(jax.random.fold_in(stream_key, 2), count)]


def gaussian(rng, extent, width, limit, pieces=(), kind=jnp.bfloat16):
    result = width * jax.random.normal(rng, extent, jnp.float32)
    if pieces:
        result = result * steps_of(rng, extent, pieces, -0.22, 0.18)
    return jnp.clip(result, -limit, limit).astype(kind)


def setup_inputs(seed: int = 0) -> dict:
    streams_of = jax.random.split(jax.random.key(seed), 14)
    hidden_input = draw_hidden_input(jax.random.fold_in(streams_of[13], 71), 0)
    output_cotangent = gaussian(streams_of[1], (TOKENS, MODEL_WIDTH), 1.0, 6.0, ((0, 8), (1, 16)))
    query_projection = draw_query_projection(jax.random.fold_in(streams_of[13], 71), 0)
    key_value_projection = draw_key_value_projection(jax.random.fold_in(streams_of[13], 71), 0)
    output_projection = gaussian(streams_of[4], (QUERY_HEADS * HEAD_SIZE, MODEL_WIDTH), (QUERY_HEADS * HEAD_SIZE) ** -0.5, 0.09375, ((0, 16),))
    adapter_qkv_down_store = gaussian(streams_of[5], (TENANT_COUNT, MODEL_WIDTH, 3 * ADAPTER_RANK), MODEL_WIDTH ** -0.5, 0.0625, ((0, 8), (1, 16)))
    adapter_query_up = gaussian(streams_of[6], (TENANT_COUNT, ADAPTER_RANK, QUERY_HEADS * HEAD_SIZE), (4 * ADAPTER_RANK) ** -0.5, 0.375, ((0, 8), (2, 16)))
    adapter_key_value_up = gaussian(streams_of[7], (TENANT_COUNT, ADAPTER_RANK, 2 * KEY_VALUE_HEADS * HEAD_SIZE), (4 * ADAPTER_RANK) ** -0.5, 0.375, ((0, 8), (2, 16)))
    adapter_output_down = gaussian(streams_of[8], (TENANT_COUNT, QUERY_HEADS * HEAD_SIZE, ADAPTER_RANK), (QUERY_HEADS * HEAD_SIZE // 4) ** -0.5, 0.1875, ((0, 8), (1, 16)))
    adapter_output_up = gaussian(streams_of[9], (TENANT_COUNT, ADAPTER_RANK, MODEL_WIDTH), ADAPTER_RANK ** -0.5, 0.75, ((0, 8), (2, 16)))
    crop_token_length = uneven_parts(streams_of[10], NSEG, TOKENS, SEG_MOST, 2).astype(jnp.int32)
    tenant_per_block = draw_tenant_per_block(jax.random.fold_in(streams_of[13], 71), 0)
    tenant_store_row = draw_tenant_store_row(jax.random.fold_in(streams_of[13], 71), 0)
    return {"hidden_input": hidden_input, "output_cotangent": output_cotangent, "query_projection": query_projection, "key_value_projection": key_value_projection, "output_projection": output_projection, "adapter_qkv_down_store": adapter_qkv_down_store, "adapter_query_up": adapter_query_up, "adapter_key_value_up": adapter_key_value_up, "adapter_output_down": adapter_output_down, "adapter_output_up": adapter_output_up, "crop_token_length": crop_token_length, "tenant_per_block": tenant_per_block, "tenant_store_row": tenant_store_row}


NEG = -1.0e30
ROPE_BASE = 1000000.0


def rope_pair(positions):
    half_dim = HEAD_SIZE // 2
    exponent = jnp.arange(half_dim, dtype=jnp.float32) * (2.0 / HEAD_SIZE)
    frequency = jnp.exp(-exponent * math.log(ROPE_BASE))
    angles = positions.astype(jnp.float32)[:, None] * frequency[None, :]
    return jnp.cos(angles), jnp.sin(angles)


def rotate(values, cosine, sine_tab):
    half_dim = values.shape[-1] // 2
    first_half = values[..., :half_dim]
    second = values[..., half_dim:]
    return jnp.concatenate([first_half * cosine - second * sine_tab, second * cosine + first_half * sine_tab], axis=-1)


def rotate_back(gradient, cosine, sine_tab):
    half_dim = gradient.shape[-1] // 2
    first_half = gradient[..., :half_dim]
    second = gradient[..., half_dim:]
    return jnp.concatenate([first_half * cosine + second * sine_tab, second * cosine - first_half * sine_tab], axis=-1)


def stored(values):
    return lax.optimization_barrier(values.astype(jnp.bfloat16))


def expand_to_width(values):
    return values.astype(jnp.float32)


def reference(hidden_input, output_cotangent, query_projection, key_value_projection, output_projection, adapter_qkv_down_store, adapter_query_up, adapter_key_value_up, adapter_output_down, adapter_output_up, crop_token_length, tenant_per_block, tenant_store_row):
    rows_per_block = tenant_store_row[tenant_per_block].astype(jnp.int32)
    block_count = TOKENS // BLK
    x_blocks = expand_to_width(hidden_input).reshape(block_count, BLK, MODEL_WIDTH)
    query_key_value_down = expand_to_width(adapter_qkv_down_store[rows_per_block])
    query_up_map = expand_to_width(adapter_query_up[rows_per_block])
    key_value_up_map = expand_to_width(adapter_key_value_up[rows_per_block])
    output_down_map = expand_to_width(adapter_output_down[rows_per_block])
    output_up_map = expand_to_width(adapter_output_up[rows_per_block])

    low_in = stored(jnp.einsum('nkd,ndr->nkr', x_blocks, query_key_value_down))
    low_wide = expand_to_width(low_in)
    low_q = low_wide[..., :ADAPTER_RANK]
    low_k = low_wide[..., ADAPTER_RANK:2 * ADAPTER_RANK]
    low_v = low_wide[..., 2 * ADAPTER_RANK:]

    positions = jnp.arange(TOKENS, dtype=jnp.int32)
    cosine, sine_tab = rope_pair(positions)
    query_lin = jnp.dot(hidden_input, query_projection, preferred_element_type=jnp.float32) + jnp.einsum('nkr,nrc->nkc', low_q, query_up_map).reshape(TOKENS, QUERY_HEADS * HEAD_SIZE)
    query_rot = stored(rotate(query_lin.reshape(TOKENS, QUERY_HEADS, HEAD_SIZE), cosine[:, None, :], sine_tab[:, None, :]))
    column_ids = jnp.arange(2 * KEY_VALUE_HEADS * HEAD_SIZE, dtype=jnp.int32)
    is_value = (column_ids // HEAD_SIZE) % 2 == 1
    kv_low = jnp.where(is_value, jnp.einsum('nkr,nrc->nkc', low_v, key_value_up_map), jnp.einsum('nkr,nrc->nkc', low_k, key_value_up_map)).reshape(TOKENS, 2 * KEY_VALUE_HEADS * HEAD_SIZE)
    keyval = stored(jnp.dot(hidden_input, key_value_projection, preferred_element_type=jnp.float32) + kv_low).reshape(TOKENS, KEY_VALUE_HEADS, 2, HEAD_SIZE)
    key_rot = stored(rotate(expand_to_width(keyval[:, :, 0]), cosine[:, None, :], sine_tab[:, None, :]))
    value_all = keyval[:, :, 1]

    crop_ends = jnp.cumsum(crop_token_length).astype(jnp.int32)
    segment = jnp.sum((positions[:, None] >= crop_ends[None, :]).astype(jnp.int32), axis=1)
    allowed = (positions[None, :] <= positions[:, None]) & (segment[None, :] == segment[:, None])
    score_scale = HEAD_SIZE ** -0.5

    def scores_of(head_kv):
        queries = expand_to_width(query_rot[:, head_kv * GROUP:(head_kv + 1) * GROUP])
        raw_scores = jnp.einsum('qhd,kd->hqk', queries, expand_to_width(key_rot[:, head_kv])) * score_scale
        return jnp.where(allowed[None], raw_scores, NEG)

    head_out = []
    norms = []
    for head_kv in range(KEY_VALUE_HEADS):
        scores = scores_of(head_kv)
        row_max = jnp.max(scores, axis=2, keepdims=True)
        log_norm = row_max + jnp.log(jnp.sum(jnp.exp(scores - row_max), axis=2, keepdims=True))
        weights = expand_to_width(stored(jnp.exp(scores - log_norm)))
        head_out.append(stored(jnp.einsum('hqk,kd->qhd', weights, expand_to_width(value_all[:, head_kv]))))
        norms.append(log_norm)
    attn_out = jnp.concatenate(head_out, axis=1).reshape(TOKENS, QUERY_HEADS * HEAD_SIZE)
    out_blocks = expand_to_width(attn_out).reshape(block_count, BLK, QUERY_HEADS * HEAD_SIZE)
    lowrank_output = stored(jnp.einsum('nkc,ncr->nkr', out_blocks, output_down_map))

    group_list = jnp.arange(N_TP, dtype=jnp.int32)

    def add_heads(running, group_no):
        columns = lax.dynamic_slice_in_dim(attn_out, group_no * (HEAD_GROUP * HEAD_SIZE), HEAD_GROUP * HEAD_SIZE, 1)
        weight_rows = lax.dynamic_slice_in_dim(output_projection, group_no * (HEAD_GROUP * HEAD_SIZE), HEAD_GROUP * HEAD_SIZE, 0)
        return running + expand_to_width(stored(jnp.dot(columns, weight_rows, preferred_element_type=jnp.float32))), None

    heads_total_sum, unused = lax.scan(add_heads, jnp.zeros((TOKENS, MODEL_WIDTH), jnp.float32), group_list)
    output = (heads_total_sum + jnp.einsum('nkr,nrc->nkc', expand_to_width(lowrank_output), output_up_map).reshape(TOKENS, MODEL_WIDTH)).astype(jnp.bfloat16)

    grad_blocks = expand_to_width(output_cotangent).reshape(block_count, BLK, MODEL_WIDTH)
    low_grad_o = stored(jnp.einsum('nkc,nrc->nkr', grad_blocks, output_up_map))

    def add_columns(running, group_no):
        columns = lax.dynamic_slice_in_dim(output_cotangent, group_no * COL_GROUP, COL_GROUP, 1)
        weight_cols = lax.dynamic_slice_in_dim(output_projection, group_no * COL_GROUP, COL_GROUP, 1)
        return running + expand_to_width(stored(jnp.dot(columns, weight_cols.T, preferred_element_type=jnp.float32))), None

    grad_sum, unused = lax.scan(add_columns, jnp.zeros((TOKENS, QUERY_HEADS * HEAD_SIZE), jnp.float32), group_list)
    attention_gradient = stored(grad_sum + jnp.einsum('nkr,ncr->nkc', expand_to_width(low_grad_o), output_down_map).reshape(TOKENS, QUERY_HEADS * HEAD_SIZE))
    head_gradient = attention_gradient.reshape(TOKENS, QUERY_HEADS, HEAD_SIZE)
    out_heads = attn_out.reshape(TOKENS, QUERY_HEADS, HEAD_SIZE)

    grad_q_parts = []
    key_parts = []
    value_parts = []
    for head_kv in range(KEY_VALUE_HEADS):
        first_head = head_kv * GROUP
        end_head = first_head + GROUP
        scores = scores_of(head_kv)
        weights = jnp.exp(scores - norms[head_kv])
        weights_narrow = expand_to_width(stored(weights))
        grad_here = expand_to_width(head_gradient[:, first_head:end_head])
        grad_weights = jnp.einsum('qhd,kd->hqk', grad_here, expand_to_width(value_all[:, head_kv]))
        row_delta = jnp.sum(grad_here * expand_to_width(out_heads[:, first_head:end_head]), axis=2)
        grad_scores = expand_to_width(stored(weights * (grad_weights - row_delta.T[:, :, None])))
        grad_q_parts.append(jnp.einsum('hqk,kd->qhd', grad_scores, expand_to_width(key_rot[:, head_kv])) * score_scale)
        key_parts.append(jnp.einsum('hqk,qhd->kd', grad_scores, expand_to_width(query_rot[:, first_head:end_head])) * score_scale)
        value_parts.append(jnp.einsum('hqk,qhd->kd', weights_narrow, grad_here))
    grad_q = stored(rotate_back(jnp.concatenate(grad_q_parts, axis=1), cosine[:, None, :], sine_tab[:, None, :]).reshape(TOKENS, QUERY_HEADS * HEAD_SIZE))
    key_grad = rotate_back(jnp.stack(key_parts, axis=1), cosine[:, None, :], sine_tab[:, None, :])
    grad_kv = stored(jnp.stack([key_grad, jnp.stack(value_parts, axis=1)], axis=2).reshape(TOKENS, 2 * KEY_VALUE_HEADS * HEAD_SIZE))

    grad_q_blocks = expand_to_width(grad_q).reshape(block_count, BLK, QUERY_HEADS * HEAD_SIZE)
    grad_kv_blocks = expand_to_width(grad_kv).reshape(block_count, BLK, 2 * KEY_VALUE_HEADS * HEAD_SIZE)
    key_part = jnp.where(is_value, 0.0, grad_kv_blocks)
    value_part = jnp.where(is_value, grad_kv_blocks, 0.0)
    lowrank_gradient = stored(jnp.concatenate([
        jnp.einsum('nkc,nrc->nkr', grad_q_blocks, query_up_map),
        jnp.einsum('nkc,nrc->nkr', key_part, key_value_up_map),
        jnp.einsum('nkc,nrc->nkr', value_part, key_value_up_map)], axis=2))

    def add_inputs(running, group_no):
        query_cols = lax.dynamic_slice_in_dim(grad_q, group_no * (HEAD_GROUP * HEAD_SIZE), HEAD_GROUP * HEAD_SIZE, 1)
        query_weights = lax.dynamic_slice_in_dim(query_projection, group_no * (HEAD_GROUP * HEAD_SIZE), HEAD_GROUP * HEAD_SIZE, 1)
        keyval_cols = lax.dynamic_slice_in_dim(grad_kv, group_no * KV_GROUP, KV_GROUP, 1)
        keyval_weights = lax.dynamic_slice_in_dim(key_value_projection, group_no * KV_GROUP, KV_GROUP, 1)
        group_terms = jnp.dot(query_cols, query_weights.T, preferred_element_type=jnp.float32) + jnp.dot(keyval_cols, keyval_weights.T, preferred_element_type=jnp.float32)
        return running + expand_to_width(stored(group_terms)), None

    input_total_sum, unused = lax.scan(add_inputs, jnp.zeros((TOKENS, MODEL_WIDTH), jnp.float32), group_list)
    low_grad_wide = expand_to_width(lowrank_gradient)
    hidden_input_gradient = (input_total_sum + jnp.einsum('nkr,ndr->nkd', low_grad_wide, query_key_value_down).reshape(TOKENS, MODEL_WIDTH)).astype(jnp.bfloat16)

    grad_down_qkv = jnp.zeros((TENANT_COUNT, MODEL_WIDTH, 3 * ADAPTER_RANK), jnp.float32).at[rows_per_block].add(jnp.einsum('nkd,nkr->ndr', x_blocks, low_grad_wide))
    grad_up_q = jnp.zeros((TENANT_COUNT, ADAPTER_RANK, QUERY_HEADS * HEAD_SIZE), jnp.float32).at[rows_per_block].add(jnp.einsum('nkr,nkc->nrc', low_q, grad_q_blocks))
    grad_up_kv = jnp.zeros((TENANT_COUNT, ADAPTER_RANK, 2 * KEY_VALUE_HEADS * HEAD_SIZE), jnp.float32).at[rows_per_block].add(jnp.where(is_value, jnp.einsum('nkr,nkc->nrc', low_v, grad_kv_blocks), jnp.einsum('nkr,nkc->nrc', low_k, grad_kv_blocks)))
    grad_down_o = jnp.zeros((TENANT_COUNT, QUERY_HEADS * HEAD_SIZE, ADAPTER_RANK), jnp.float32).at[rows_per_block].add(jnp.einsum('nkc,nkr->ncr', out_blocks, expand_to_width(low_grad_o)))
    grad_up_o = jnp.zeros((TENANT_COUNT, ADAPTER_RANK, MODEL_WIDTH), jnp.float32).at[rows_per_block].add(jnp.einsum('nkr,nkc->nrc', expand_to_width(lowrank_output), grad_blocks))
    return (output, hidden_input_gradient, grad_down_qkv, grad_up_q, grad_up_kv, grad_down_o, grad_up_o)
```

```python
import functools
import math

import jax
import jax.numpy as jnp
from jax import lax
from jax.experimental import pallas as pl
from jax.experimental.pallas import tpu as pltpu
from jax.sharding import PartitionSpec as P

HEAD = 128
RANK = 64
BLK = 128
NEG = -1e30
ROPE_BASE = 1000000.0
F32 = jnp.float32
BF16 = jnp.bfloat16
MESH = pl.DeviceIdType.MESH
VMEM = pltpu.VMEM


def nn(a, b):
    return lax.dot_general(a, b, (((1,), (0,)), ((), ())), preferred_element_type=F32)


def nt(a, b):
    return lax.dot_general(a, b, (((1,), (1,)), ((), ())), preferred_element_type=F32)


class Dims:
    def __init__(self, rows, width, heads):
        self.rows = rows
        self.width = width
        self.heads = heads
        self.blocks = rows // BLK
        self.v = width
        self.qu = self.v + width // 2
        self.kvu = self.qu + heads * RANK
        self.od = self.kvu + RANK
        self.ou = self.od + HEAD
        self.total = self.ou + (width // HEAD) * RANK


def any_spec():
    return pl.BlockSpec(memory_space=pl.ANY)


def vmem_spec():
    return pl.BlockSpec(memory_space=VMEM)


def cost(flops, moved):
    return pl.CostEstimate(flops=int(flops), bytes_accessed=int(moved), transcendentals=0)


def serve_body(dim, index_ref, down, q_up, kv_up, o_down, o_up, out):
    half = dim.width // 2
    out[0, 0 : dim.width, :] = down[0, :, 0:HEAD]
    out[0, dim.v : dim.v + half, 0:RANK] = down[0, 0:half, HEAD:]
    out[0, dim.v : dim.v + half, RANK:] = down[0, half:, HEAD:]
    for head in range(dim.heads):
        at = dim.qu + head * RANK
        out[0, at : at + RANK, :] = q_up[0, :, head * HEAD : (head + 1) * HEAD]
        out[0, dim.od : dim.od + HEAD, head * RANK : (head + 1) * RANK] = o_down[
            0, head * HEAD : (head + 1) * HEAD, :
        ]
    out[0, dim.kvu : dim.kvu + RANK, :] = kv_up[0]
    for chunk in range(dim.width // HEAD):
        at = dim.ou + chunk * RANK
        out[0, at : at + RANK, :] = o_up[0, :, chunk * HEAD : (chunk + 1) * HEAD]


def serve(dim, index, down, q_up, kv_up, o_down, o_up):
    count = index.shape[0]

    def picked(array):
        return pl.BlockSpec((1,) + array.shape[1:], lambda i, idx: (idx[i], 0, 0))

    return pl.pallas_call(
        functools.partial(serve_body, dim),
        out_shape=jax.ShapeDtypeStruct((count, dim.total, HEAD), BF16),
        grid_spec=pltpu.PrefetchScalarGridSpec(
            num_scalar_prefetch=1,
            grid=(count,),
            in_specs=[picked(a) for a in (down, q_up, kv_up, o_down, o_up)],
            out_specs=pl.BlockSpec((1, dim.total, HEAD), lambda i, idx: (i, 0, 0)),
        ),
        cost_estimate=cost(0, 2 * count * dim.total * HEAD * 2),
        name="serve",
    )(index, down, q_up, kv_up, o_down, o_up)


def low_parts_body(dim, index_ref, fetched, x, cot, part, maps):
    half = dim.width // 2
    m = fetched.at[0]
    xb = x[...]
    part[0] = nn(xb, m[0 : dim.width, :]).astype(BF16)
    vv = m[dim.v : dim.v + half, :]
    low_v = nn(xb[:, :half], vv)[:, :RANK] + nn(xb[:, half:], vv)[:, RANK:]
    low_o = jnp.zeros((BLK, RANK), F32)
    for chunk in range(dim.width // HEAD):
        at = dim.ou + chunk * RANK
        low_o += nt(cot[:, chunk * HEAD : (chunk + 1) * HEAD], m[at : at + RANK, :])
    part[1] = jnp.concatenate([low_v, low_o], axis=1).astype(BF16)
    maps[...] = fetched[...]


def low_parts(dim, index, fetched, hidden, cot):
    return pl.pallas_call(
        functools.partial(low_parts_body, dim),
        out_shape=(
            jax.ShapeDtypeStruct((2, dim.rows, HEAD), BF16),
            jax.ShapeDtypeStruct((dim.blocks, dim.total, HEAD), BF16),
        ),
        grid_spec=pltpu.PrefetchScalarGridSpec(
            num_scalar_prefetch=1,
            grid=(dim.blocks,),
            in_specs=[
                pl.BlockSpec((1, dim.total, HEAD), lambda b, idx: (idx[b], 0, 0)),
                pl.BlockSpec((BLK, dim.width), lambda b, idx: (b, idx[dim.blocks])),
                pl.BlockSpec((BLK, dim.width), lambda b, idx: (b, 0)),
            ],
            out_specs=(
                pl.BlockSpec((2, BLK, HEAD), lambda b, idx: (0, b, 0)),
                pl.BlockSpec((1, dim.total, HEAD), lambda b, idx: (b, 0, 0)),
            ),
        ),
        cost_estimate=cost(2 * dim.rows * dim.width * 256, 3 * dim.total * HEAD * 4),
        name="low_parts",
    )(index, fetched, hidden, cot)


def sum_tp_body(n, x_ref, o_ref, recv, own, send_a, recv_a, send_b, recv_b):
    me = lax.axis_index("tp")
    row = lax.axis_index("ctx")
    barrier = pltpu.get_barrier_semaphore()
    for k in range(1, n):
        pl.semaphore_signal(
            barrier, inc=1, device_id=(row, lax.rem(me + k, n)), device_id_type=MESH
        )
    pl.semaphore_wait(barrier, n - 1)
    first = []
    for k in range(1, n):
        peer = lax.rem(me + k, n)
        copy = pltpu.make_async_remote_copy(
            src_ref=x_ref.at[peer],
            dst_ref=recv.at[k],
            send_sem=send_a.at[k],
            recv_sem=recv_a.at[k],
            device_id=(row, peer),
            device_id_type=MESH,
        )
        copy.start()
        first.append(copy)
    total = x_ref[me].astype(F32)
    for k in range(1, n):
        first[k - 1].wait_recv()
        total = total + recv[k].astype(F32)
    own[...] = total.astype(BF16)
    o_ref[me] = total.astype(BF16)
    second = []
    for k in range(1, n):
        peer = lax.rem(me + k, n)
        copy = pltpu.make_async_remote_copy(
            src_ref=own,
            dst_ref=o_ref.at[me],
            send_sem=send_b.at[k],
            recv_sem=recv_b.at[k],
            device_id=(row, peer),
            device_id_type=MESH,
        )
        copy.start()
        second.append(copy)
    for k in range(1, n):
        first[k - 1].wait_send()
        second[k - 1].wait()


def sum_tp(part, collective_id):
    n = lax.axis_size("tp")
    shape = part.shape
    piece = part.size // HEAD // n
    x = part.reshape(n, piece, HEAD)
    out = pl.pallas_call(
        functools.partial(sum_tp_body, n),
        out_shape=jax.ShapeDtypeStruct((n, piece, HEAD), BF16),
        in_specs=[vmem_spec()],
        out_specs=vmem_spec(),
        scratch_shapes=[
            pltpu.VMEM((n, piece, HEAD), BF16),
            pltpu.VMEM((piece, HEAD), BF16),
            pltpu.SemaphoreType.DMA((n,)),
            pltpu.SemaphoreType.DMA((n,)),
            pltpu.SemaphoreType.DMA((n,)),
            pltpu.SemaphoreType.DMA((n,)),
        ],
        compiler_params=pltpu.CompilerParams(collective_id=collective_id, has_side_effects=True),
        cost_estimate=cost(3e9, 3e7),
        name="sum_tp",
    )(x)
    return out.reshape(shape)


def finalize_body(dim, xq, xkv, low, maps, ctab, stab, q_out, kv_out, delta_out):
    core = lax.rem(lax.axis_index("tp"), 2)
    is_value = core == 1
    for b in range(dim.blocks):
        rows = slice(b * BLK, (b + 1) * BLK)
        m = maps.at[b]
        first = low[0, rows, :]
        second = low[1, rows, :]
        low_q = first[:, :RANK]
        low_kv = jnp.where(is_value, second[:, :RANK], first[:, RANK:])
        low_o = second[:, RANK:]
        cosine = ctab[rows, :]
        sine = stab[rows, :]
        for head in range(dim.heads):
            cols = slice(head * HEAD, (head + 1) * HEAD)
            at = dim.qu + head * RANK
            q = xq[rows, cols] + nn(low_q, m[at : at + RANK, :])
            q_out[rows, cols] = (q * cosine + pltpu.roll(q, HEAD // 2, 1) * sine).astype(BF16)
            lane = slice(head * RANK, (head + 1) * RANK)
            delta_out[rows, cols] = nt(low_o, m[dim.od : dim.od + HEAD, lane])
        kv = xkv[rows, :] + nn(low_kv, m[dim.kvu : dim.kvu + RANK, :])
        kv = kv.astype(BF16).astype(F32)
        turned = kv * cosine + pltpu.roll(kv, HEAD // 2, 1) * sine
        kv_out[rows, :] = jnp.where(is_value, kv, turned).astype(BF16)


def finalize(dim, xq, xkv, low, maps, ctab, stab):
    cols = dim.heads * HEAD
    return pl.pallas_call(
        functools.partial(finalize_body, dim),
        out_shape=(
            jax.ShapeDtypeStruct((dim.rows, cols), BF16),
            jax.ShapeDtypeStruct((dim.rows, HEAD), BF16),
            jax.ShapeDtypeStruct((dim.rows, cols), F32),
        ),
        in_specs=[vmem_spec()] * 6,
        out_specs=(vmem_spec(),) * 3,
        cost_estimate=cost(1e8, 4e6),
        name="finalize",
    )(xq, xkv, low, maps, ctab, stab)


def gather_kv_body(n, x_ref, o_ref, send_a, recv_a, send_b, recv_b):
    c = lax.axis_index("ctx")
    t = lax.axis_index("tp")
    core = lax.rem(t, 2)
    partner = t + 1 - 2 * core
    barrier = pltpu.get_barrier_semaphore()
    pl.semaphore_signal(barrier, inc=1, device_id=(c, partner), device_id_type=MESH)
    for k in range(1, n):
        pl.semaphore_signal(barrier, inc=1, device_id=(lax.rem(c + k, n), t), device_id_type=MESH)
    pl.semaphore_wait(barrier, n)
    copies = []
    for k in range(1, n):
        copy = pltpu.make_async_remote_copy(
            src_ref=x_ref,
            dst_ref=o_ref.at[core, c],
            send_sem=send_a.at[k],
            recv_sem=recv_a.at[k],
            device_id=(lax.rem(c + k, n), t),
            device_id_type=MESH,
        )
        copy.start()
        copies.append(copy)
    forwards = []
    copy = pltpu.make_async_remote_copy(
        src_ref=x_ref,
        dst_ref=o_ref.at[core, c],
        send_sem=send_b.at[0],
        recv_sem=recv_b.at[0],
        device_id=(c, partner),
        device_id_type=MESH,
    )
    copy.start()
    forwards.append(copy)
    o_ref[core, c] = x_ref[...]
    for k in range(1, n):
        source = lax.rem(c - k + n, n)
        copies[k - 1].wait_recv()
        copy = pltpu.make_async_remote_copy(
            src_ref=o_ref.at[core, source],
            dst_ref=o_ref.at[core, source],
            send_sem=send_b.at[k],
            recv_sem=recv_b.at[k],
            device_id=(c, partner),
            device_id_type=MESH,
        )
        copy.start()
        forwards.append(copy)
    for k in range(1, n):
        copies[k - 1].wait_send()
    for copy in forwards:
        copy.wait()


def gather_kv(kv, collective_id):
    n = lax.axis_size("ctx")
    rows = kv.shape[0]
    return pl.pallas_call(
        functools.partial(gather_kv_body, n),
        out_shape=jax.ShapeDtypeStruct((2, n, rows, HEAD), BF16),
        in_specs=[vmem_spec()],
        out_specs=vmem_spec(),
        scratch_shapes=[pltpu.SemaphoreType.DMA((n,))] * 4,
        compiler_params=pltpu.CompilerParams(collective_id=collective_id, has_side_effects=True),
        cost_estimate=cost(3e9, 3e7),
        name="gather_kv",
    )(kv)


def allowed_tile(j, rows, first_pos, start):
    key_pos = j * rows + lax.broadcasted_iota(jnp.int32, (rows, rows), 0)
    query_pos = first_pos + lax.broadcasted_iota(jnp.int32, (1, rows), 1)
    return (key_pos <= query_pos) & (key_pos >= start)


def attend_body(dim, meta, start_ref, q_ref, kv_ref, o_ref, lse_ref, s_scr, acc):
    rows = dim.rows
    scale = HEAD ** (-0.5)
    lo = meta[0]
    hi = meta[1]
    first_pos = meta[2]
    start = start_ref[...]
    heads = range(dim.heads)

    def scores(j, peaks):
        kj = kv_ref[0, j]
        ok = allowed_tile(j, rows, first_pos, start)
        fresh = []
        for h in heads:
            s = nt(kj, q_ref[:, h * HEAD : (h + 1) * HEAD]) * scale
            s = jnp.where(ok, s, NEG)
            s_scr[h, j] = s
            fresh.append(jnp.maximum(peaks[h], jnp.max(s, axis=0, keepdims=True)))
        return tuple(fresh)

    peaks = lax.fori_loop(lo, hi, scores, tuple(jnp.full((1, rows), NEG, F32) for h in heads))
    acc[...] = jnp.zeros_like(acc)

    def mix(j, sums):
        vt = kv_ref[1, j].T
        fresh = []
        for h in heads:
            p = jnp.exp(s_scr[h, j] - peaks[h])
            fresh.append(sums[h] + jnp.sum(p, axis=0, keepdims=True))
            acc[h] += nn(vt, p.astype(BF16))
        return tuple(fresh)

    sums = lax.fori_loop(lo, hi, mix, tuple(jnp.zeros((1, rows), F32) for h in heads))
    for h in heads:
        o_ref[:, h * HEAD : (h + 1) * HEAD] = (acc[h] / sums[h]).T.astype(BF16)
        lse_ref[h] = peaks[h] + jnp.log(sums[h])


def attend(dim, meta, start, q, kv):
    n = kv.shape[1]
    rows = dim.rows
    return pl.pallas_call(
        functools.partial(attend_body, dim),
        out_shape=(
            jax.ShapeDtypeStruct(q.shape, BF16),
            jax.ShapeDtypeStruct((dim.heads, 1, rows), F32),
        ),
        in_specs=[pl.BlockSpec(memory_space=pltpu.SMEM)] + [vmem_spec()] * 3,
        out_specs=(vmem_spec(), vmem_spec()),
        scratch_shapes=[
            pltpu.VMEM((dim.heads, n, rows, rows), F32),
            pltpu.VMEM((dim.heads, HEAD, rows), F32),
        ],
        compiler_params=pltpu.CompilerParams(vmem_limit_bytes=40 << 20),
        cost_estimate=cost(4 * dim.heads * rows * rows * n * HEAD * 4, 3e7),
        name="attend",
    )(meta, start, q, kv)


def attend_back_body(
    dim, n, meta, start_ref, q_ref, kv_ref, o_ref, lse_ref, do_ref, ctab, stab, dq_ref, dkv_ref, acc
):
    rows = dim.rows
    scale = HEAD ** (-0.5)
    lo = meta[0]
    hi = meta[1]
    first_pos = meta[2]
    start = start_ref[...]
    heads = range(dim.heads)
    acc[...] = jnp.zeros_like(acc)

    def clear(j, carry):
        dkv_ref[0, j] = jnp.zeros((rows, HEAD), BF16)
        dkv_ref[1, j] = jnp.zeros((rows, HEAD), BF16)
        return carry

    lax.fori_loop(0, lo, clear, 0)
    lax.fori_loop(hi, n, clear, 0)
    delta = []
    for h in heads:
        cols = slice(h * HEAD, (h + 1) * HEAD)
        both = do_ref[:, cols].astype(F32) * o_ref[:, cols].astype(F32)
        delta.append(jnp.sum(both.T, axis=0, keepdims=True))

    def step(j, carry):
        kj = kv_ref[0, j]
        vj = kv_ref[1, j]
        kt = kj.T
        ok = allowed_tile(j, rows, first_pos, start)
        dk = jnp.zeros((rows, HEAD), F32)
        dv = jnp.zeros((rows, HEAD), F32)
        for h in heads:
            qh = q_ref[:, h * HEAD : (h + 1) * HEAD]
            doh = do_ref[:, h * HEAD : (h + 1) * HEAD]
            s = jnp.where(ok, nt(kj, qh) * scale, NEG)
            p = jnp.exp(s - lse_ref[h])
            ds = (p * (nt(vj, doh) - delta[h])).astype(BF16)
            acc[h] += nn(kt, ds)
            dk += nn(ds, qh)
            dv += nn(p.astype(BF16), doh)
        dkv_ref[0, j] = (dk * scale).astype(BF16)
        dkv_ref[1, j] = dv.astype(BF16)
        return carry

    lax.fori_loop(lo, hi, step, 0)
    for h in heads:
        dq = (acc[h] * scale).T
        dq = dq * ctab[...] - pltpu.roll(dq, HEAD // 2, 1) * stab[...]
        dq_ref[:, h * HEAD : (h + 1) * HEAD] = dq.astype(BF16)


def attend_back(dim, meta, start, q, kv, out, lse, grad, ctab, stab):
    n = kv.shape[1]
    rows = dim.rows
    return pl.pallas_call(
        functools.partial(attend_back_body, dim, n),
        out_shape=(
            jax.ShapeDtypeStruct(q.shape, BF16),
            jax.ShapeDtypeStruct(kv.shape, BF16),
        ),
        in_specs=[pl.BlockSpec(memory_space=pltpu.SMEM)] + [vmem_spec()] * 8,
        out_specs=(vmem_spec(), vmem_spec()),
        scratch_shapes=[pltpu.VMEM((dim.heads, HEAD, rows), F32)],
        compiler_params=pltpu.CompilerParams(vmem_limit_bytes=40 << 20),
        cost_estimate=cost(10 * dim.heads * rows * rows * n * HEAD * 4, 3e7),
        name="attend_back",
    )(meta, start, q, kv, out, lse, grad, ctab, stab)


def scatter_kv_body(
    n, x_ref, ctab, stab, o_ref, half, mine, arrived, send_a, recv_a, send_b, recv_b
):
    c = lax.axis_index("ctx")
    t = lax.axis_index("tp")
    core = lax.rem(t, 2)
    partner = t + 1 - 2 * core
    barrier = pltpu.get_barrier_semaphore()
    pl.semaphore_signal(barrier, inc=1, device_id=(c, partner), device_id_type=MESH)
    for k in range(1, n):
        pl.semaphore_signal(barrier, inc=1, device_id=(lax.rem(c + k, n), t), device_id_type=MESH)
    pl.semaphore_wait(barrier, n)
    order = list(range(1, n)) + [0]
    swaps = {}
    for k in order:
        copy = pltpu.make_async_remote_copy(
            src_ref=x_ref.at[1 - core, lax.rem(c + k, n)],
            dst_ref=half.at[k],
            send_sem=send_a.at[k],
            recv_sem=recv_a.at[k],
            device_id=(c, partner),
            device_id_type=MESH,
        )
        copy.start()
        swaps[k] = copy
    sends = {}
    for k in range(1, n):
        swaps[k].wait_recv()
        mine[k] = (
            x_ref[core, lax.rem(c + k, n)].astype(F32) + half[k].astype(F32)
        ).astype(BF16)
        copy = pltpu.make_async_remote_copy(
            src_ref=mine.at[k],
            dst_ref=arrived.at[k],
            send_sem=send_b.at[k],
            recv_sem=recv_b.at[k],
            device_id=(lax.rem(c + k, n), t),
            device_id_type=MESH,
        )
        copy.start()
        sends[k] = copy
    swaps[0].wait_recv()
    total = x_ref[core, c].astype(F32) + half[0].astype(F32)
    for k in range(1, n):
        sends[k].wait_recv()
        total = total + arrived[k].astype(F32)
    turned = total * ctab[...] - pltpu.roll(total, HEAD // 2, 1) * stab[...]
    o_ref[...] = jnp.where(core == 1, total, turned).astype(BF16)
    for k in order:
        swaps[k].wait_send()
    for k in range(1, n):
        sends[k].wait_send()


def scatter_kv(grads, ctab, stab, collective_id):
    n = grads.shape[1]
    rows = grads.shape[2]
    return pl.pallas_call(
        functools.partial(scatter_kv_body, n),
        out_shape=jax.ShapeDtypeStruct((rows, HEAD), BF16),
        in_specs=[vmem_spec()] * 3,
        out_specs=vmem_spec(),
        scratch_shapes=[
            pltpu.VMEM((n, rows, HEAD), BF16),
            pltpu.VMEM((n, rows, HEAD), BF16),
            pltpu.VMEM((n, rows, HEAD), BF16),
        ]
        + [pltpu.SemaphoreType.DMA((n,))] * 4,
        compiler_params=pltpu.CompilerParams(collective_id=collective_id, has_side_effects=True),
        cost_estimate=cost(3e9, 3e7),
        name="scatter_kv",
    )(grads, ctab, stab)


def low_grads_body(dim, attn, grad_q, grad_kv, maps, part):
    core = lax.rem(lax.axis_index("tp"), 2)
    m = maps.at[0]
    low_q = jnp.zeros((BLK, RANK), F32)
    low_out = jnp.zeros((BLK, RANK), F32)
    for head in range(dim.heads):
        cols = slice(head * HEAD, (head + 1) * HEAD)
        lane = slice(head * RANK, (head + 1) * RANK)
        at = dim.qu + head * RANK
        low_q += nt(grad_q[:, cols], m[at : at + RANK, :])
        low_out += nn(attn[:, cols], m[dim.od : dim.od + HEAD, lane])
    low_kv = nt(grad_kv[...], m[dim.kvu : dim.kvu + RANK, :])
    zero = jnp.zeros_like(low_kv)
    low_k = jnp.where(core == 0, low_kv, zero)
    low_v = jnp.where(core == 1, low_kv, zero)
    part[0] = jnp.concatenate([low_q, low_k], axis=1).astype(BF16)
    part[1] = jnp.concatenate([low_v, low_out], axis=1).astype(BF16)


def low_grads(dim, attn, grad_q, grad_kv, maps):
    cols = dim.heads * HEAD
    return pl.pallas_call(
        functools.partial(low_grads_body, dim),
        out_shape=jax.ShapeDtypeStruct((2, dim.rows, HEAD), BF16),
        grid=(dim.blocks,),
        in_specs=[
            pl.BlockSpec((BLK, cols), lambda b: (b, 0)),
            pl.BlockSpec((BLK, cols), lambda b: (b, 0)),
            pl.BlockSpec((BLK, HEAD), lambda b: (b, 0)),
            pl.BlockSpec((1, dim.total, HEAD), lambda b: (b, 0, 0)),
        ],
        out_specs=pl.BlockSpec((2, BLK, HEAD), lambda b: (0, b, 0)),
        cost_estimate=cost(1e8, 4e6),
        name="low_grads",
    )(attn, grad_q, grad_kv, maps)


def block_grads_body(
    dim, index_ref, x, cot, low_in, low_grad, attn, grad_q, grad_kv, maps, out, d_in, d_out
):
    half = dim.width // 2
    core = lax.rem(lax.axis_index("tp"), 2)
    m = maps.at[0]
    low_qk_t = low_in[0].T
    low_vo_t = low_in[1].T
    low_q_t = low_qk_t[:RANK]
    low_kv_t = jnp.where(core == 1, low_vo_t[:RANK], low_qk_t[RANK:])
    low_o = low_in[1, :, RANK:]
    g_qk = low_grad[0]
    g_v = low_grad[1, :, :RANK]
    low_out = low_grad[1, :, RANK:]
    low_out_t = low_out.T
    xt = x[...].T
    out[0, 0 : dim.width, :] = nn(xt, g_qk).astype(BF16)
    up = nn(xt, g_v).astype(BF16)
    out[0, dim.v : dim.v + half, 0:RANK] = up[:half]
    out[0, dim.v : dim.v + half, RANK:] = up[half:]
    for head in range(dim.heads):
        cols = slice(head * HEAD, (head + 1) * HEAD)
        lane = slice(head * RANK, (head + 1) * RANK)
        at = dim.qu + head * RANK
        out[0, at : at + RANK, :] = nn(low_q_t, grad_q[:, cols]).astype(BF16)
        out[0, dim.od : dim.od + HEAD, lane] = nn(attn[:, cols].T, low_o).astype(BF16)
    out[0, dim.kvu : dim.kvu + RANK, :] = nn(low_kv_t, grad_kv[...]).astype(BF16)
    for chunk in range(dim.width // HEAD):
        cols = slice(chunk * HEAD, (chunk + 1) * HEAD)
        at = dim.ou + chunk * RANK
        out[0, at : at + RANK, :] = nn(low_out_t, cot[:, cols]).astype(BF16)
        d_out[:, cols] = nn(low_out, m[at : at + RANK, :])
    vv = m[dim.v : dim.v + half, :]
    d_qk = nt(g_qk, m[0 : dim.width, :])
    d_in[:, :half] = d_qk[:, :half] + nt(g_v, vv[:, :RANK])
    d_in[:, half:] = d_qk[:, half:] + nt(g_v, vv[:, RANK:])


def block_grads(dim, index, owners, hidden, cot, low_in, low_grad, attn, grad_q, grad_kv, maps):
    cols = dim.heads * HEAD
    low_spec = pl.BlockSpec((2, BLK, HEAD), lambda b, idx: (0, b, 0))
    wide_spec = pl.BlockSpec((BLK, dim.width), lambda b, idx: (b, 0))
    return pl.pallas_call(
        functools.partial(block_grads_body, dim),
        out_shape=(
            jax.ShapeDtypeStruct((owners, dim.total, HEAD), BF16),
            jax.ShapeDtypeStruct((dim.rows, dim.width), F32),
            jax.ShapeDtypeStruct((dim.rows, dim.width), F32),
        ),
        grid_spec=pltpu.PrefetchScalarGridSpec(
            num_scalar_prefetch=1,
            grid=(dim.blocks,),
            in_specs=[
                pl.BlockSpec((BLK, dim.width), lambda b, idx: (b, idx[dim.blocks])),
                wide_spec,
                low_spec,
                low_spec,
                pl.BlockSpec((BLK, cols), lambda b, idx: (b, 0)),
                pl.BlockSpec((BLK, cols), lambda b, idx: (b, 0)),
                pl.BlockSpec((BLK, HEAD), lambda b, idx: (b, 0)),
                pl.BlockSpec((1, dim.total, HEAD), lambda b, idx: (b, 0, 0)),
            ],
            out_specs=(
                pl.BlockSpec((1, dim.total, HEAD), lambda b, idx: (idx[b], 0, 0)),
                wide_spec,
                wide_spec,
            ),
        ),
        cost_estimate=cost(1e9, 6e6),
        name="block_grads",
    )(index, hidden, cot, low_in, low_grad, attn, grad_q, grad_kv, maps)


def store_body(dim, count, row_ref, arrived, down, q_up, kv_up, o_down, o_up, acc):
    half = dim.width // 2
    i = pl.program_id(0)

    @pl.when(i == 0)
    def _():
        acc[...] = jnp.zeros_like(acc)

    row = row_ref[i]

    @pl.when(row >= 0)
    def _():
        acc[row] += arrived[0].astype(F32)

    @pl.when(i == count - 1)
    def _():
        for s in range(acc.shape[0]):
            down[s, :, 0:HEAD] = acc[s, 0 : dim.width, :]
            down[s, :half, HEAD:] = acc[s, dim.v : dim.v + half, :RANK]
            down[s, half:, HEAD:] = acc[s, dim.v : dim.v + half, RANK:]
            for head in range(dim.heads):
                cols = slice(head * HEAD, (head + 1) * HEAD)
                at = dim.qu + head * RANK
                q_up[s, :, cols] = acc[s, at : at + RANK, :]
                o_down[s, cols, :] = acc[
                    s, dim.od : dim.od + HEAD, head * RANK : (head + 1) * RANK
                ]
            kv_up[s] = acc[s, dim.kvu : dim.kvu + RANK, :]
            for chunk in range(dim.width // HEAD):
                at = dim.ou + chunk * RANK
                o_up[s, :, chunk * HEAD : (chunk + 1) * HEAD] = acc[s, at : at + RANK, :]


def to_store(dim, rows, arrived, shapes):
    count = arrived.shape[0]
    tenants = shapes[0][0]

    def whole(shape):
        return pl.BlockSpec(shape, lambda i, idx: (0, 0, 0))

    return pl.pallas_call(
        functools.partial(store_body, dim, count),
        out_shape=tuple(jax.ShapeDtypeStruct(s, F32) for s in shapes),
        grid_spec=pltpu.PrefetchScalarGridSpec(
            num_scalar_prefetch=1,
            grid=(count,),
            in_specs=[pl.BlockSpec((1, dim.total, HEAD), lambda i, idx: (i, 0, 0))],
            out_specs=tuple(whole(s) for s in shapes),
            scratch_shapes=[pltpu.VMEM((tenants, dim.total, HEAD), F32)],
        ),
        cost_estimate=cost(0, 6e6),
        name="to_store",
    )(rows, arrived)


def body(
    hidden_input,
    output_cotangent,
    query_projection,
    key_value_projection,
    output_projection,
    adapter_qkv_down_store,
    adapter_query_up,
    adapter_key_value_up,
    adapter_output_down,
    adapter_output_up,
    crop_token_length,
    tenant_per_block,
    tenant_store_row,
):
    ctx_count = lax.axis_size("ctx")
    ctx_index = lax.axis_index("ctx")
    tp_index = lax.axis_index("tp")
    rows_dev = hidden_input.shape[0]
    out_cols = output_cotangent.shape[1]
    tenants = adapter_qkv_down_store.shape[0]
    dim = Dims(rows_dev, out_cols, query_projection.shape[1] // HEAD)
    stores = (
        adapter_qkv_down_store,
        adapter_query_up,
        adapter_key_value_up,
        adapter_output_down,
        adapter_output_up,
    )

    tenant_ids = jnp.arange(tenant_store_row.shape[0], dtype=jnp.int32)
    rows_per_block = jnp.sum(
        jnp.where(tenant_per_block[:, None] == tenant_ids[None, :], tenant_store_row[None, :], 0),
        axis=1,
    )
    shard_rows = rows_per_block.reshape(ctx_count, dim.blocks)
    shard_owner = shard_rows // tenants
    served = shard_owner == ctx_index
    served_row = jnp.max(jnp.where(served, shard_rows - ctx_index * tenants, -1), axis=1)
    serve_index = jnp.maximum(served_row, 0)
    my_owner = lax.dynamic_index_in_dim(shard_owner, ctx_index, 0, keepdims=False)
    pick_index = jnp.concatenate([my_owner, tp_index[None]]).astype(jnp.int32)

    my_pos = ctx_index * rows_dev + jnp.arange(rows_dev, dtype=jnp.int32)
    crop_ends = jnp.cumsum(crop_token_length)
    row_start = jnp.max(
        jnp.where(crop_ends[:, None] <= my_pos[None, :], crop_ends[:, None], 0), axis=0
    ).astype(jnp.int32)
    first_pos = ctx_index * rows_dev
    first_start = jnp.max(jnp.where(crop_ends <= first_pos, crop_ends, 0))
    meta = jnp.stack([first_start // rows_dev, ctx_index + 1, first_pos]).astype(jnp.int32)
    start = row_start[None, :]
    half_dim = HEAD // 2
    exponent = jnp.arange(half_dim, dtype=F32) * (2.0 / HEAD)
    frequency = jnp.exp(-exponent * math.log(ROPE_BASE))
    angles = my_pos.astype(F32)[:, None] * jnp.concatenate([frequency, frequency])[None, :]
    sign = jnp.where(jnp.arange(HEAD) < half_dim, -1.0, 1.0).astype(F32)
    ctab = jnp.cos(angles)
    stab = jnp.sin(angles) * sign[None, :]

    fetched = lax.all_to_all(
        serve(dim, serve_index, *stores), "ctx", split_axis=0, concat_axis=0, tiled=True
    )
    pieces = lax.all_gather(output_cotangent, "tp", axis=1, tiled=True)
    xq = jnp.dot(hidden_input, query_projection, preferred_element_type=F32)
    xkv = jnp.dot(hidden_input, key_value_projection, preferred_element_type=F32)

    part, maps = low_parts(dim, pick_index, fetched, hidden_input, output_cotangent)
    low_in = sum_tp(part, 0)
    query, keyval, o_delta = finalize(dim, xq, xkv, low_in, maps, ctab, stab)
    kv_all = gather_kv(keyval, 1)
    attn, lse = attend(dim, meta, start, query, kv_all)

    heads_total = lax.psum_scatter(
        jnp.dot(attn, output_projection, preferred_element_type=F32).astype(BF16),
        "tp",
        scatter_dimension=1,
        tiled=True,
    ).astype(F32)

    grad_attn = (
        lax.dot_general(
            pieces, output_projection, (((1,), (1,)), ((), ())), preferred_element_type=F32
        )
        + o_delta
    ).astype(BF16)
    grad_q, grad_kv_all = attend_back(
        dim, meta, start, query, kv_all, attn, lse, grad_attn, ctab, stab
    )
    grad_kv = scatter_kv(grad_kv_all, ctab, stab, 2)

    low_grad = sum_tp(low_grads(dim, attn, grad_q, grad_kv, maps), 0)
    input_part = nt(grad_q, query_projection) + nt(grad_kv, key_value_projection)
    input_total = lax.psum_scatter(
        input_part.astype(BF16), "tp", scatter_dimension=1, tiled=True
    ).astype(F32)
    sent, d_in, d_out = block_grads(
        dim,
        pick_index,
        ctx_count,
        hidden_input,
        output_cotangent,
        low_in,
        low_grad,
        attn,
        grad_q,
        grad_kv,
        maps,
    )
    output = (heads_total + d_out).astype(BF16)
    hidden_input_gradient = (input_total + d_in).astype(BF16)
    returned = lax.all_to_all(sent, "ctx", split_axis=0, concat_axis=0, tiled=True)
    grads = to_store(dim, served_row, returned, [s.shape for s in stores])
    return (output, hidden_input_gradient) + tuple(grads)


def solution(mesh):
    in_specs = (
        P("ctx", None),
        P("ctx", "tp"),
        P(None, "tp"),
        P(None, "tp"),
        P("tp", None),
        P("ctx", "tp", None),
        P("ctx", None, "tp"),
        P("ctx", None, "tp"),
        P("ctx", "tp", None),
        P("ctx", None, "tp"),
        P(),
        P(),
        P(),
    )
    out_specs = (
        P("ctx", "tp"),
        P("ctx", "tp"),
        P("ctx", "tp", None),
        P("ctx", None, "tp"),
        P("ctx", None, "tp"),
        P("ctx", "tp", None),
        P("ctx", None, "tp"),
    )
    return jax.shard_map(body, mesh=mesh, in_specs=in_specs, out_specs=out_specs, check_vma=False)
```

```python
import functools
import math

import jax
import jax.numpy as jnp
from jax import lax
from jax.experimental import pallas as pl
from jax.experimental.pallas import tpu as pltpu
from jax.sharding import PartitionSpec as P

HEAD = 128
RANK = 64
BLK = 128
NEG = -1e30
ROPE_BASE = 1000000.0
F32 = jnp.float32
BF16 = jnp.bfloat16
MESH = pl.DeviceIdType.MESH
VMEM = pltpu.VMEM


def nn(a, b):
    return lax.dot_general(a, b, (((1,), (0,)), ((), ())), preferred_element_type=F32)


def nt(a, b):
    return lax.dot_general(a, b, (((1,), (1,)), ((), ())), preferred_element_type=F32)


class Dims:
    def __init__(self, rows, width, heads):
        self.rows = rows
        self.width = width
        self.heads = heads
        self.cols = heads * HEAD
        self.blocks = rows // BLK
        self.dq = slice(0, width)
        self.dk = slice(width, 2 * width)
        self.dv = slice(2 * width, 3 * width)
        at = 3 * width
        self.qu = slice(at, at + self.cols)
        at += self.cols
        self.kvu = slice(at, at + HEAD)
        at += HEAD
        self.od = slice(at, at + self.cols)
        at += self.cols
        self.ou = slice(at, at + width)
        self.total = at + width


def any_spec():
    return pl.BlockSpec(memory_space=pl.ANY)


def vmem_spec():
    return pl.BlockSpec(memory_space=VMEM)


def cost(flops, moved):
    return pl.CostEstimate(flops=int(flops), bytes_accessed=int(moved), transcendentals=0)


def serve_body(dim, index_ref, down, q_up, kv_up, o_down, o_up, out):
    out[0, :, dim.dq] = down[0, 0:RANK, :]
    out[0, :, dim.dk] = down[0, RANK : 2 * RANK, :]
    out[0, :, dim.dv] = down[0, 2 * RANK :, :]
    out[0, :, dim.qu] = q_up[0]
    out[0, :, dim.kvu] = kv_up[0]
    out[0, :, dim.od] = o_down[0]
    out[0, :, dim.ou] = o_up[0]


def serve(dim, index, stores):
    count = index.shape[0]

    def picked(array):
        return pl.BlockSpec((1,) + array.shape[1:], lambda i, idx: (idx[i], 0, 0))

    return pl.pallas_call(
        functools.partial(serve_body, dim),
        out_shape=jax.ShapeDtypeStruct((count, RANK, dim.total), BF16),
        grid_spec=pltpu.PrefetchScalarGridSpec(
            num_scalar_prefetch=1,
            grid=(count,),
            in_specs=[picked(a) for a in stores],
            out_specs=pl.BlockSpec((1, RANK, dim.total), lambda i, idx: (i, 0, 0)),
        ),
        cost_estimate=cost(0, 2 * count * dim.total * RANK * 2),
        name="serve",
    )(index, *stores)


def low_parts_body(dim, index_ref, fetched, x, cot, part, maps):
    m = fetched.at[0]
    xb = x[...]
    low = [nt(xb, m[:, at]) for at in (dim.dq, dim.dk, dim.dv)]
    low.append(nt(cot[...], m[:, dim.ou]))
    part[0] = jnp.concatenate(low[:2], axis=1).astype(BF16)
    part[1] = jnp.concatenate(low[2:], axis=1).astype(BF16)
    maps[...] = fetched[...]


def low_parts(dim, index, fetched, hidden, cot):
    return pl.pallas_call(
        functools.partial(low_parts_body, dim),
        out_shape=(
            jax.ShapeDtypeStruct((2, dim.rows, HEAD), BF16),
            jax.ShapeDtypeStruct((dim.blocks, RANK, dim.total), BF16),
        ),
        grid_spec=pltpu.PrefetchScalarGridSpec(
            num_scalar_prefetch=1,
            grid=(dim.blocks,),
            in_specs=[
                pl.BlockSpec((1, RANK, dim.total), lambda b, idx: (idx[b], 0, 0)),
                pl.BlockSpec((BLK, dim.width), lambda b, idx: (b, idx[dim.blocks])),
                pl.BlockSpec((BLK, dim.width), lambda b, idx: (b, 0)),
            ],
            out_specs=(
                pl.BlockSpec((2, BLK, HEAD), lambda b, idx: (0, b, 0)),
                pl.BlockSpec((1, RANK, dim.total), lambda b, idx: (b, 0, 0)),
            ),
        ),
        cost_estimate=cost(2 * dim.rows * dim.width * 256, 3 * dim.total * RANK * 4),
        name="low_parts",
    )(index, fetched, hidden, cot)


def sum_tp_body(n, x_ref, o_ref, recv, own, send_a, recv_a, send_b, recv_b):
    me = lax.axis_index("tp")
    row = lax.axis_index("ctx")
    barrier = pltpu.get_barrier_semaphore()
    for k in range(1, n):
        pl.semaphore_signal(
            barrier, inc=1, device_id=(row, lax.rem(me + k, n)), device_id_type=MESH
        )
    pl.semaphore_wait(barrier, n - 1)
    first = []
    for k in range(1, n):
        peer = lax.rem(me + k, n)
        copy = pltpu.make_async_remote_copy(
            src_ref=x_ref.at[peer],
            dst_ref=recv.at[k],
            send_sem=send_a.at[k],
            recv_sem=recv_a.at[k],
            device_id=(row, peer),
            device_id_type=MESH,
        )
        copy.start()
        first.append(copy)
    total = x_ref[me].astype(F32)
    for k in range(1, n):
        first[k - 1].wait_recv()
        total = total + recv[k].astype(F32)
    own[...] = total.astype(BF16)
    o_ref[me] = total.astype(BF16)
    second = []
    for k in range(1, n):
        peer = lax.rem(me + k, n)
        copy = pltpu.make_async_remote_copy(
            src_ref=own,
            dst_ref=o_ref.at[me],
            send_sem=send_b.at[k],
            recv_sem=recv_b.at[k],
            device_id=(row, peer),
            device_id_type=MESH,
        )
        copy.start()
        second.append(copy)
    for k in range(1, n):
        first[k - 1].wait_send()
        second[k - 1].wait()


def sum_tp(part, collective_id):
    n = lax.axis_size("tp")
    shape = part.shape
    piece = part.size // HEAD // n
    x = part.reshape(n, piece, HEAD)
    out = pl.pallas_call(
        functools.partial(sum_tp_body, n),
        out_shape=jax.ShapeDtypeStruct((n, piece, HEAD), BF16),
        in_specs=[vmem_spec()],
        out_specs=vmem_spec(),
        scratch_shapes=[
            pltpu.VMEM((n, piece, HEAD), BF16),
            pltpu.VMEM((piece, HEAD), BF16),
            pltpu.SemaphoreType.DMA((n,)),
            pltpu.SemaphoreType.DMA((n,)),
            pltpu.SemaphoreType.DMA((n,)),
            pltpu.SemaphoreType.DMA((n,)),
        ],
        compiler_params=pltpu.CompilerParams(collective_id=collective_id, has_side_effects=True),
        cost_estimate=cost(3e9, 3e7),
        name="sum_tp",
    )(x)
    return out.reshape(shape)


def scatter_tp_body(
    n,
    parts,
    by_rows,
    pair_only,
    *refs,
):
    count = len(parts)
    lhs = refs[0 : 2 * count : 2]
    rhs = refs[1 : 2 * count : 2]
    if pair_only:
        o_ref, away, cross, own, cross_send, cross_recv = refs[2 * count :]
    else:
        (
            o_ref,
            away,
            cross,
            own,
            far,
            near,
            kept,
            turn,
            last,
            cross_send,
            cross_recv,
            far_send,
            far_recv,
            near_send,
            near_recv,
            last_send,
            last_recv,
        ) = refs[2 * count :]
    width = own.shape[-1]
    chips = n // 2
    nz = chips // 2
    row = lax.axis_index("ctx")
    me = lax.axis_index("tp")
    core = lax.rem(me, 2)
    chip = me // 2
    z = lax.rem(chip, nz)
    xh = chip // nz
    partner = me + 1 - 2 * core

    def device(x_at, z_at):
        return (x_at * nz + z_at) * 2 + core

    up_z = lax.rem(z + 1, nz)
    down_z = lax.rem(z + nz - 1, nz)
    across_z = lax.rem(z + 2, nz)
    upper = device(xh, up_z)
    lower = device(xh, down_z)
    opposite = device(1 - xh, z)
    barrier = pltpu.get_barrier_semaphore()
    peers = [partner] if pair_only else [partner, upper, lower, opposite]
    for peer in peers:
        pl.semaphore_signal(barrier, inc=1, device_id=(row, peer), device_id_type=MESH)
    pl.semaphore_wait(barrier, len(peers))

    def product(r, block):
        rows = pl.ds(r * BLK, BLK)
        at = pl.ds(pl.multiple_of(block * width, width), width)
        total = None
        for a, w in zip(lhs, rhs):
            term = nt(a[rows, :], w[at, :]) if by_rows else nn(a[rows, :], w[:, at])
            total = term if total is None else total + term
        return total.astype(BF16)

    def swap(r, zz, xx):
        return pltpu.make_async_remote_copy(
            src_ref=away.at[r, zz, xx],
            dst_ref=cross.at[r, zz, xx],
            send_sem=cross_send.at[r, zz, xx],
            recv_sem=cross_recv.at[r, zz, xx],
            device_id=(row, partner),
            device_id_type=MESH,
        )

    def places(step):
        zz = lax.rem(z + jnp.where(step < 2, 2, jnp.where(step < 4, 1, jnp.where(step < 6, nz - 1, 0))), nz)
        return zz, lax.rem(step, 2)

    def multiply(r):
        def one(step, carry):
            zz, xx = places(step)
            chip_at = xx * nz + zz
            away[r, zz, xx] = product(r, chip_at * 2 + 1 - core)
            swap(r, zz, xx).start()
            own[r, zz, xx] = product(r, chip_at * 2 + core)
            return carry

        lax.fori_loop(0, chips, one, 0)

    def join(r, zz, rows=slice(0, BLK)):
        for xx in range(2):
            swap(r, zz, xx).wait_recv()
            own[r, zz, xx] = (own[r, zz, xx].astype(F32) + cross[r, zz, xx].astype(F32)).astype(BF16)

    half = (slice(0, BLK // 2), slice(BLK // 2, BLK))

    def far_copy(r, way):
        return pltpu.make_async_remote_copy(
            src_ref=own.at[r, across_z, :, half[way], :],
            dst_ref=far.at[r, way],
            send_sem=far_send.at[r, way],
            recv_sem=far_recv.at[r, way],
            device_id=(row, upper if way == 0 else lower),
            device_id_type=MESH,
        )

    def near_copy(r, way):
        return pltpu.make_async_remote_copy(
            src_ref=own.at[r, up_z if way == 0 else down_z],
            dst_ref=near.at[r, way],
            send_sem=near_send.at[r, way],
            recv_sem=near_recv.at[r, way],
            device_id=(row, upper if way == 0 else lower),
            device_id_type=MESH,
        )

    def last_copy(r):
        return pltpu.make_async_remote_copy(
            src_ref=turn.at[r],
            dst_ref=last.at[r],
            send_sem=last_send.at[r],
            recv_sem=last_recv.at[r],
            device_id=(row, opposite),
            device_id_type=MESH,
        )

    def stage_far(r):
        join(r, across_z)
        for way in range(2):
            far_copy(r, way).start()
        for zz in (up_z, down_z, z):
            join(r, zz)

    def stage_near(r):
        for way in range(2):
            far_copy(r, way).wait_recv()
            zz = up_z if way == 0 else down_z
            own[r, zz, :, half[way], :] = (
                own[r, zz, :, half[way], :].astype(F32) + far[r, way].astype(F32)
            ).astype(BF16)
            near_copy(r, way).start()

    def stage_last(r):
        for way in range(2):
            near_copy(r, way).wait_recv()
        for other in range(2):
            xx = xh if other == 0 else 1 - xh
            total = (
                own[r, z, xx].astype(F32)
                + near[r, 0, xx].astype(F32)
                + near[r, 1, xx].astype(F32)
            )
            if other == 0:
                kept[r] = total
            else:
                turn[r] = total.astype(BF16)
        last_copy(r).start()

    def finish(r):
        last_copy(r).wait_recv()
        o_ref[pl.ds(r * BLK, BLK), :] = kept[r] + last[r].astype(F32)

    chunks = own.shape[0]
    if pair_only:
        for r in range(chunks + 1):
            if r < chunks:
                multiply(r)
            if r >= 1:
                for zz in range(nz):
                    join(r - 1, zz)
                    for xx in range(2):
                        o_ref[xx * nz + zz, pl.ds((r - 1) * BLK, BLK), :] = own[r - 1, zz, xx]
    else:
        stages = (multiply, stage_far, stage_near, stage_last, finish)
        for tick in range(chunks + len(stages) - 1):
            for depth in reversed(range(len(stages))):
                if 0 <= tick - depth < chunks:
                    stages[depth](tick - depth)
    for r in range(chunks):
        for zz in range(nz):
            for xx in range(2):
                swap(r, zz, xx).wait_send()
        if not pair_only:
            for way in range(2):
                far_copy(r, way).wait_send()
                near_copy(r, way).wait_send()
            last_copy(r).wait_send()


def scatter_tp(parts, by_rows, pair_only, width, collective_id):
    n = lax.axis_size("tp")
    chips = n // 2
    nz = chips // 2
    rows = parts[0][0].shape[0]
    chunks = rows // BLK
    sems = pltpu.SemaphoreType.DMA
    big = pltpu.VMEM((chunks, nz, 2, BLK, width), BF16)
    scratch = [big, big, big]
    sem_shapes = [sems((chunks, nz, 2))] * 2
    if pair_only:
        out_shape = jax.ShapeDtypeStruct((chips, rows, width), BF16)
    else:
        out_shape = jax.ShapeDtypeStruct((rows, width), F32)
        scratch += [
            pltpu.VMEM((chunks, 2, 2, BLK // 2, width), BF16),
            pltpu.VMEM((chunks, 2, 2, BLK, width), BF16),
            pltpu.VMEM((chunks, BLK, width), F32),
            pltpu.VMEM((chunks, BLK, width), BF16),
            pltpu.VMEM((chunks, BLK, width), BF16),
        ]
        sem_shapes += [sems((chunks, 2))] * 4 + [sems((chunks,))] * 2
    flat = [x for pair in parts for x in pair]
    return pl.pallas_call(
        functools.partial(scatter_tp_body, n, parts, by_rows, pair_only),
        out_shape=out_shape,
        in_specs=[vmem_spec()] * len(flat),
        out_specs=vmem_spec(),
        scratch_shapes=scratch + sem_shapes,
        compiler_params=pltpu.CompilerParams(
            collective_id=collective_id, has_side_effects=True, vmem_limit_bytes=44 << 20
        ),
        cost_estimate=cost(3e10, 1e8),
        name="pair_tp" if pair_only else "scatter_tp",
    )(*flat)


def finalize_body(dim, xq, xkv, low, maps, ctab, stab, q_out, kv_out, delta_out):
    core = lax.rem(lax.axis_index("tp"), 2)
    is_value = core == 1
    for b in range(dim.blocks):
        rows = slice(b * BLK, (b + 1) * BLK)
        m = maps.at[b]
        first = low[0, rows, :]
        second = low[1, rows, :]
        low_q = first[:, :RANK]
        low_kv = jnp.where(is_value, second[:, :RANK], first[:, RANK:])
        low_o = second[:, RANK:]
        cosine = ctab[rows, :]
        sine = stab[rows, :]
        delta_out[rows, :] = nn(low_o, m[:, dim.od])
        turn = xq[rows, :] + nn(low_q, m[:, dim.qu])
        for head in range(dim.heads):
            cols = slice(head * HEAD, (head + 1) * HEAD)
            q = turn[:, cols]
            q_out[rows, cols] = (q * cosine + pltpu.roll(q, HEAD // 2, 1) * sine).astype(BF16)
        kv = xkv[rows, :] + nn(low_kv, m[:, dim.kvu])
        kv = kv.astype(BF16).astype(F32)
        turned = kv * cosine + pltpu.roll(kv, HEAD // 2, 1) * sine
        kv_out[rows, :] = jnp.where(is_value, kv, turned).astype(BF16)


def finalize(dim, xq, xkv, low, maps, ctab, stab):
    cols = dim.heads * HEAD
    return pl.pallas_call(
        functools.partial(finalize_body, dim),
        out_shape=(
            jax.ShapeDtypeStruct((dim.rows, cols), BF16),
            jax.ShapeDtypeStruct((dim.rows, HEAD), BF16),
            jax.ShapeDtypeStruct((dim.rows, cols), F32),
        ),
        in_specs=[vmem_spec()] * 6,
        out_specs=(vmem_spec(),) * 3,
        cost_estimate=cost(1e8, 4e6),
        name="finalize",
    )(xq, xkv, low, maps, ctab, stab)


def gather_kv_body(n, x_ref, o_ref, send_a, recv_a, send_b, recv_b):
    c = lax.axis_index("ctx")
    t = lax.axis_index("tp")
    core = lax.rem(t, 2)
    partner = t + 1 - 2 * core
    barrier = pltpu.get_barrier_semaphore()
    pl.semaphore_signal(barrier, inc=1, device_id=(c, partner), device_id_type=MESH)
    for k in range(1, n):
        pl.semaphore_signal(barrier, inc=1, device_id=(lax.rem(c + k, n), t), device_id_type=MESH)
    pl.semaphore_wait(barrier, n)
    copies = []
    for k in range(1, n):
        copy = pltpu.make_async_remote_copy(
            src_ref=x_ref,
            dst_ref=o_ref.at[core, c],
            send_sem=send_a.at[k],
            recv_sem=recv_a.at[k],
            device_id=(lax.rem(c + k, n), t),
            device_id_type=MESH,
        )
        copy.start()
        copies.append(copy)
    forwards = []
    copy = pltpu.make_async_remote_copy(
        src_ref=x_ref,
        dst_ref=o_ref.at[core, c],
        send_sem=send_b.at[0],
        recv_sem=recv_b.at[0],
        device_id=(c, partner),
        device_id_type=MESH,
    )
    copy.start()
    forwards.append(copy)
    o_ref[core, c] = x_ref[...]
    for k in range(1, n):
        source = lax.rem(c - k + n, n)
        copies[k - 1].wait_recv()
        copy = pltpu.make_async_remote_copy(
            src_ref=o_ref.at[core, source],
            dst_ref=o_ref.at[core, source],
            send_sem=send_b.at[k],
            recv_sem=recv_b.at[k],
            device_id=(c, partner),
            device_id_type=MESH,
        )
        copy.start()
        forwards.append(copy)
    for k in range(1, n):
        copies[k - 1].wait_send()
    for copy in forwards:
        copy.wait()


def gather_kv(kv, collective_id):
    n = lax.axis_size("ctx")
    rows = kv.shape[0]
    return pl.pallas_call(
        functools.partial(gather_kv_body, n),
        out_shape=jax.ShapeDtypeStruct((2, n, rows, HEAD), BF16),
        in_specs=[vmem_spec()],
        out_specs=vmem_spec(),
        scratch_shapes=[pltpu.SemaphoreType.DMA((n,))] * 4,
        compiler_params=pltpu.CompilerParams(collective_id=collective_id, has_side_effects=True),
        cost_estimate=cost(3e9, 3e7),
        name="gather_kv",
    )(kv)


def allowed_tile(j, rows, first_pos, start):
    key_pos = j * rows + lax.broadcasted_iota(jnp.int32, (rows, rows), 0)
    query_pos = first_pos + lax.broadcasted_iota(jnp.int32, (1, rows), 1)
    return (key_pos <= query_pos) & (key_pos >= start)


def attend_body(dim, meta, start_ref, q_ref, kv_ref, o_ref, lse_ref, s_scr, acc):
    rows = dim.rows
    scale = HEAD ** (-0.5)
    lo = meta[0]
    hi = meta[1]
    first_pos = meta[2]
    start = start_ref[...]
    heads = range(dim.heads)

    def scores(j, peaks):
        kj = kv_ref[0, j]
        ok = allowed_tile(j, rows, first_pos, start)
        fresh = []
        for h in heads:
            s = nt(kj, q_ref[:, h * HEAD : (h + 1) * HEAD]) * scale
            s = jnp.where(ok, s, NEG)
            s_scr[h, j] = s
            fresh.append(jnp.maximum(peaks[h], jnp.max(s, axis=0, keepdims=True)))
        return tuple(fresh)

    peaks = lax.fori_loop(lo, hi, scores, tuple(jnp.full((1, rows), NEG, F32) for h in heads))
    acc[...] = jnp.zeros_like(acc)

    def mix(j, sums):
        vt = kv_ref[1, j].T
        fresh = []
        for h in heads:
            p = jnp.exp(s_scr[h, j] - peaks[h])
            fresh.append(sums[h] + jnp.sum(p, axis=0, keepdims=True))
            acc[h] += nn(vt, p.astype(BF16))
        return tuple(fresh)

    sums = lax.fori_loop(lo, hi, mix, tuple(jnp.zeros((1, rows), F32) for h in heads))
    for h in heads:
        o_ref[:, h * HEAD : (h + 1) * HEAD] = (acc[h] / sums[h]).T.astype(BF16)
        lse_ref[h] = peaks[h] + jnp.log(sums[h])


def attend(dim, meta, start, q, kv):
    n = kv.shape[1]
    rows = dim.rows
    return pl.pallas_call(
        functools.partial(attend_body, dim),
        out_shape=(
            jax.ShapeDtypeStruct(q.shape, BF16),
            jax.ShapeDtypeStruct((dim.heads, 1, rows), F32),
        ),
        in_specs=[pl.BlockSpec(memory_space=pltpu.SMEM)] + [vmem_spec()] * 3,
        out_specs=(vmem_spec(), vmem_spec()),
        scratch_shapes=[
            pltpu.VMEM((dim.heads, n, rows, rows), F32),
            pltpu.VMEM((dim.heads, HEAD, rows), F32),
        ],
        compiler_params=pltpu.CompilerParams(vmem_limit_bytes=40 << 20),
        cost_estimate=cost(4 * dim.heads * rows * rows * n * HEAD * 4, 3e7),
        name="attend",
    )(meta, start, q, kv)


def attend_back_body(
    dim, n, meta, start_ref, q_ref, kv_ref, o_ref, lse_ref, do_ref, ctab, stab, dq_ref, dkv_ref, acc
):
    rows = dim.rows
    scale = HEAD ** (-0.5)
    lo = meta[0]
    hi = meta[1]
    first_pos = meta[2]
    start = start_ref[...]
    heads = range(dim.heads)
    acc[...] = jnp.zeros_like(acc)

    def clear(j, carry):
        dkv_ref[0, j] = jnp.zeros((rows, HEAD), BF16)
        dkv_ref[1, j] = jnp.zeros((rows, HEAD), BF16)
        return carry

    lax.fori_loop(0, lo, clear, 0)
    lax.fori_loop(hi, n, clear, 0)
    delta = []
    for h in heads:
        cols = slice(h * HEAD, (h + 1) * HEAD)
        both = do_ref[:, cols].astype(F32) * o_ref[:, cols].astype(F32)
        delta.append(jnp.sum(both.T, axis=0, keepdims=True))

    def step(j, carry):
        kj = kv_ref[0, j]
        vj = kv_ref[1, j]
        kt = kj.T
        ok = allowed_tile(j, rows, first_pos, start)
        dk = jnp.zeros((rows, HEAD), F32)
        dv = jnp.zeros((rows, HEAD), F32)
        for h in heads:
            qh = q_ref[:, h * HEAD : (h + 1) * HEAD]
            doh = do_ref[:, h * HEAD : (h + 1) * HEAD]
            s = jnp.where(ok, nt(kj, qh) * scale, NEG)
            p = jnp.exp(s - lse_ref[h])
            ds = (p * (nt(vj, doh) - delta[h])).astype(BF16)
            acc[h] += nn(kt, ds)
            dk += nn(ds, qh)
            dv += nn(p.astype(BF16), doh)
        dkv_ref[0, j] = (dk * scale).astype(BF16)
        dkv_ref[1, j] = dv.astype(BF16)
        return carry

    lax.fori_loop(lo, hi, step, 0)
    for h in heads:
        dq = (acc[h] * scale).T
        dq = dq * ctab[...] - pltpu.roll(dq, HEAD // 2, 1) * stab[...]
        dq_ref[:, h * HEAD : (h + 1) * HEAD] = dq.astype(BF16)


def attend_back(dim, meta, start, q, kv, out, lse, grad, ctab, stab):
    n = kv.shape[1]
    rows = dim.rows
    return pl.pallas_call(
        functools.partial(attend_back_body, dim, n),
        out_shape=(
            jax.ShapeDtypeStruct(q.shape, BF16),
            jax.ShapeDtypeStruct(kv.shape, BF16),
        ),
        in_specs=[pl.BlockSpec(memory_space=pltpu.SMEM)] + [vmem_spec()] * 8,
        out_specs=(vmem_spec(), vmem_spec()),
        scratch_shapes=[pltpu.VMEM((dim.heads, HEAD, rows), F32)],
        compiler_params=pltpu.CompilerParams(vmem_limit_bytes=40 << 20),
        cost_estimate=cost(10 * dim.heads * rows * rows * n * HEAD * 4, 3e7),
        name="attend_back",
    )(meta, start, q, kv, out, lse, grad, ctab, stab)


def scatter_kv_body(
    n, x_ref, ctab, stab, o_ref, half, mine, arrived, send_a, recv_a, send_b, recv_b
):
    c = lax.axis_index("ctx")
    t = lax.axis_index("tp")
    core = lax.rem(t, 2)
    partner = t + 1 - 2 * core
    barrier = pltpu.get_barrier_semaphore()
    pl.semaphore_signal(barrier, inc=1, device_id=(c, partner), device_id_type=MESH)
    for k in range(1, n):
        pl.semaphore_signal(barrier, inc=1, device_id=(lax.rem(c + k, n), t), device_id_type=MESH)
    pl.semaphore_wait(barrier, n)
    order = list(range(1, n)) + [0]
    swaps = {}
    for k in order:
        copy = pltpu.make_async_remote_copy(
            src_ref=x_ref.at[1 - core, lax.rem(c + k, n)],
            dst_ref=half.at[k],
            send_sem=send_a.at[k],
            recv_sem=recv_a.at[k],
            device_id=(c, partner),
            device_id_type=MESH,
        )
        copy.start()
        swaps[k] = copy
    sends = {}
    for k in range(1, n):
        swaps[k].wait_recv()
        mine[k] = (
            x_ref[core, lax.rem(c + k, n)].astype(F32) + half[k].astype(F32)
        ).astype(BF16)
        copy = pltpu.make_async_remote_copy(
            src_ref=mine.at[k],
            dst_ref=arrived.at[k],
            send_sem=send_b.at[k],
            recv_sem=recv_b.at[k],
            device_id=(lax.rem(c + k, n), t),
            device_id_type=MESH,
        )
        copy.start()
        sends[k] = copy
    swaps[0].wait_recv()
    total = x_ref[core, c].astype(F32) + half[0].astype(F32)
    for k in range(1, n):
        sends[k].wait_recv()
        total = total + arrived[k].astype(F32)
    turned = total * ctab[...] - pltpu.roll(total, HEAD // 2, 1) * stab[...]
    o_ref[...] = jnp.where(core == 1, total, turned).astype(BF16)
    for k in order:
        swaps[k].wait_send()
    for k in range(1, n):
        sends[k].wait_send()


def scatter_kv(grads, ctab, stab, collective_id):
    n = grads.shape[1]
    rows = grads.shape[2]
    return pl.pallas_call(
        functools.partial(scatter_kv_body, n),
        out_shape=jax.ShapeDtypeStruct((rows, HEAD), BF16),
        in_specs=[vmem_spec()] * 3,
        out_specs=vmem_spec(),
        scratch_shapes=[
            pltpu.VMEM((n, rows, HEAD), BF16),
            pltpu.VMEM((n, rows, HEAD), BF16),
            pltpu.VMEM((n, rows, HEAD), BF16),
        ]
        + [pltpu.SemaphoreType.DMA((n,))] * 4,
        compiler_params=pltpu.CompilerParams(collective_id=collective_id, has_side_effects=True),
        cost_estimate=cost(3e9, 3e7),
        name="scatter_kv",
    )(grads, ctab, stab)


def low_grads_body(dim, attn, grad_q, grad_kv, maps, part):
    core = lax.rem(lax.axis_index("tp"), 2)
    m = maps.at[0]
    low_q = nt(grad_q[...], m[:, dim.qu])
    low_out = nt(attn[...], m[:, dim.od])
    low_kv = nt(grad_kv[...], m[:, dim.kvu])
    zero = jnp.zeros_like(low_kv)
    low_k = jnp.where(core == 0, low_kv, zero)
    low_v = jnp.where(core == 1, low_kv, zero)
    part[0] = jnp.concatenate([low_q, low_k], axis=1).astype(BF16)
    part[1] = jnp.concatenate([low_v, low_out], axis=1).astype(BF16)


def low_grads(dim, attn, grad_q, grad_kv, maps):
    cols = dim.heads * HEAD
    return pl.pallas_call(
        functools.partial(low_grads_body, dim),
        out_shape=jax.ShapeDtypeStruct((2, dim.rows, HEAD), BF16),
        grid=(dim.blocks,),
        in_specs=[
            pl.BlockSpec((BLK, cols), lambda b: (b, 0)),
            pl.BlockSpec((BLK, cols), lambda b: (b, 0)),
            pl.BlockSpec((BLK, HEAD), lambda b: (b, 0)),
            pl.BlockSpec((1, RANK, dim.total), lambda b: (b, 0, 0)),
        ],
        out_specs=pl.BlockSpec((2, BLK, HEAD), lambda b: (0, b, 0)),
        cost_estimate=cost(1e8, 4e6),
        name="low_grads",
    )(attn, grad_q, grad_kv, maps)


def block_grads_body(
    dim, index_ref, x, cot, low_in, low_grad, attn, grad_q, grad_kv, maps, out, d_in, d_out
):
    core = lax.rem(lax.axis_index("tp"), 2)
    m = maps.at[0]
    first_t = low_in[0].T
    second_t = low_in[1].T
    low_kv_t = jnp.where(core == 1, second_t[:RANK], first_t[RANK:])
    g_qk_t = low_grad[0].T
    g_vo_t = low_grad[1].T
    xb = x[...]
    out[0, :, dim.dq] = nn(g_qk_t[:RANK], xb).astype(BF16)
    out[0, :, dim.dk] = nn(g_qk_t[RANK:], xb).astype(BF16)
    out[0, :, dim.dv] = nn(g_vo_t[:RANK], xb).astype(BF16)
    out[0, :, dim.qu] = nn(first_t[:RANK], grad_q[...]).astype(BF16)
    out[0, :, dim.kvu] = nn(low_kv_t, grad_kv[...]).astype(BF16)
    out[0, :, dim.od] = nn(second_t[RANK:], attn[...]).astype(BF16)
    out[0, :, dim.ou] = nn(g_vo_t[RANK:], cot[...]).astype(BF16)
    d_out[...] = nn(low_grad[1, :, RANK:], m[:, dim.ou])
    d_in[...] = (
        nn(low_grad[0, :, :RANK], m[:, dim.dq])
        + nn(low_grad[0, :, RANK:], m[:, dim.dk])
        + nn(low_grad[1, :, :RANK], m[:, dim.dv])
    )


def block_grads(dim, index, owners, hidden, cot, low_in, low_grad, attn, grad_q, grad_kv, maps):
    cols = dim.heads * HEAD
    low_spec = pl.BlockSpec((2, BLK, HEAD), lambda b, idx: (0, b, 0))
    wide_spec = pl.BlockSpec((BLK, dim.width), lambda b, idx: (b, 0))
    return pl.pallas_call(
        functools.partial(block_grads_body, dim),
        out_shape=(
            jax.ShapeDtypeStruct((owners, RANK, dim.total), BF16),
            jax.ShapeDtypeStruct((dim.rows, dim.width), F32),
            jax.ShapeDtypeStruct((dim.rows, dim.width), F32),
        ),
        grid_spec=pltpu.PrefetchScalarGridSpec(
            num_scalar_prefetch=1,
            grid=(dim.blocks,),
            in_specs=[
                pl.BlockSpec((BLK, dim.width), lambda b, idx: (b, idx[dim.blocks])),
                wide_spec,
                low_spec,
                low_spec,
                pl.BlockSpec((BLK, cols), lambda b, idx: (b, 0)),
                pl.BlockSpec((BLK, cols), lambda b, idx: (b, 0)),
                pl.BlockSpec((BLK, HEAD), lambda b, idx: (b, 0)),
                pl.BlockSpec((1, RANK, dim.total), lambda b, idx: (b, 0, 0)),
            ],
            out_specs=(
                pl.BlockSpec((1, RANK, dim.total), lambda b, idx: (idx[b], 0, 0)),
                wide_spec,
                wide_spec,
            ),
        ),
        cost_estimate=cost(1e9, 6e6),
        name="block_grads",
    )(index, hidden, cot, low_in, low_grad, attn, grad_q, grad_kv, maps)


def store_body(dim, row_ref, arrived, down, q_up, kv_up, o_down, o_up):
    i = pl.program_id(0)

    @pl.when(i == 0)
    def _():
        for ref in (down, q_up, kv_up, o_down, o_up):
            ref[...] = jnp.zeros_like(ref)

    row = row_ref[i]

    @pl.when(row >= 0)
    def _():
        def piece(at):
            return arrived[0, :, at].astype(F32)

        down[row, 0:RANK, :] += piece(dim.dq)
        down[row, RANK : 2 * RANK, :] += piece(dim.dk)
        down[row, 2 * RANK :, :] += piece(dim.dv)
        q_up[row] += piece(dim.qu)
        kv_up[row] += piece(dim.kvu)
        o_down[row] += piece(dim.od)
        o_up[row] += piece(dim.ou)


def to_store(dim, rows, arrived, shapes):
    count = arrived.shape[0]

    def whole(shape):
        return pl.BlockSpec(shape, lambda i, idx: (0, 0, 0))

    return pl.pallas_call(
        functools.partial(store_body, dim),
        out_shape=tuple(jax.ShapeDtypeStruct(s, F32) for s in shapes),
        grid_spec=pltpu.PrefetchScalarGridSpec(
            num_scalar_prefetch=1,
            grid=(count,),
            in_specs=[pl.BlockSpec((1, RANK, dim.total), lambda i, idx: (i, 0, 0))],
            out_specs=tuple(whole(s) for s in shapes),
        ),
        cost_estimate=cost(0, 6e6),
        name="to_store",
    )(rows, arrived)


def body(
    hidden_input,
    output_cotangent,
    query_projection,
    key_value_projection,
    output_projection,
    adapter_qkv_down_store,
    adapter_query_up,
    adapter_key_value_up,
    adapter_output_down,
    adapter_output_up,
    crop_token_length,
    tenant_per_block,
    tenant_store_row,
):
    ctx_count = lax.axis_size("ctx")
    ctx_index = lax.axis_index("ctx")
    tp_index = lax.axis_index("tp")
    rows_dev = hidden_input.shape[0]
    out_cols = output_cotangent.shape[1]
    tenants = adapter_qkv_down_store.shape[0]
    dim = Dims(rows_dev, out_cols, query_projection.shape[1] // HEAD)
    stores = (
        jnp.swapaxes(adapter_qkv_down_store, 1, 2),
        adapter_query_up,
        adapter_key_value_up,
        jnp.swapaxes(adapter_output_down, 1, 2),
        adapter_output_up,
    )

    tenant_ids = jnp.arange(tenant_store_row.shape[0], dtype=jnp.int32)
    rows_per_block = jnp.sum(
        jnp.where(tenant_per_block[:, None] == tenant_ids[None, :], tenant_store_row[None, :], 0),
        axis=1,
    )
    shard_rows = rows_per_block.reshape(ctx_count, dim.blocks)
    shard_owner = shard_rows // tenants
    served = shard_owner == ctx_index
    served_row = jnp.max(jnp.where(served, shard_rows - ctx_index * tenants, -1), axis=1)
    serve_index = jnp.maximum(served_row, 0)
    my_owner = lax.dynamic_index_in_dim(shard_owner, ctx_index, 0, keepdims=False)
    pick_index = jnp.concatenate([my_owner, tp_index[None]]).astype(jnp.int32)

    my_pos = ctx_index * rows_dev + jnp.arange(rows_dev, dtype=jnp.int32)
    crop_ends = jnp.cumsum(crop_token_length)
    row_start = jnp.max(
        jnp.where(crop_ends[:, None] <= my_pos[None, :], crop_ends[:, None], 0), axis=0
    ).astype(jnp.int32)
    first_pos = ctx_index * rows_dev
    first_start = jnp.max(jnp.where(crop_ends <= first_pos, crop_ends, 0))
    meta = jnp.stack([first_start // rows_dev, ctx_index + 1, first_pos]).astype(jnp.int32)
    start = row_start[None, :]
    half_dim = HEAD // 2
    exponent = jnp.arange(half_dim, dtype=F32) * (2.0 / HEAD)
    frequency = jnp.exp(-exponent * math.log(ROPE_BASE))
    angles = my_pos.astype(F32)[:, None] * jnp.concatenate([frequency, frequency])[None, :]
    sign = jnp.where(jnp.arange(HEAD) < half_dim, -1.0, 1.0).astype(F32)
    ctab = jnp.cos(angles)
    stab = jnp.sin(angles) * sign[None, :]

    fetched = lax.all_to_all(
        serve(dim, serve_index, stores), "ctx", split_axis=0, concat_axis=0, tiled=True
    )
    pieces = lax.all_gather(output_cotangent, "tp", axis=1, tiled=True)
    xq = jnp.dot(hidden_input, query_projection, preferred_element_type=F32)
    xkv = jnp.dot(hidden_input, key_value_projection, preferred_element_type=F32)

    part, maps = low_parts(dim, pick_index, fetched, hidden_input, output_cotangent)
    low_in = sum_tp(part, 0)
    query, keyval, o_delta = finalize(dim, xq, xkv, low_in, maps, ctab, stab)
    kv_all = gather_kv(keyval, 1)
    attn, lse = attend(dim, meta, start, query, kv_all)

    tp_count = lax.axis_size("tp")
    groups = [[2 * i + core for i in range(tp_count // 2)] for core in range(2)]
    paired = scatter_tp(((attn, output_projection),), False, True, out_cols, 4)
    heads_total = lax.psum_scatter(
        paired, "tp", scatter_dimension=0, axis_index_groups=groups, tiled=True
    )[0].astype(F32)

    grad_attn = (
        lax.dot_general(
            pieces, output_projection, (((1,), (1,)), ((), ())), preferred_element_type=F32
        )
        + o_delta
    ).astype(BF16)
    grad_q, grad_kv_all = attend_back(
        dim, meta, start, query, kv_all, attn, lse, grad_attn, ctab, stab
    )
    grad_kv = scatter_kv(grad_kv_all, ctab, stab, 2)

    low_grad = sum_tp(low_grads(dim, attn, grad_q, grad_kv, maps), 0)
    sent, d_in, d_out = block_grads(
        dim,
        pick_index,
        ctx_count,
        hidden_input,
        output_cotangent,
        low_in,
        low_grad,
        attn,
        grad_q,
        grad_kv,
        maps,
    )
    grad_q_late, grad_kv_late, sent = lax.optimization_barrier((grad_q, grad_kv, sent))
    input_total = scatter_tp(
        ((grad_q_late, query_projection), (grad_kv_late, key_value_projection)),
        True,
        False,
        out_cols,
        3,
    )
    output = (heads_total + d_out).astype(BF16)
    hidden_input_gradient = (input_total + d_in).astype(BF16)
    returned = lax.all_to_all(sent, "ctx", split_axis=0, concat_axis=0, tiled=True)
    grads = to_store(dim, served_row, returned, [s.shape for s in stores])
    return (
        output,
        hidden_input_gradient,
        jnp.swapaxes(grads[0], 1, 2),
        grads[1],
        grads[2],
        jnp.swapaxes(grads[3], 1, 2),
        grads[4],
    )


def solution(mesh):
    in_specs = (
        P("ctx", None),
        P("ctx", "tp"),
        P(None, "tp"),
        P(None, "tp"),
        P("tp", None),
        P("ctx", "tp", None),
        P("ctx", None, "tp"),
        P("ctx", None, "tp"),
        P("ctx", "tp", None),
        P("ctx", None, "tp"),
        P(),
        P(),
        P(),
    )
    out_specs = (
        P("ctx", "tp"),
        P("ctx", "tp"),
        P("ctx", "tp", None),
        P("ctx", None, "tp"),
        P("ctx", None, "tp"),
        P("ctx", "tp", None),
        P("ctx", None, "tp"),
    )
    return jax.shard_map(body, mesh=mesh, in_specs=in_specs, out_specs=out_specs, check_vma=False)
```

```python
import functools
import math

import jax
import jax.numpy as jnp
from jax import lax
from jax.experimental import pallas as pl
from jax.experimental.pallas import tpu as pltpu
from jax.sharding import PartitionSpec as P

HEAD = 128
RANK = 64
BLK = 128
NEG = -1e30
ROPE_BASE = 1000000.0
F32 = jnp.float32
BF16 = jnp.bfloat16
MESH = pl.DeviceIdType.MESH
VMEM = pltpu.VMEM


def nn(a, b):
    return lax.dot_general(a, b, (((1,), (0,)), ((), ())), preferred_element_type=F32)


def nt(a, b):
    return lax.dot_general(a, b, (((1,), (1,)), ((), ())), preferred_element_type=F32)


class Dims:
    def __init__(self, rows, width, heads):
        self.rows = rows
        self.width = width
        self.heads = heads
        self.cols = heads * HEAD
        self.blocks = rows // BLK
        self.dq = slice(0, width)
        self.dk = slice(width, 2 * width)
        self.dv = slice(2 * width, 3 * width)
        at = 3 * width
        self.ou = slice(at, at + width)
        at += width
        self.first = at
        self.qu = slice(at, at + self.cols)
        at += self.cols
        self.kvu = slice(at, at + HEAD)
        at += HEAD
        self.od = slice(at, at + self.cols)
        self.total = at + self.cols

    def late(self, at):
        return slice(at.start - self.first, at.stop - self.first)


def any_spec():
    return pl.BlockSpec(memory_space=pl.ANY)


def vmem_spec():
    return pl.BlockSpec(memory_space=VMEM)


def cost(flops, moved):
    return pl.CostEstimate(flops=int(flops), bytes_accessed=int(moved), transcendentals=0)


def front_body(
    dim,
    n_ctx,
    n_tp,
    tenant,
    store_row,
    down_hbm,
    q_up_hbm,
    kv_up_hbm,
    o_down_hbm,
    o_up_hbm,
    cot,
    x_hbm,
    wq_hbm,
    wkv_hbm,
    maps,
    low_out,
    xq,
    xkv,
    cot_all,
    x_mine,
    x,
    wq,
    wkv,
    down,
    q_up,
    kv_up,
    o_down,
    o_up,
    give_a,
    give_b,
    got_a,
    got_b,
    part,
    recv,
    own,
    load_sem,
    sa_send,
    sa_recv,
    sb_send,
    sb_recv,
    side_send,
    side_recv,
    half_send,
    half_recv,
    cross_send,
    cross_recv,
    ar_send,
    ar_recv,
    br_send,
    br_recv,
):
    c = lax.axis_index("ctx")
    me = lax.axis_index("tp")
    core = lax.rem(me, 2)
    partner = me + 1 - 2 * core
    chip = me // 2
    nz = n_tp // 4
    z = lax.rem(chip, nz)
    xh = chip // nz
    up_z = lax.rem(z + 1, nz)
    down_z = lax.rem(z + nz - 1, nz)
    far_z = lax.rem(z + 2, nz)

    def device(x_at, z_at):
        return (x_at * nz + z_at) * 2 + core

    upper = device(xh, up_z)
    lower = device(xh, down_z)
    opposite = device(1 - xh, z)
    barrier = pltpu.get_barrier_semaphore()
    for k in range(1, n_ctx):
        pl.semaphore_signal(
            barrier, inc=1, device_id=(lax.rem(c + k, n_ctx), me), device_id_type=MESH
        )
    for k in range(1, n_tp):
        pl.semaphore_signal(
            barrier, inc=1, device_id=(c, lax.rem(me + k, n_tp)), device_id_type=MESH
        )
    tenants = down.shape[0]

    def row_of(i, b):
        return store_row[tenant[i * dim.blocks + b]]

    def served(i):
        found = 0
        for b in range(dim.blocks):
            row = row_of(i, b) - c * tenants
            found = found + jnp.where((row >= 0) & (row < tenants), row, 0)
        return found

    stores = [
        pltpu.make_async_copy(source, target, load_sem.at[4 + i])
        for i, (source, target) in enumerate(
            (
                (down_hbm, down),
                (o_up_hbm, o_up),
                (q_up_hbm, q_up),
                (kv_up_hbm, kv_up),
                (o_down_hbm, o_down),
            )
        )
    ]
    for load in stores:
        load.start()
    loads = [
        pltpu.make_async_copy(x_hbm, x, load_sem.at[0]),
        pltpu.make_async_copy(wq_hbm, wq, load_sem.at[1]),
        pltpu.make_async_copy(wkv_hbm, wkv, load_sem.at[2]),
        pltpu.make_async_copy(cot, cot_all.at[me], load_sem.at[3]),
    ]
    for load in loads:
        load.start()

    def fill_first(slot_a, at, row):
        slot_a[at, :, dim.dq] = down[row, 0:RANK, :]
        slot_a[at, :, dim.dk] = down[row, RANK : 2 * RANK, :]
        slot_a[at, :, dim.dv] = down[row, 2 * RANK :, :]
        slot_a[at, :, dim.ou] = o_up[row]

    def fill_late(slot_b, at, row):
        slot_b[at, :, dim.late(dim.qu)] = q_up[row]
        slot_b[at, :, dim.late(dim.kvu)] = kv_up[row]
        slot_b[at, :, dim.late(dim.od)] = o_down[row]

    def hand(k, source, target, send, arrive):
        return pltpu.make_async_remote_copy(
            src_ref=source.at[k],
            dst_ref=target.at[c],
            send_sem=send.at[k],
            recv_sem=arrive.at[k],
            device_id=(lax.rem(c + k, n_ctx), me),
            device_id_type=MESH,
        )

    stores[0].wait()
    stores[1].wait()
    order = [4, 5, 3, 6, 2, 7, 1]
    rows_for = {k: served(lax.rem(c + k, n_ctx)) for k in range(n_ctx)}
    for k in order:
        fill_first(give_a, k, rows_for[k])
        if k == order[0]:
            pl.semaphore_wait(barrier, n_ctx + n_tp - 2)
        hand(k, give_a, got_a, sa_send, sa_recv).start()
    fill_first(got_a, c, rows_for[0])

    def block(line, z_at):
        return device(xh if line == 0 else 1 - xh, z_at)

    def side_copy(way, line):
        source = cot if line == 0 else cot_all.at[block(1, z)]
        return pltpu.make_async_remote_copy(
            src_ref=source,
            dst_ref=cot_all.at[block(line, z)],
            send_sem=side_send.at[way, line],
            recv_sem=side_recv.at[way, line],
            device_id=(c, (upper, lower, opposite)[way]),
            device_id_type=MESH,
        )

    middle = dim.rows // 2
    halves = (slice(0, middle), slice(middle, dim.rows))

    def half_copy(way, line):
        at = block(line, down_z if way == 0 else up_z)
        return pltpu.make_async_remote_copy(
            src_ref=cot_all.at[at, halves[way], :],
            dst_ref=cot_all.at[at, halves[way], :],
            send_sem=half_send.at[way, line],
            recv_sem=half_recv.at[way, line],
            device_id=(c, upper if way == 0 else lower),
            device_id_type=MESH,
        )

    def cross_copy(slot, line, z_at):
        at = block(line, z_at)
        return pltpu.make_async_remote_copy(
            src_ref=cot if slot == 0 else cot_all.at[at],
            dst_ref=cot_all.at[at],
            send_sem=cross_send.at[slot],
            recv_sem=cross_recv.at[slot],
            device_id=(c, partner),
            device_id_type=MESH,
        )

    for way in range(2):
        side_copy(way, 0).start()
    passed = [cross_copy(0, 0, z)]
    passed[0].start()
    for load in stores[2:]:
        load.wait()
    for k in order:
        fill_late(give_b, k, rows_for[k])
    fill_late(got_b, c, rows_for[0])

    def pass_on(line, z_at):
        copy = cross_copy(len(passed), line, z_at)
        copy.start()
        passed.append(copy)

    def relay(line):
        side_copy(0, line).wait_recv()
        half_copy(0, line).start()
        pass_on(line, down_z)
        side_copy(1, line).wait_recv()
        half_copy(1, line).start()
        pass_on(line, up_z)

    for load in loads:
        load.wait()
    depth = x.shape[1]
    step = depth // 8
    xq[...] = jnp.zeros_like(xq)
    xkv[...] = jnp.zeros_like(xkv)

    def project(first, last):
        def one(i, carry):
            at = pl.ds(pl.multiple_of(i * step, step), step)
            xs = x[:, at]
            xq[...] += nn(xs, wq[at, :])
            xkv[...] += nn(xs, wkv[at, :])
            return carry

        lax.fori_loop(first, last, one, 0)

    project(0, 5)
    relay(0)
    project(5, 8)
    side_copy(2, 0).start()
    for k in range(1, n_ctx):
        hand(k, give_a, got_a, sa_send, sa_recv).wait_recv()
    for k in order:
        hand(k, give_b, got_b, sb_send, sb_recv).start()
    owners = [row_of(c, b) // tenants for b in range(dim.blocks)]
    mine = pl.ds(pl.multiple_of(me * dim.width, dim.width), dim.width)
    for b in range(dim.blocks):
        rows = slice(b * BLK, (b + 1) * BLK)
        m = got_a[owners[b]]
        xb = x[rows, mine]
        x_mine[b] = xb
        low = [nt(xb, m[:, at]) for at in (dim.dq, dim.dk, dim.dv)]
        low.append(nt(cot[rows, :], m[:, dim.ou]))
        part[rows, :] = jnp.concatenate(low[:2], axis=1).astype(BF16)
        part[dim.rows + b * BLK : dim.rows + (b + 1) * BLK, :] = jnp.concatenate(
            low[2:], axis=1
        ).astype(BF16)
        maps[b, :, : dim.first] = m
    piece = 2 * dim.rows // n_tp

    def slab(peer):
        return pl.ds(pl.multiple_of(peer * piece, piece), piece)

    def spread(k):
        peer = lax.rem(me + k, n_tp)
        return pltpu.make_async_remote_copy(
            src_ref=part.at[slab(peer), :],
            dst_ref=recv.at[k],
            send_sem=ar_send.at[k],
            recv_sem=ar_recv.at[k],
            device_id=(c, peer),
            device_id_type=MESH,
        )

    def share(k):
        return pltpu.make_async_remote_copy(
            src_ref=own,
            dst_ref=low_out.at[slab(me), :],
            send_sem=br_send.at[k],
            recv_sem=br_recv.at[k],
            device_id=(c, lax.rem(me + k, n_tp)),
            device_id_type=MESH,
        )

    for k in range(1, n_tp):
        spread(k).start()
    side_copy(2, 0).wait_recv()
    for way in range(2):
        side_copy(way, 1).start()
    pass_on(1, z)
    total = part[slab(me), :].astype(F32)
    for k in range(1, n_tp):
        spread(k).wait_recv()
        total = total + recv[k].astype(F32)
    own[...] = total.astype(BF16)
    low_out[slab(me), :] = total.astype(BF16)
    for k in range(1, n_tp):
        share(k).start()
    relay(1)
    for line in range(2):
        for way in range(2):
            half_copy(way, line).wait_recv()
        pass_on(line, far_z)
    for k in range(1, n_ctx):
        hand(k, give_b, got_b, sb_send, sb_recv).wait_recv()
    for b in range(dim.blocks):
        maps[b, :, dim.first :] = got_b[owners[b]]
    for k in range(1, n_tp):
        share(k).wait_recv()
    for k in range(1, n_tp):
        spread(k).wait_send()
        share(k).wait_send()
    for k in range(1, n_ctx):
        hand(k, give_a, got_a, sa_send, sa_recv).wait_send()
        hand(k, give_b, got_b, sb_send, sb_recv).wait_send()
    for way in range(3):
        side_copy(way, 0).wait_send()
    for way in range(2):
        side_copy(way, 1).wait_send()
        for line in range(2):
            half_copy(way, line).wait_send()
    for copy in passed:
        copy.wait()


def front(dim, tenant, store_row, stores, cot, hidden, wq, wkv, collective_id):
    n_ctx = lax.axis_size("ctx")
    n_tp = lax.axis_size("tp")
    sems = pltpu.SemaphoreType.DMA
    rest = dim.total - dim.first
    piece = 2 * dim.rows // n_tp
    return pl.pallas_call(
        functools.partial(front_body, dim, n_ctx, n_tp),
        out_shape=(
            jax.ShapeDtypeStruct((dim.blocks, RANK, dim.total), BF16),
            jax.ShapeDtypeStruct((2 * dim.rows, HEAD), BF16),
            jax.ShapeDtypeStruct((dim.rows, dim.cols), F32),
            jax.ShapeDtypeStruct((dim.rows, HEAD), F32),
            jax.ShapeDtypeStruct((n_tp, dim.rows, dim.width), BF16),
            jax.ShapeDtypeStruct((dim.blocks, BLK, dim.width), BF16),
        ),
        in_specs=[pl.BlockSpec(memory_space=pltpu.SMEM)] * 2
        + [any_spec()] * 5
        + [vmem_spec()]
        + [any_spec()] * 3,
        out_specs=(vmem_spec(),) * 4 + (any_spec(), vmem_spec()),
        scratch_shapes=[
            pltpu.VMEM(hidden.shape, BF16),
            pltpu.VMEM(wq.shape, BF16),
            pltpu.VMEM(wkv.shape, BF16),
        ]
        + [pltpu.VMEM(a.shape, BF16) for a in stores]
        + [
            pltpu.VMEM((n_ctx, RANK, dim.first), BF16),
            pltpu.VMEM((n_ctx, RANK, rest), BF16),
            pltpu.VMEM((n_ctx, RANK, dim.first), BF16),
            pltpu.VMEM((n_ctx, RANK, rest), BF16),
            pltpu.VMEM((2 * dim.rows, HEAD), BF16),
            pltpu.VMEM((n_tp, piece, HEAD), BF16),
            pltpu.VMEM((piece, HEAD), BF16),
            sems((9,)),
            sems((n_ctx,)),
            sems((n_ctx,)),
            sems((n_ctx,)),
            sems((n_ctx,)),
            sems((3, 2)),
            sems((3, 2)),
            sems((2, 2)),
            sems((2, 2)),
            sems((n_tp // 2,)),
            sems((n_tp // 2,)),
            sems((n_tp,)),
            sems((n_tp,)),
            sems((n_tp,)),
            sems((n_tp,)),
        ],
        compiler_params=pltpu.CompilerParams(
            collective_id=collective_id, has_side_effects=True, vmem_limit_bytes=60 << 20
        ),
        cost_estimate=cost(3e10, 1e8),
        name="front",
    )(tenant, store_row, *stores, cot, hidden, wq, wkv)


class SumTp:
    def __init__(self, n, part, out, recv, own, send_a, recv_a, send_b, recv_b):
        self.n = n
        self.part = part
        self.out = out
        self.recv = recv
        self.own = own
        self.sems = (send_a, recv_a, send_b, recv_b)
        self.me = lax.axis_index("tp")
        self.row = lax.axis_index("ctx")
        self.piece = part.shape[0] // n

    def slab(self, peer):
        return pl.ds(pl.multiple_of(peer * self.piece, self.piece), self.piece)

    def spread(self, k):
        peer = lax.rem(self.me + k, self.n)
        return pltpu.make_async_remote_copy(
            src_ref=self.part.at[self.slab(peer), :],
            dst_ref=self.recv.at[k],
            send_sem=self.sems[0].at[k],
            recv_sem=self.sems[1].at[k],
            device_id=(self.row, peer),
            device_id_type=MESH,
        )

    def share(self, k):
        return pltpu.make_async_remote_copy(
            src_ref=self.own,
            dst_ref=self.out.at[self.slab(self.me), :],
            send_sem=self.sems[2].at[k],
            recv_sem=self.sems[3].at[k],
            device_id=(self.row, lax.rem(self.me + k, self.n)),
            device_id_type=MESH,
        )

    def start(self):
        for k in range(1, self.n):
            self.spread(k).start()

    def middle(self):
        total = self.part[self.slab(self.me), :].astype(F32)
        for k in range(1, self.n):
            self.spread(k).wait_recv()
            total = total + self.recv[k].astype(F32)
        self.own[...] = total.astype(self.own.dtype)
        self.out[self.slab(self.me), :] = total.astype(self.out.dtype)
        for k in range(1, self.n):
            self.share(k).start()

    def arrive(self):
        for k in range(1, self.n):
            self.share(k).wait_recv()

    def drain(self):
        for k in range(1, self.n):
            self.spread(k).wait_send()
            self.share(k).wait_send()

    @staticmethod
    def scratch(n, shape, dtype):
        piece = shape[0] // n
        return [
            pltpu.VMEM((n, piece, shape[1]), dtype),
            pltpu.VMEM((piece, shape[1]), dtype),
        ] + [pltpu.SemaphoreType.DMA((n,))] * 4


class ScatterTp:
    def __init__(self, n, product, refs):
        (
            self.away,
            self.cross,
            self.own,
            self.far,
            self.near,
            self.kept,
            self.turn,
            self.last,
            self.cross_send,
            self.cross_recv,
            self.far_send,
            self.far_recv,
            self.near_send,
            self.near_recv,
            self.last_send,
            self.last_recv,
        ) = refs
        self.product = product
        self.chunks = self.own.shape[0]
        rows = self.own.shape[-2]
        self.half = (slice(0, rows // 2), slice(rows // 2, rows))
        self.chips = n // 2
        self.nz = self.chips // 2
        nz = self.nz
        self.row = lax.axis_index("ctx")
        me = lax.axis_index("tp")
        self.core = lax.rem(me, 2)
        chip = me // 2
        self.z = lax.rem(chip, nz)
        self.xh = chip // nz
        self.partner = me + 1 - 2 * self.core
        self.up = lax.rem(self.z + 1, nz)
        self.down = lax.rem(self.z + nz - 1, nz)
        self.across = lax.rem(self.z + 2, nz)
        self.upper = self.device(self.xh, self.up)
        self.lower = self.device(self.xh, self.down)
        self.opposite = self.device(1 - self.xh, self.z)

    def device(self, x_at, z_at):
        return (x_at * self.nz + z_at) * 2 + self.core

    def copy(self, source, target, send, arrive, peer):
        return pltpu.make_async_remote_copy(
            src_ref=source,
            dst_ref=target,
            send_sem=send,
            recv_sem=arrive,
            device_id=(self.row, peer),
            device_id_type=MESH,
        )

    def swap(self, r, zz, xx):
        return self.copy(
            self.away.at[r, zz, xx],
            self.cross.at[r, zz, xx],
            self.cross_send.at[r, zz, xx],
            self.cross_recv.at[r, zz, xx],
            self.partner,
        )

    def multiply(self, r, first, end):
        nz = self.nz

        def one(step, carry):
            shift = jnp.where(
                step < 2, 2, jnp.where(step < 4, 1, jnp.where(step < 6, nz - 1, 0))
            )
            zz = lax.rem(self.z + shift, nz)
            xx = lax.rem(step, 2)
            block = (xx * nz + zz) * 2
            self.away[r, zz, xx] = self.product(r, block + 1 - self.core).astype(BF16)
            self.swap(r, zz, xx).start()
            self.own[r, zz, xx] = self.product(r, block + self.core).astype(BF16)
            return carry

        lax.fori_loop(first, end, one, 0)

    def join(self, r, zz):
        for xx in range(2):
            self.swap(r, zz, xx).wait_recv()
            self.own[r, zz, xx] = (
                self.own[r, zz, xx].astype(F32) + self.cross[r, zz, xx].astype(F32)
            ).astype(BF16)

    def far_copy(self, r, way):
        return self.copy(
            self.own.at[r, self.across, :, self.half[way], :],
            self.far.at[r, way],
            self.far_send.at[r, way],
            self.far_recv.at[r, way],
            self.upper if way == 0 else self.lower,
        )

    def near_copy(self, r, way):
        return self.copy(
            self.own.at[r, self.up if way == 0 else self.down],
            self.near.at[r, way],
            self.near_send.at[r, way],
            self.near_recv.at[r, way],
            self.upper if way == 0 else self.lower,
        )

    def last_copy(self, r):
        return self.copy(
            self.turn.at[r], self.last.at[r], self.last_send.at[r], self.last_recv.at[r], self.opposite
        )

    def go_far(self, r):
        self.join(r, self.across)
        for way in range(2):
            self.far_copy(r, way).start()

    def go_near(self, r):
        for way in range(2):
            zz = self.up if way == 0 else self.down
            self.join(r, zz)
            self.far_copy(r, way).wait_recv()
            half = self.half[way]
            self.own[r, zz, :, half, :] = (
                self.own[r, zz, :, half, :].astype(F32) + self.far[r, way].astype(F32)
            ).astype(BF16)
            self.near_copy(r, way).start()

    def begin(self):
        self.multiply(0, 0, 2)
        self.multiply(1, 0, 2)
        self.go_far(0)
        self.multiply(0, 2, self.chips)
        self.go_far(1)
        self.multiply(1, 2, self.chips)

    def go_last(self, r):
        self.join(r, self.z)
        for way in range(2):
            self.near_copy(r, way).wait_recv()
        for other in (1, 0):
            xx = self.xh if other == 0 else 1 - self.xh
            total = (
                self.own[r, self.z, xx].astype(F32)
                + self.near[r, 0, xx].astype(F32)
                + self.near[r, 1, xx].astype(F32)
            )
            if other == 0:
                self.kept[r] = total
            else:
                self.turn[r] = total.astype(BF16)
                self.last_copy(r).start()

    def total(self, r):
        self.last_copy(r).wait_recv()
        return self.kept[r] + self.last[r].astype(F32)

    def drain(self):
        for r in range(self.chunks):
            for zz in range(self.nz):
                for xx in range(2):
                    self.swap(r, zz, xx).wait_send()
            for way in range(2):
                self.far_copy(r, way).wait_send()
                self.near_copy(r, way).wait_send()
            self.last_copy(r).wait_send()

    count = 16

    @staticmethod
    def scratch(n, rows, wide, chunks):
        nz = n // 4
        sems = pltpu.SemaphoreType.DMA
        return (
            [pltpu.VMEM((chunks, nz, 2, rows, wide), BF16)] * 3
            + [
                pltpu.VMEM((chunks, 2, 2, rows // 2, wide), BF16),
                pltpu.VMEM((chunks, 2, 2, rows, wide), BF16),
                pltpu.VMEM((chunks, rows, wide), F32),
                pltpu.VMEM((chunks, rows, wide), BF16),
                pltpu.VMEM((chunks, rows, wide), BF16),
            ]
            + [sems((chunks, nz, 2))] * 2
            + [sems((chunks, 2))] * 4
            + [sems((chunks,))] * 2
        )


def greet(n_ctx, n_tp):
    c = lax.axis_index("ctx")
    t = lax.axis_index("tp")
    barrier = pltpu.get_barrier_semaphore()
    for k in range(1, n_tp):
        pl.semaphore_signal(
            barrier, inc=1, device_id=(c, lax.rem(t + k, n_tp)), device_id_type=MESH
        )
    for k in range(1, n_ctx):
        pl.semaphore_signal(barrier, inc=1, device_id=(lax.rem(c + k, n_ctx), t), device_id_type=MESH)
    return lambda: pl.semaphore_wait(barrier, n_ctx + n_tp - 2)


def tail_body(
    dim,
    n_ctx,
    n,
    tenant,
    store_row,
    part,
    xs,
    maps,
    gq,
    gkv,
    wq_hbm,
    wkv_hbm,
    o_ref,
    low_grad,
    x_got,
    low_got,
    wq,
    wkv,
    gq_t,
    gkv_t,
    x_give,
    low_give,
    load_sem,
    x_send,
    x_recv,
    low_send,
    low_recv,
    *refs,
):
    row = lax.axis_index("ctx")
    me = lax.axis_index("tp")
    entered = greet(n_ctx, n)
    loads = [
        pltpu.make_async_copy(wq_hbm, wq, load_sem.at[0]),
        pltpu.make_async_copy(wkv_hbm, wkv, load_sem.at[1]),
    ]
    for load in loads:
        load.start()
    sums = SumTp(n, part, low_grad, *refs[:6])
    wide = dim.width // 2

    def product(r, block):
        at = pl.ds(pl.multiple_of(block * dim.width + r * wide, wide), wide)
        return nn(wq[at, :], gq_t[...]) + nn(wkv[at, :], gkv_t[...])

    scatter = ScatterTp(n, product, refs[6:])
    tenants = store_row.shape[0] // n_ctx
    owners = [store_row[tenant[row * dim.blocks + b]] // tenants for b in range(dim.blocks)]

    def chosen(k, values):
        owner = lax.rem(row + k, n_ctx)
        value = values[0]
        for b in range(1, dim.blocks):
            value = jnp.where(owners[b] == owner, values[b], value)
        return value

    def hand(k, source, target, send, arrive):
        return pltpu.make_async_remote_copy(
            src_ref=source.at[k],
            dst_ref=target.at[row],
            send_sem=send.at[k],
            recv_sem=arrive.at[k],
            device_id=(lax.rem(row + k, n_ctx), me),
            device_id_type=MESH,
        )

    def hand_x():
        for k in range(1, n_ctx):
            x_give[k] = chosen(k, [xs[b] for b in range(dim.blocks)])
            hand(k, x_give, x_got, x_send, x_recv).start()
        x_got[row] = chosen(0, [xs[b] for b in range(dim.blocks)])

    def lows(b):
        return jnp.concatenate(
            [
                low_grad[b * BLK : (b + 1) * BLK, :],
                low_grad[dim.rows + b * BLK : dim.rows + (b + 1) * BLK, :],
            ],
            axis=0,
        )

    def hand_low():
        sums.arrive()
        values = [lows(b) for b in range(dim.blocks)]
        for k in range(1, n_ctx):
            low_give[k] = chosen(k, values)
            hand(k, low_give, low_got, low_send, low_recv).start()
        low_got[row] = chosen(0, values)

    def finish(r):
        total = scatter.total(r).T
        cols = slice(r * wide, (r + 1) * wide)
        for b in range(dim.blocks):
            rows = slice(b * BLK, (b + 1) * BLK)
            first = low_grad[rows, :]
            second = low_grad[dim.rows + b * BLK : dim.rows + (b + 1) * BLK, :]

            def columns(at):
                return maps[b, :, at.start + cols.start : at.start + cols.stop]

            low = (
                nn(first[:, :RANK], columns(dim.dq))
                + nn(first[:, RANK:], columns(dim.dk))
                + nn(second[:, :RANK], columns(dim.dv))
            )
            o_ref[rows, cols] = (total[rows, :] + low).astype(BF16)

    gq_t[...] = gq[...].T
    gkv_t[...] = gkv[...].T
    entered()
    sums.start()
    for load in loads:
        load.wait()
    scatter.begin()
    hand_x()
    sums.middle()
    for r in range(2):
        scatter.go_near(r)
    hand_low()
    for r in range(2):
        scatter.go_last(r)
    for r in range(2):
        finish(r)
    for k in range(1, n_ctx):
        hand(k, x_give, x_got, x_send, x_recv).wait()
        hand(k, low_give, low_got, low_send, low_recv).wait()
    sums.drain()
    scatter.drain()


def tail(dim, tenant, store_row, part, xs, maps, grad_q, grad_kv, wq, wkv, collective_id):
    n = lax.axis_size("tp")
    n_ctx = lax.axis_size("ctx")
    low_shape = (n_ctx, 2 * BLK, HEAD)
    smem = pl.BlockSpec(memory_space=pltpu.SMEM)
    sems = pltpu.SemaphoreType.DMA
    return pl.pallas_call(
        functools.partial(tail_body, dim, n_ctx, n),
        out_shape=(
            jax.ShapeDtypeStruct((dim.rows, dim.width), BF16),
            jax.ShapeDtypeStruct(part.shape, BF16),
            jax.ShapeDtypeStruct((n_ctx, BLK, dim.width), BF16),
            jax.ShapeDtypeStruct(low_shape, BF16),
        ),
        in_specs=[smem, smem] + [vmem_spec()] * 5 + [any_spec()] * 2,
        out_specs=(vmem_spec(),) * 4,
        scratch_shapes=[
            pltpu.VMEM(wq.shape, BF16),
            pltpu.VMEM(wkv.shape, BF16),
            pltpu.VMEM(grad_q.shape[::-1], BF16),
            pltpu.VMEM(grad_kv.shape[::-1], BF16),
            pltpu.VMEM((n_ctx, BLK, dim.width), BF16),
            pltpu.VMEM(low_shape, BF16),
            sems((2,)),
        ]
        + [sems((n_ctx,))] * 4
        + SumTp.scratch(n, part.shape, BF16)
        + ScatterTp.scratch(n, dim.width // 2, dim.rows, 2),
        compiler_params=pltpu.CompilerParams(
            collective_id=collective_id, has_side_effects=True, vmem_limit_bytes=60 << 20
        ),
        cost_estimate=cost(3e10, 1e8),
        name="tail",
    )(tenant, store_row, part, xs, maps, grad_q, grad_kv, wq, wkv)


def finalize_body(dim, xq, xkv, low, maps, ctab, stab, q_out, kv_out, delta_out):
    core = lax.rem(lax.axis_index("tp"), 2)
    is_value = core == 1
    for b in range(dim.blocks):
        rows = slice(b * BLK, (b + 1) * BLK)
        m = maps.at[b]
        first = low[0, rows, :]
        second = low[1, rows, :]
        low_q = first[:, :RANK]
        low_kv = jnp.where(is_value, second[:, :RANK], first[:, RANK:])
        low_o = second[:, RANK:]
        cosine = ctab[rows, :]
        sine = stab[rows, :]
        delta_out[rows, :] = nn(low_o, m[:, dim.od])
        turn = xq[rows, :] + nn(low_q, m[:, dim.qu])
        for head in range(dim.heads):
            cols = slice(head * HEAD, (head + 1) * HEAD)
            q = turn[:, cols]
            q_out[rows, cols] = (q * cosine + pltpu.roll(q, HEAD // 2, 1) * sine).astype(BF16)
        kv = xkv[rows, :] + nn(low_kv, m[:, dim.kvu])
        kv = kv.astype(BF16).astype(F32)
        turned = kv * cosine + pltpu.roll(kv, HEAD // 2, 1) * sine
        kv_out[rows, :] = jnp.where(is_value, kv, turned).astype(BF16)


def finalize(dim, xq, xkv, low, maps, ctab, stab):
    cols = dim.heads * HEAD
    return pl.pallas_call(
        functools.partial(finalize_body, dim),
        out_shape=(
            jax.ShapeDtypeStruct((dim.rows, cols), BF16),
            jax.ShapeDtypeStruct((dim.rows, HEAD), BF16),
            jax.ShapeDtypeStruct((dim.rows, cols), F32),
        ),
        in_specs=[vmem_spec()] * 6,
        out_specs=(vmem_spec(),) * 3,
        cost_estimate=cost(1e8, 4e6),
        name="finalize",
    )(xq, xkv, low, maps, ctab, stab)


def gather_kv_body(n, x_ref, o_ref, send_a, recv_a, send_b, recv_b):
    c = lax.axis_index("ctx")
    t = lax.axis_index("tp")
    core = lax.rem(t, 2)
    partner = t + 1 - 2 * core
    barrier = pltpu.get_barrier_semaphore()
    pl.semaphore_signal(barrier, inc=1, device_id=(c, partner), device_id_type=MESH)
    for k in range(1, n):
        pl.semaphore_signal(barrier, inc=1, device_id=(lax.rem(c + k, n), t), device_id_type=MESH)
    pl.semaphore_wait(barrier, n)
    copies = []
    for k in range(1, n):
        copy = pltpu.make_async_remote_copy(
            src_ref=x_ref,
            dst_ref=o_ref.at[core, c],
            send_sem=send_a.at[k],
            recv_sem=recv_a.at[k],
            device_id=(lax.rem(c + k, n), t),
            device_id_type=MESH,
        )
        copy.start()
        copies.append(copy)
    forwards = []
    copy = pltpu.make_async_remote_copy(
        src_ref=x_ref,
        dst_ref=o_ref.at[core, c],
        send_sem=send_b.at[0],
        recv_sem=recv_b.at[0],
        device_id=(c, partner),
        device_id_type=MESH,
    )
    copy.start()
    forwards.append(copy)
    o_ref[core, c] = x_ref[...]
    for k in range(1, n):
        source = lax.rem(c - k + n, n)
        copies[k - 1].wait_recv()
        copy = pltpu.make_async_remote_copy(
            src_ref=o_ref.at[core, source],
            dst_ref=o_ref.at[core, source],
            send_sem=send_b.at[k],
            recv_sem=recv_b.at[k],
            device_id=(c, partner),
            device_id_type=MESH,
        )
        copy.start()
        forwards.append(copy)
    for k in range(1, n):
        copies[k - 1].wait_send()
    for copy in forwards:
        copy.wait()


def gather_kv(kv, collective_id):
    n = lax.axis_size("ctx")
    rows = kv.shape[0]
    return pl.pallas_call(
        functools.partial(gather_kv_body, n),
        out_shape=jax.ShapeDtypeStruct((2, n, rows, HEAD), BF16),
        in_specs=[vmem_spec()],
        out_specs=vmem_spec(),
        scratch_shapes=[pltpu.SemaphoreType.DMA((n,))] * 4,
        compiler_params=pltpu.CompilerParams(collective_id=collective_id, has_side_effects=True),
        cost_estimate=cost(3e9, 3e7),
        name="gather_kv",
    )(kv)


def allowed_tile(j, rows, first_pos, start):
    key_pos = j * rows + lax.broadcasted_iota(jnp.int32, (rows, rows), 0)
    query_pos = first_pos + lax.broadcasted_iota(jnp.int32, (1, rows), 1)
    return (key_pos <= query_pos) & (key_pos >= start)


def attend_body(dim, meta, start_ref, q_ref, kv_ref, maps, o_ref, lse_ref, part, s_scr, acc):
    rows = dim.rows
    scale = HEAD ** (-0.5)
    lo = meta[0]
    hi = meta[1]
    first_pos = meta[2]
    start = start_ref[...]
    heads = range(dim.heads)

    def scores(j, peaks):
        kj = kv_ref[0, j]
        ok = allowed_tile(j, rows, first_pos, start)
        fresh = []
        for h in heads:
            s = nt(kj, q_ref[:, h * HEAD : (h + 1) * HEAD]) * scale
            s = jnp.where(ok, s, NEG)
            s_scr[h, j] = s
            fresh.append(jnp.maximum(peaks[h], jnp.max(s, axis=0, keepdims=True)))
        return tuple(fresh)

    peaks = lax.fori_loop(lo, hi, scores, tuple(jnp.full((1, rows), NEG, F32) for h in heads))
    acc[...] = jnp.zeros_like(acc)

    def mix(j, sums):
        vt = kv_ref[1, j].T
        fresh = []
        for h in heads:
            p = jnp.exp(s_scr[h, j] - peaks[h])
            fresh.append(sums[h] + jnp.sum(p, axis=0, keepdims=True))
            acc[h] += nn(vt, p.astype(BF16))
        return tuple(fresh)

    sums = lax.fori_loop(lo, hi, mix, tuple(jnp.zeros((1, rows), F32) for h in heads))
    for h in heads:
        o_ref[:, h * HEAD : (h + 1) * HEAD] = (acc[h] / sums[h]).T.astype(BF16)
        lse_ref[h] = peaks[h] + jnp.log(sums[h])
    for b in range(dim.blocks):
        at = slice(b * BLK, (b + 1) * BLK)
        part[at, :] = nt(o_ref[at, :], maps[b, :, dim.od])


def attend(dim, meta, start, q, kv, maps):
    n = kv.shape[1]
    rows = dim.rows
    return pl.pallas_call(
        functools.partial(attend_body, dim),
        out_shape=(
            jax.ShapeDtypeStruct(q.shape, BF16),
            jax.ShapeDtypeStruct((dim.heads, 1, rows), F32),
            jax.ShapeDtypeStruct((rows, RANK), F32),
        ),
        in_specs=[pl.BlockSpec(memory_space=pltpu.SMEM)] + [vmem_spec()] * 4,
        out_specs=(vmem_spec(),) * 3,
        scratch_shapes=[
            pltpu.VMEM((dim.heads, n, rows, rows), F32),
            pltpu.VMEM((dim.heads, HEAD, rows), F32),
        ],
        compiler_params=pltpu.CompilerParams(vmem_limit_bytes=40 << 20),
        cost_estimate=cost(4 * dim.heads * rows * rows * n * HEAD * 4, 3e7),
        name="attend",
    )(meta, start, q, kv, maps)


def back_body(
    dim,
    n_ctx,
    n_tp,
    start_ref,
    q_ref,
    kv_ref,
    o_ref,
    lse_ref,
    low_part,
    o_delta,
    ctab,
    stab,
    maps,
    cot_hbm,
    wo_hbm,
    out_ref,
    dq_ref,
    gkv_ref,
    low_out,
    cot_ref,
    wo_ref,
    dkv_ref,
    acc,
    grad,
    do_ref,
    half,
    mine,
    arrived,
    load_sem,
    send_a,
    recv_a,
    send_b,
    recv_b,
    *refs,
):
    c = lax.axis_index("ctx")
    t = lax.axis_index("tp")
    core = lax.rem(t, 2)
    partner = t + 1 - 2 * core
    rows = dim.rows
    scale = HEAD ** (-0.5)
    heads = range(dim.heads)
    entered = greet(n_ctx, n_tp)
    load_wo = pltpu.make_async_copy(wo_hbm, wo_ref, load_sem.at[0])
    load_cot = pltpu.make_async_copy(cot_hbm, cot_ref, load_sem.at[1])
    load_wo.start()
    load_cot.start()
    sums = SumTp(n_tp, low_part, low_out, *refs[:6])
    wide = dim.width // 2

    def product(r, block):
        at = block * dim.width + r * wide
        return nn(o_ref[...], wo_ref[:, pl.ds(pl.multiple_of(at, wide), wide)])

    scatter = ScatterTp(n_tp, product, refs[6:])
    entered()
    sums.start()
    load_wo.wait()
    scatter.begin()
    sums.middle()

    load_cot.wait()
    grad[...] = o_delta[...]

    def features(g, carry):
        at = pl.ds(pl.multiple_of(g * dim.width, dim.width), dim.width)
        grad[...] += nt(cot_ref[g], wo_ref[:, at])
        return carry

    middle = n_tp // 2
    lax.fori_loop(0, middle, features, 0)
    for r in range(scatter.chunks):
        scatter.go_near(r)
    lax.fori_loop(middle, n_tp, features, 0)
    do_ref[...] = grad[...].astype(BF16)

    start = start_ref[...]
    acc[...] = jnp.zeros_like(acc)

    def clear(j, carry):
        dkv_ref[0, j] = jnp.zeros((rows, HEAD), BF16)
        dkv_ref[1, j] = jnp.zeros((rows, HEAD), BF16)
        return carry

    lax.fori_loop(c + 1, n_ctx, clear, 0)
    delta = []
    for h in heads:
        cols = slice(h * HEAD, (h + 1) * HEAD)
        both = do_ref[:, cols].astype(F32) * o_ref[:, cols].astype(F32)
        delta.append(jnp.sum(both.T, axis=0, keepdims=True))

    def step(j, carry):
        kj = kv_ref[0, j]
        vj = kv_ref[1, j]
        kt = kj.T
        ok = allowed_tile(j, rows, c * rows, start)
        dk = jnp.zeros((rows, HEAD), F32)
        dv = jnp.zeros((rows, HEAD), F32)
        for h in heads:
            qh = q_ref[:, h * HEAD : (h + 1) * HEAD]
            doh = do_ref[:, h * HEAD : (h + 1) * HEAD]
            s = jnp.where(ok, nt(kj, qh) * scale, NEG)
            p = jnp.exp(s - lse_ref[h])
            ds = (p * (nt(vj, doh) - delta[h])).astype(BF16)
            acc[h] += nn(kt, ds)
            dk += nn(ds, qh)
            dv += nn(p.astype(BF16), doh)
        dkv_ref[0, j] = (dk * scale).astype(BF16)
        dkv_ref[1, j] = dv.astype(BF16)
        return carry

    lax.fori_loop(0, c + 1, step, 0)

    order = list(range(1, n_ctx)) + [0]

    def swap(k):
        return pltpu.make_async_remote_copy(
            src_ref=dkv_ref.at[1 - core, lax.rem(c + k, n_ctx)],
            dst_ref=half.at[k],
            send_sem=send_a.at[k],
            recv_sem=recv_a.at[k],
            device_id=(c, partner),
            device_id_type=MESH,
        )

    def send(k):
        return pltpu.make_async_remote_copy(
            src_ref=mine.at[k],
            dst_ref=arrived.at[k],
            send_sem=send_b.at[k],
            recv_sem=recv_b.at[k],
            device_id=(lax.rem(c + k, n_ctx), t),
            device_id_type=MESH,
        )

    for k in order:
        swap(k).start()
    for h in heads:
        dq = (acc[h] * scale).T
        dq = dq * ctab[...] - pltpu.roll(dq, HEAD // 2, 1) * stab[...]
        dq_ref[:, h * HEAD : (h + 1) * HEAD] = dq.astype(BF16)
    for k in range(1, n_ctx):
        swap(k).wait_recv()
        mine[k] = (
            dkv_ref[core, lax.rem(c + k, n_ctx)].astype(F32) + half[k].astype(F32)
        ).astype(BF16)
        send(k).start()
    for r in range(scatter.chunks):
        scatter.go_last(r)
    sums.arrive()
    for r in range(scatter.chunks):
        total = scatter.total(r)
        cols = slice(r * wide, (r + 1) * wide)
        for b in range(dim.blocks):
            at = slice(b * BLK, (b + 1) * BLK)
            low = nn(
                low_out[at, :].astype(BF16),
                maps[b, :, dim.ou.start + cols.start : dim.ou.start + cols.stop],
            )
            out_ref[at, cols] = (total[at, :] + low).astype(BF16)
    swap(0).wait_recv()
    total = dkv_ref[core, c].astype(F32) + half[0].astype(F32)
    for k in range(1, n_ctx):
        send(k).wait_recv()
        total = total + arrived[k].astype(F32)
    turned = total * ctab[...] - pltpu.roll(total, HEAD // 2, 1) * stab[...]
    gkv_ref[...] = jnp.where(core == 1, total, turned).astype(BF16)
    for k in order:
        swap(k).wait_send()
    for k in range(1, n_ctx):
        send(k).wait_send()
    sums.drain()
    scatter.drain()


def back(dim, start, q, kv, out, lse, low_part, o_delta, ctab, stab, maps, cot_all, wo, collective_id):
    n_ctx = lax.axis_size("ctx")
    n_tp = lax.axis_size("tp")
    rows = dim.rows
    sems = pltpu.SemaphoreType.DMA
    return pl.pallas_call(
        functools.partial(back_body, dim, n_ctx, n_tp),
        out_shape=(
            jax.ShapeDtypeStruct((rows, dim.width), BF16),
            jax.ShapeDtypeStruct(q.shape, BF16),
            jax.ShapeDtypeStruct((rows, HEAD), BF16),
            jax.ShapeDtypeStruct(low_part.shape, F32),
        ),
        in_specs=[vmem_spec()] * 10 + [any_spec()] * 2,
        out_specs=(vmem_spec(),) * 4,
        scratch_shapes=[
            pltpu.VMEM(cot_all.shape, BF16),
            pltpu.VMEM(wo.shape, BF16),
            pltpu.VMEM(kv.shape, BF16),
            pltpu.VMEM((dim.heads, HEAD, rows), F32),
            pltpu.VMEM((rows, dim.cols), F32),
            pltpu.VMEM((rows, dim.cols), BF16),
            pltpu.VMEM((n_ctx, rows, HEAD), BF16),
            pltpu.VMEM((n_ctx, rows, HEAD), BF16),
            pltpu.VMEM((n_ctx, rows, HEAD), BF16),
            sems((2,)),
        ]
        + [sems((n_ctx,))] * 4
        + SumTp.scratch(n_tp, low_part.shape, F32)
        + ScatterTp.scratch(n_tp, rows, dim.width // 2, 2),
        compiler_params=pltpu.CompilerParams(
            collective_id=collective_id, has_side_effects=True, vmem_limit_bytes=60 << 20
        ),
        cost_estimate=cost(3e10, 1e8),
        name="back",
    )(start, q, kv, out, lse, low_part, o_delta, ctab, stab, maps, cot_all, wo)


def middle_body(
    dim, index_ref, cot, low_in, low_out_ref, attn, grad_q, grad_kv, maps, part, out
):
    core = lax.rem(lax.axis_index("tp"), 2)
    m = maps.at[0]
    low_q = nt(grad_q[...], m[:, dim.qu])
    low_kv = nt(grad_kv[...], m[:, dim.kvu])
    zero = jnp.zeros_like(low_kv)
    part[0] = jnp.concatenate([low_q, jnp.where(core == 0, low_kv, zero)], axis=1).astype(BF16)
    part[1] = jnp.concatenate([jnp.where(core == 1, low_kv, zero), zero], axis=1).astype(BF16)
    first_t = low_in[0].T
    second_t = low_in[1].T
    low_kv_t = jnp.where(core == 1, second_t[:RANK], first_t[RANK:])
    base = dim.ou.start

    def put(at, value):
        out[0, :, at.start - base : at.stop - base] = value.astype(BF16)

    put(dim.ou, nn(low_out_ref[...].T.astype(BF16), cot[...]))
    put(dim.qu, nn(first_t[:RANK], grad_q[...]))
    put(dim.kvu, nn(low_kv_t, grad_kv[...]))
    put(dim.od, nn(second_t[RANK:], attn[...]))


def middle(dim, index, owners, cot, low_in, low_out, attn, grad_q, grad_kv, maps):
    small = dim.total - dim.ou.start
    low_spec = pl.BlockSpec((2, BLK, HEAD), lambda b, idx: (0, b, 0))

    def rows_spec(width):
        return pl.BlockSpec((BLK, width), lambda b, idx: (b, 0))

    return pl.pallas_call(
        functools.partial(middle_body, dim),
        out_shape=(
            jax.ShapeDtypeStruct((2, dim.rows, HEAD), BF16),
            jax.ShapeDtypeStruct((owners, RANK, small), BF16),
        ),
        grid_spec=pltpu.PrefetchScalarGridSpec(
            num_scalar_prefetch=1,
            grid=(dim.blocks,),
            in_specs=[
                rows_spec(dim.width),
                low_spec,
                rows_spec(RANK),
                rows_spec(dim.cols),
                rows_spec(dim.cols),
                rows_spec(HEAD),
                pl.BlockSpec((1, RANK, dim.total), lambda b, idx: (b, 0, 0)),
            ],
            out_specs=(
                low_spec,
                pl.BlockSpec((1, RANK, small), lambda b, idx: (idx[b], 0, 0)),
            ),
        ),
        cost_estimate=cost(1e9, 6e6),
        name="middle",
    )(index, cot, low_in, low_out, attn, grad_q, grad_kv, maps)


def store_body(dim, row_ref, arrived, x_got, low_got, down, q_up, kv_up, o_down, o_up):
    i = pl.program_id(0)

    @pl.when(i == 0)
    def _():
        for ref in (down, q_up, kv_up, o_down, o_up):
            ref[...] = jnp.zeros_like(ref)

    row = row_ref[i]

    @pl.when(row >= 0)
    def _():
        base = dim.ou.start

        def piece(at):
            return arrived[0, :, at.start - base : at.stop - base].astype(F32)

        x = x_got[0]
        down[row, 0 : 2 * RANK, :] += nn(low_got[0, :BLK, :].T, x)
        down[row, 2 * RANK :, :] += nn(low_got[0, BLK:, :].T[:RANK], x)
        q_up[row] += piece(dim.qu)
        kv_up[row] += piece(dim.kvu)
        o_down[row] += piece(dim.od)
        o_up[row] += piece(dim.ou)


def to_store(dim, rows, arrived, x_got, low_got, shapes):
    count = arrived.shape[0]

    def whole(shape):
        return pl.BlockSpec(shape, lambda i, idx: (0, 0, 0))

    def one(array):
        return pl.BlockSpec((1,) + array.shape[1:], lambda i, idx: (i, 0, 0))

    return pl.pallas_call(
        functools.partial(store_body, dim),
        out_shape=tuple(jax.ShapeDtypeStruct(s, F32) for s in shapes),
        grid_spec=pltpu.PrefetchScalarGridSpec(
            num_scalar_prefetch=1,
            grid=(count,),
            in_specs=[one(arrived), one(x_got), one(low_got)],
            out_specs=tuple(whole(s) for s in shapes),
        ),
        cost_estimate=cost(0, 6e6),
        name="to_store",
    )(rows, arrived, x_got, low_got)


def body(
    hidden_input,
    output_cotangent,
    query_projection,
    key_value_projection,
    output_projection,
    adapter_qkv_down_store,
    adapter_query_up,
    adapter_key_value_up,
    adapter_output_down,
    adapter_output_up,
    crop_token_length,
    tenant_per_block,
    tenant_store_row,
):
    ctx_count = lax.axis_size("ctx")
    ctx_index = lax.axis_index("ctx")
    tp_index = lax.axis_index("tp")
    rows_dev = hidden_input.shape[0]
    out_cols = output_cotangent.shape[1]
    tenants = adapter_qkv_down_store.shape[0]
    dim = Dims(rows_dev, out_cols, query_projection.shape[1] // HEAD)
    stores = (
        jnp.swapaxes(adapter_qkv_down_store, 1, 2),
        adapter_query_up,
        adapter_key_value_up,
        jnp.swapaxes(adapter_output_down, 1, 2),
        adapter_output_up,
    )

    tenant_ids = jnp.arange(tenant_store_row.shape[0], dtype=jnp.int32)
    rows_per_block = jnp.sum(
        jnp.where(tenant_per_block[:, None] == tenant_ids[None, :], tenant_store_row[None, :], 0),
        axis=1,
    )
    shard_rows = rows_per_block.reshape(ctx_count, dim.blocks)
    shard_owner = shard_rows // tenants
    served = shard_owner == ctx_index
    served_row = jnp.max(jnp.where(served, shard_rows - ctx_index * tenants, -1), axis=1)
    my_owner = lax.dynamic_index_in_dim(shard_owner, ctx_index, 0, keepdims=False)

    my_pos = ctx_index * rows_dev + jnp.arange(rows_dev, dtype=jnp.int32)
    crop_ends = jnp.cumsum(crop_token_length)
    row_start = jnp.max(
        jnp.where(crop_ends[:, None] <= my_pos[None, :], crop_ends[:, None], 0), axis=0
    ).astype(jnp.int32)
    first_pos = ctx_index * rows_dev
    first_start = jnp.max(jnp.where(crop_ends <= first_pos, crop_ends, 0))
    meta = jnp.stack([first_start // rows_dev, ctx_index + 1, first_pos]).astype(jnp.int32)
    start = row_start[None, :]
    half_dim = HEAD // 2
    exponent = jnp.arange(half_dim, dtype=F32) * (2.0 / HEAD)
    frequency = jnp.exp(-exponent * math.log(ROPE_BASE))
    angles = my_pos.astype(F32)[:, None] * jnp.concatenate([frequency, frequency])[None, :]
    sign = jnp.where(jnp.arange(HEAD) < half_dim, -1.0, 1.0).astype(F32)
    ctab = jnp.cos(angles)
    stab = jnp.sin(angles) * sign[None, :]

    maps, low_in, xq, xkv, cot_all, x_mine = front(
        dim,
        tenant_per_block,
        tenant_store_row,
        stores,
        output_cotangent,
        hidden_input,
        query_projection,
        key_value_projection,
        5,
    )
    low_in = low_in.reshape(2, rows_dev, HEAD)
    query, keyval, o_delta = finalize(dim, xq, xkv, low_in, maps, ctab, stab)
    kv_all = gather_kv(keyval, 1)
    attn, lse, low_part = attend(dim, meta, start, query, kv_all, maps)

    output, grad_q, grad_kv, low_out = back(
        dim,
        start,
        query,
        kv_all,
        attn,
        lse,
        low_part,
        o_delta,
        ctab,
        stab,
        maps,
        cot_all,
        output_projection,
        2,
    )
    low_grad_part, sent = middle(
        dim, my_owner, ctx_count, output_cotangent, low_in, low_out, attn, grad_q, grad_kv, maps
    )
    hidden_input_gradient, unused, x_got, low_got = tail(
        dim,
        tenant_per_block,
        tenant_store_row,
        low_grad_part.reshape(2 * rows_dev, HEAD),
        x_mine,
        maps,
        grad_q,
        grad_kv,
        query_projection,
        key_value_projection,
        3,
    )
    returned = lax.all_to_all(sent, "ctx", split_axis=0, concat_axis=0, tiled=True)
    grads = to_store(dim, served_row, returned, x_got, low_got, [s.shape for s in stores])
    return (
        output,
        hidden_input_gradient,
        jnp.swapaxes(grads[0], 1, 2),
        grads[1],
        grads[2],
        jnp.swapaxes(grads[3], 1, 2),
        grads[4],
    )


def solution(mesh):
    in_specs = (
        P("ctx", None),
        P("ctx", "tp"),
        P(None, "tp"),
        P(None, "tp"),
        P("tp", None),
        P("ctx", "tp", None),
        P("ctx", None, "tp"),
        P("ctx", None, "tp"),
        P("ctx", "tp", None),
        P("ctx", None, "tp"),
        P(),
        P(),
        P(),
    )
    out_specs = (
        P("ctx", "tp"),
        P("ctx", "tp"),
        P("ctx", "tp", None),
        P("ctx", None, "tp"),
        P("ctx", None, "tp"),
        P("ctx", "tp", None),
        P("ctx", None, "tp"),
    )
    return jax.shard_map(body, mesh=mesh, in_specs=in_specs, out_specs=out_specs, check_vma=False)
```

```python
import functools
import math

import jax
import jax.numpy as jnp
from jax import lax
from jax.experimental import pallas as pl
from jax.experimental.pallas import tpu as pltpu
from jax.sharding import PartitionSpec as P

HEAD = 128
RANK = 64
BLK = 128
NEG = -1e30
ROPE_BASE = 1000000.0
F32 = jnp.float32
BF16 = jnp.bfloat16
MESH = pl.DeviceIdType.MESH
VMEM = pltpu.VMEM


def nn(a, b):
    return lax.dot_general(a, b, (((1,), (0,)), ((), ())), preferred_element_type=F32)


def nt(a, b):
    return lax.dot_general(a, b, (((1,), (1,)), ((), ())), preferred_element_type=F32)


class Dims:
    def __init__(self, rows, width, heads):
        self.rows = rows
        self.width = width
        self.heads = heads
        self.cols = heads * HEAD
        self.blocks = rows // BLK
        self.dq = slice(0, width)
        self.dk = slice(width, 2 * width)
        self.dv = slice(2 * width, 3 * width)
        at = 3 * width
        self.ou = slice(at, at + width)
        at += width
        self.first = at
        self.qu = slice(at, at + self.cols)
        at += self.cols
        self.kvu = slice(at, at + HEAD)
        at += HEAD
        self.od = slice(at, at + self.cols)
        self.total = at + self.cols

    def late(self, at):
        return slice(at.start - self.first, at.stop - self.first)


def any_spec():
    return pl.BlockSpec(memory_space=pl.ANY)


def vmem_spec():
    return pl.BlockSpec(memory_space=VMEM)


def cost(flops, moved):
    return pl.CostEstimate(flops=int(flops), bytes_accessed=int(moved), transcendentals=0)


def front_body(
    dim,
    n_ctx,
    n_tp,
    tenant,
    store_row,
    down_hbm,
    q_up_hbm,
    kv_up_hbm,
    o_down_hbm,
    o_up_hbm,
    cot,
    x_hbm,
    wq_hbm,
    wkv_hbm,
    maps,
    low_out,
    xq,
    xkv,
    cot_all,
    x_mine,
    x,
    wq,
    wkv,
    down,
    q_up,
    kv_up,
    o_down,
    o_up,
    give_a,
    give_b,
    got_a,
    got_b,
    part,
    recv,
    own,
    load_sem,
    sa_send,
    sa_recv,
    sb_send,
    sb_recv,
    side_send,
    side_recv,
    half_send,
    half_recv,
    cross_send,
    cross_recv,
    ar_send,
    ar_recv,
    br_send,
    br_recv,
):
    c = lax.axis_index("ctx")
    me = lax.axis_index("tp")
    core = lax.rem(me, 2)
    partner = me + 1 - 2 * core
    chip = me // 2
    nz = n_tp // 4
    z = lax.rem(chip, nz)
    xh = chip // nz
    up_z = lax.rem(z + 1, nz)
    down_z = lax.rem(z + nz - 1, nz)
    far_z = lax.rem(z + 2, nz)

    def device(x_at, z_at):
        return (x_at * nz + z_at) * 2 + core

    upper = device(xh, up_z)
    lower = device(xh, down_z)
    opposite = device(1 - xh, z)
    barrier = pltpu.get_barrier_semaphore()
    for k in range(1, n_ctx):
        pl.semaphore_signal(
            barrier, inc=1, device_id=(lax.rem(c + k, n_ctx), me), device_id_type=MESH
        )
    for k in range(1, n_tp):
        pl.semaphore_signal(
            barrier, inc=1, device_id=(c, lax.rem(me + k, n_tp)), device_id_type=MESH
        )
    tenants = down.shape[0]

    def row_of(i, b):
        return store_row[tenant[i * dim.blocks + b]]

    def served(i):
        found = 0
        for b in range(dim.blocks):
            row = row_of(i, b) - c * tenants
            found = found + jnp.where((row >= 0) & (row < tenants), row, 0)
        return found

    stores = [
        pltpu.make_async_copy(source, target, load_sem.at[4 + i])
        for i, (source, target) in enumerate(
            (
                (down_hbm, down),
                (o_up_hbm, o_up),
                (q_up_hbm, q_up),
                (kv_up_hbm, kv_up),
                (o_down_hbm, o_down),
            )
        )
    ]
    for load in stores:
        load.start()
    loads = [
        pltpu.make_async_copy(x_hbm, x, load_sem.at[0]),
        pltpu.make_async_copy(wq_hbm, wq, load_sem.at[1]),
        pltpu.make_async_copy(wkv_hbm, wkv, load_sem.at[2]),
        pltpu.make_async_copy(cot, cot_all.at[me], load_sem.at[3]),
    ]
    for load in loads:
        load.start()

    def fill_first(slot_a, at, row):
        slot_a[at, :, dim.dq] = down[row, 0:RANK, :]
        slot_a[at, :, dim.dk] = down[row, RANK : 2 * RANK, :]
        slot_a[at, :, dim.dv] = down[row, 2 * RANK :, :]
        slot_a[at, :, dim.ou] = o_up[row]

    def fill_late(slot_b, at, row):
        slot_b[at, :, dim.late(dim.qu)] = q_up[row]
        slot_b[at, :, dim.late(dim.kvu)] = kv_up[row]
        slot_b[at, :, dim.late(dim.od)] = o_down[row]

    def hand(k, source, target, send, arrive):
        return pltpu.make_async_remote_copy(
            src_ref=source.at[k],
            dst_ref=target.at[c],
            send_sem=send.at[k],
            recv_sem=arrive.at[k],
            device_id=(lax.rem(c + k, n_ctx), me),
            device_id_type=MESH,
        )

    stores[0].wait()
    stores[1].wait()
    order = [4, 5, 3, 6, 2, 7, 1]
    rows_for = {k: served(lax.rem(c + k, n_ctx)) for k in range(n_ctx)}
    for k in order:
        fill_first(give_a, k, rows_for[k])
        if k == order[0]:
            pl.semaphore_wait(barrier, n_ctx + n_tp - 2)
        hand(k, give_a, got_a, sa_send, sa_recv).start()
    fill_first(got_a, c, rows_for[0])

    def block(line, z_at):
        return device(xh if line == 0 else 1 - xh, z_at)

    def side_copy(way, line):
        source = cot if line == 0 else cot_all.at[block(1, z)]
        return pltpu.make_async_remote_copy(
            src_ref=source,
            dst_ref=cot_all.at[block(line, z)],
            send_sem=side_send.at[way, line],
            recv_sem=side_recv.at[way, line],
            device_id=(c, (upper, lower, opposite)[way]),
            device_id_type=MESH,
        )

    middle = dim.rows // 2
    halves = (slice(0, middle), slice(middle, dim.rows))

    def half_copy(way, line):
        at = block(line, down_z if way == 0 else up_z)
        return pltpu.make_async_remote_copy(
            src_ref=cot_all.at[at, halves[way], :],
            dst_ref=cot_all.at[at, halves[way], :],
            send_sem=half_send.at[way, line],
            recv_sem=half_recv.at[way, line],
            device_id=(c, upper if way == 0 else lower),
            device_id_type=MESH,
        )

    def cross_copy(slot, line, z_at):
        at = block(line, z_at)
        return pltpu.make_async_remote_copy(
            src_ref=cot if slot == 0 else cot_all.at[at],
            dst_ref=cot_all.at[at],
            send_sem=cross_send.at[slot],
            recv_sem=cross_recv.at[slot],
            device_id=(c, partner),
            device_id_type=MESH,
        )

    for way in range(2):
        side_copy(way, 0).start()
    passed = [cross_copy(0, 0, z)]
    passed[0].start()
    for load in stores[2:]:
        load.wait()
    for k in order:
        fill_late(give_b, k, rows_for[k])
    fill_late(got_b, c, rows_for[0])

    def pass_on(line, z_at):
        copy = cross_copy(len(passed), line, z_at)
        copy.start()
        passed.append(copy)

    def relay(line):
        side_copy(0, line).wait_recv()
        half_copy(0, line).start()
        pass_on(line, down_z)
        side_copy(1, line).wait_recv()
        half_copy(1, line).start()
        pass_on(line, up_z)

    for load in loads:
        load.wait()
    depth = x.shape[1]
    step = depth // 8
    xq[...] = jnp.zeros_like(xq)
    xkv[...] = jnp.zeros_like(xkv)

    def project(first, last):
        def one(i, carry):
            at = pl.ds(pl.multiple_of(i * step, step), step)
            xs = x[:, at]
            xq[...] += nn(xs, wq[at, :])
            xkv[...] += nn(xs, wkv[at, :])
            return carry

        lax.fori_loop(first, last, one, 0)

    project(0, 5)
    relay(0)
    project(5, 8)
    side_copy(2, 0).start()
    for k in range(1, n_ctx):
        hand(k, give_a, got_a, sa_send, sa_recv).wait_recv()
    for k in order:
        hand(k, give_b, got_b, sb_send, sb_recv).start()
    owners = [row_of(c, b) // tenants for b in range(dim.blocks)]
    mine = pl.ds(pl.multiple_of(me * dim.width, dim.width), dim.width)
    for b in range(dim.blocks):
        rows = slice(b * BLK, (b + 1) * BLK)
        m = got_a[owners[b]]
        xb = x[rows, mine]
        x_mine[b] = xb
        low = [nt(xb, m[:, at]) for at in (dim.dq, dim.dk, dim.dv)]
        low.append(nt(cot[rows, :], m[:, dim.ou]))
        part[rows, :] = jnp.concatenate(low[:2], axis=1).astype(BF16)
        part[dim.rows + b * BLK : dim.rows + (b + 1) * BLK, :] = jnp.concatenate(
            low[2:], axis=1
        ).astype(BF16)
        maps[b, :, : dim.first] = m
    piece = 2 * dim.rows // n_tp

    def slab(peer):
        return pl.ds(pl.multiple_of(peer * piece, piece), piece)

    def spread(k):
        peer = lax.rem(me + k, n_tp)
        return pltpu.make_async_remote_copy(
            src_ref=part.at[slab(peer), :],
            dst_ref=recv.at[k],
            send_sem=ar_send.at[k],
            recv_sem=ar_recv.at[k],
            device_id=(c, peer),
            device_id_type=MESH,
        )

    def share(k):
        return pltpu.make_async_remote_copy(
            src_ref=own,
            dst_ref=low_out.at[slab(me), :],
            send_sem=br_send.at[k],
            recv_sem=br_recv.at[k],
            device_id=(c, lax.rem(me + k, n_tp)),
            device_id_type=MESH,
        )

    for k in range(1, n_tp):
        spread(k).start()
    side_copy(2, 0).wait_recv()
    for way in range(2):
        side_copy(way, 1).start()
    pass_on(1, z)
    total = part[slab(me), :].astype(F32)
    for k in range(1, n_tp):
        spread(k).wait_recv()
        total = total + recv[k].astype(F32)
    own[...] = total.astype(BF16)
    low_out[slab(me), :] = total.astype(BF16)
    for k in range(1, n_tp):
        share(k).start()
    relay(1)
    for line in range(2):
        for way in range(2):
            half_copy(way, line).wait_recv()
        pass_on(line, far_z)
    for k in range(1, n_ctx):
        hand(k, give_b, got_b, sb_send, sb_recv).wait_recv()
    for b in range(dim.blocks):
        maps[b, :, dim.first :] = got_b[owners[b]]
    for k in range(1, n_tp):
        share(k).wait_recv()
    for k in range(1, n_tp):
        spread(k).wait_send()
        share(k).wait_send()
    for k in range(1, n_ctx):
        hand(k, give_a, got_a, sa_send, sa_recv).wait_send()
        hand(k, give_b, got_b, sb_send, sb_recv).wait_send()
    for way in range(3):
        side_copy(way, 0).wait_send()
    for way in range(2):
        side_copy(way, 1).wait_send()
        for line in range(2):
            half_copy(way, line).wait_send()
    for copy in passed:
        copy.wait()


def front(dim, tenant, store_row, stores, cot, hidden, wq, wkv, collective_id):
    n_ctx = lax.axis_size("ctx")
    n_tp = lax.axis_size("tp")
    sems = pltpu.SemaphoreType.DMA
    rest = dim.total - dim.first
    piece = 2 * dim.rows // n_tp
    return pl.pallas_call(
        functools.partial(front_body, dim, n_ctx, n_tp),
        out_shape=(
            jax.ShapeDtypeStruct((dim.blocks, RANK, dim.total), BF16),
            jax.ShapeDtypeStruct((2 * dim.rows, HEAD), BF16),
            jax.ShapeDtypeStruct((dim.rows, dim.cols), F32),
            jax.ShapeDtypeStruct((dim.rows, HEAD), F32),
            jax.ShapeDtypeStruct((n_tp, dim.rows, dim.width), BF16),
            jax.ShapeDtypeStruct((dim.blocks, BLK, dim.width), BF16),
        ),
        in_specs=[pl.BlockSpec(memory_space=pltpu.SMEM)] * 2
        + [any_spec()] * 5
        + [vmem_spec()]
        + [any_spec()] * 3,
        out_specs=(vmem_spec(),) * 4 + (any_spec(), vmem_spec()),
        scratch_shapes=[
            pltpu.VMEM(hidden.shape, BF16),
            pltpu.VMEM(wq.shape, BF16),
            pltpu.VMEM(wkv.shape, BF16),
        ]
        + [pltpu.VMEM(a.shape, BF16) for a in stores]
        + [
            pltpu.VMEM((n_ctx, RANK, dim.first), BF16),
            pltpu.VMEM((n_ctx, RANK, rest), BF16),
            pltpu.VMEM((n_ctx, RANK, dim.first), BF16),
            pltpu.VMEM((n_ctx, RANK, rest), BF16),
            pltpu.VMEM((2 * dim.rows, HEAD), BF16),
            pltpu.VMEM((n_tp, piece, HEAD), BF16),
            pltpu.VMEM((piece, HEAD), BF16),
            sems((9,)),
            sems((n_ctx,)),
            sems((n_ctx,)),
            sems((n_ctx,)),
            sems((n_ctx,)),
            sems((3, 2)),
            sems((3, 2)),
            sems((2, 2)),
            sems((2, 2)),
            sems((n_tp // 2,)),
            sems((n_tp // 2,)),
            sems((n_tp,)),
            sems((n_tp,)),
            sems((n_tp,)),
            sems((n_tp,)),
        ],
        compiler_params=pltpu.CompilerParams(
            collective_id=collective_id, has_side_effects=True, vmem_limit_bytes=60 << 20
        ),
        cost_estimate=cost(3e10, 1e8),
        name="front",
    )(tenant, store_row, *stores, cot, hidden, wq, wkv)


class SumTp:
    def __init__(self, n, part, out, recv, own, send_a, recv_a, send_b, recv_b):
        self.n = n
        self.part = part
        self.out = out
        self.recv = recv
        self.own = own
        self.sems = (send_a, recv_a, send_b, recv_b)
        self.me = lax.axis_index("tp")
        self.row = lax.axis_index("ctx")
        self.piece = part.shape[0] // n

    def slab(self, peer):
        return pl.ds(pl.multiple_of(peer * self.piece, self.piece), self.piece)

    def spread(self, k):
        peer = lax.rem(self.me + k, self.n)
        return pltpu.make_async_remote_copy(
            src_ref=self.part.at[self.slab(peer), :],
            dst_ref=self.recv.at[k],
            send_sem=self.sems[0].at[k],
            recv_sem=self.sems[1].at[k],
            device_id=(self.row, peer),
            device_id_type=MESH,
        )

    def share(self, k):
        return pltpu.make_async_remote_copy(
            src_ref=self.own,
            dst_ref=self.out.at[self.slab(self.me), :],
            send_sem=self.sems[2].at[k],
            recv_sem=self.sems[3].at[k],
            device_id=(self.row, lax.rem(self.me + k, self.n)),
            device_id_type=MESH,
        )

    def start(self):
        for k in range(1, self.n):
            self.spread(k).start()

    def middle(self):
        total = self.part[self.slab(self.me), :].astype(F32)
        for k in range(1, self.n):
            self.spread(k).wait_recv()
            total = total + self.recv[k].astype(F32)
        self.own[...] = total.astype(self.own.dtype)
        self.out[self.slab(self.me), :] = total.astype(self.out.dtype)
        for k in range(1, self.n):
            self.share(k).start()

    def arrive(self):
        for k in range(1, self.n):
            self.share(k).wait_recv()

    def drain(self):
        for k in range(1, self.n):
            self.spread(k).wait_send()
            self.share(k).wait_send()

    @staticmethod
    def scratch(n, shape, dtype):
        piece = shape[0] // n
        return [
            pltpu.VMEM((n, piece, shape[1]), dtype),
            pltpu.VMEM((piece, shape[1]), dtype),
        ] + [pltpu.SemaphoreType.DMA((n,))] * 4


class ScatterTp:
    def __init__(self, n, product, refs):
        (
            self.away,
            self.cross,
            self.own,
            self.far,
            self.near,
            self.kept,
            self.turn,
            self.last,
            self.cross_send,
            self.cross_recv,
            self.far_send,
            self.far_recv,
            self.near_send,
            self.near_recv,
            self.last_send,
            self.last_recv,
        ) = refs
        self.product = product
        self.chunks = self.own.shape[0]
        rows = self.own.shape[-2]
        self.half = (slice(0, rows // 2), slice(rows // 2, rows))
        self.chips = n // 2
        self.nz = self.chips // 2
        nz = self.nz
        self.row = lax.axis_index("ctx")
        me = lax.axis_index("tp")
        self.core = lax.rem(me, 2)
        chip = me // 2
        self.z = lax.rem(chip, nz)
        self.xh = chip // nz
        self.partner = me + 1 - 2 * self.core
        self.up = lax.rem(self.z + 1, nz)
        self.down = lax.rem(self.z + nz - 1, nz)
        self.across = lax.rem(self.z + 2, nz)
        self.upper = self.device(self.xh, self.up)
        self.lower = self.device(self.xh, self.down)
        self.opposite = self.device(1 - self.xh, self.z)

    def device(self, x_at, z_at):
        return (x_at * self.nz + z_at) * 2 + self.core

    def copy(self, source, target, send, arrive, peer):
        return pltpu.make_async_remote_copy(
            src_ref=source,
            dst_ref=target,
            send_sem=send,
            recv_sem=arrive,
            device_id=(self.row, peer),
            device_id_type=MESH,
        )

    def swap(self, r, zz, xx):
        return self.copy(
            self.away.at[r, zz, xx],
            self.cross.at[r, zz, xx],
            self.cross_send.at[r, zz, xx],
            self.cross_recv.at[r, zz, xx],
            self.partner,
        )

    def multiply(self, r, first, end):
        nz = self.nz

        def one(step, carry):
            shift = jnp.where(
                step < 2, 2, jnp.where(step < 4, 1, jnp.where(step < 6, nz - 1, 0))
            )
            zz = lax.rem(self.z + shift, nz)
            xx = lax.rem(step, 2)
            block = (xx * nz + zz) * 2
            self.away[r, zz, xx] = self.product(r, block + 1 - self.core).astype(BF16)
            self.swap(r, zz, xx).start()
            self.own[r, zz, xx] = self.product(r, block + self.core).astype(BF16)
            return carry

        lax.fori_loop(first, end, one, 0)

    def join(self, r, zz):
        for xx in range(2):
            self.swap(r, zz, xx).wait_recv()
            self.own[r, zz, xx] = (
                self.own[r, zz, xx].astype(F32) + self.cross[r, zz, xx].astype(F32)
            ).astype(BF16)

    def far_copy(self, r, way):
        return self.copy(
            self.own.at[r, self.across, :, self.half[way], :],
            self.far.at[r, way],
            self.far_send.at[r, way],
            self.far_recv.at[r, way],
            self.upper if way == 0 else self.lower,
        )

    def near_copy(self, r, way):
        return self.copy(
            self.own.at[r, self.up if way == 0 else self.down],
            self.near.at[r, way],
            self.near_send.at[r, way],
            self.near_recv.at[r, way],
            self.upper if way == 0 else self.lower,
        )

    def last_copy(self, r):
        return self.copy(
            self.turn.at[r], self.last.at[r], self.last_send.at[r], self.last_recv.at[r], self.opposite
        )

    def go_far(self, r):
        self.join(r, self.across)
        for way in range(2):
            self.far_copy(r, way).start()

    def go_near(self, r):
        for way in range(2):
            zz = self.up if way == 0 else self.down
            self.join(r, zz)
            self.far_copy(r, way).wait_recv()
            half = self.half[way]
            self.own[r, zz, :, half, :] = (
                self.own[r, zz, :, half, :].astype(F32) + self.far[r, way].astype(F32)
            ).astype(BF16)
            self.near_copy(r, way).start()

    def begin(self, between=lambda: None):
        self.multiply(0, 0, 2)
        self.multiply(1, 0, 2)
        self.go_far(0)
        between()
        self.multiply(0, 2, self.chips)
        self.go_far(1)
        self.multiply(1, 2, self.chips)

    def go_last(self, r):
        self.join(r, self.z)
        for way in range(2):
            self.near_copy(r, way).wait_recv()
        for other in (1, 0):
            xx = self.xh if other == 0 else 1 - self.xh
            total = (
                self.own[r, self.z, xx].astype(F32)
                + self.near[r, 0, xx].astype(F32)
                + self.near[r, 1, xx].astype(F32)
            )
            if other == 0:
                self.kept[r] = total
            else:
                self.turn[r] = total.astype(BF16)
                self.last_copy(r).start()

    def total(self, r):
        self.last_copy(r).wait_recv()
        return self.kept[r] + self.last[r].astype(F32)

    def drain(self):
        for r in range(self.chunks):
            for zz in range(self.nz):
                for xx in range(2):
                    self.swap(r, zz, xx).wait_send()
            for way in range(2):
                self.far_copy(r, way).wait_send()
                self.near_copy(r, way).wait_send()
            self.last_copy(r).wait_send()

    count = 16

    @staticmethod
    def scratch(n, rows, wide, chunks):
        nz = n // 4
        sems = pltpu.SemaphoreType.DMA
        return (
            [pltpu.VMEM((chunks, nz, 2, rows, wide), BF16)] * 3
            + [
                pltpu.VMEM((chunks, 2, 2, rows // 2, wide), BF16),
                pltpu.VMEM((chunks, 2, 2, rows, wide), BF16),
                pltpu.VMEM((chunks, rows, wide), F32),
                pltpu.VMEM((chunks, rows, wide), BF16),
                pltpu.VMEM((chunks, rows, wide), BF16),
            ]
            + [sems((chunks, nz, 2))] * 2
            + [sems((chunks, 2))] * 4
            + [sems((chunks,))] * 2
        )


def chooser(dim, n_ctx, tenant, store_row):
    row = lax.axis_index("ctx")
    tenants = store_row.shape[0] // n_ctx
    owners = [store_row[tenant[row * dim.blocks + b]] // tenants for b in range(dim.blocks)]

    def chosen(k, values):
        owner = lax.rem(row + k, n_ctx)
        value = values[0]
        for b in range(1, dim.blocks):
            value = jnp.where(owners[b] == owner, values[b], value)
        return value

    return chosen


def greet(n_ctx, n_tp):
    c = lax.axis_index("ctx")
    t = lax.axis_index("tp")
    barrier = pltpu.get_barrier_semaphore()
    for k in range(1, n_tp):
        pl.semaphore_signal(
            barrier, inc=1, device_id=(c, lax.rem(t + k, n_tp)), device_id_type=MESH
        )
    for k in range(1, n_ctx):
        pl.semaphore_signal(barrier, inc=1, device_id=(lax.rem(c + k, n_ctx), t), device_id_type=MESH)
    return lambda: pl.semaphore_wait(barrier, n_ctx + n_tp - 2)


def tail_body(
    dim,
    n_ctx,
    n,
    tenant,
    store_row,
    part,
    gq,
    gkv,
    wq_hbm,
    wkv_hbm,
    maps_hbm,
    sent,
    o_ref,
    low_grad,
    low_got,
    arrived,
    wq,
    wkv,
    maps,
    gq_t,
    gkv_t,
    low_give,
    load_sem,
    low_send,
    low_recv,
    up_send,
    up_recv,
    *refs,
):
    row = lax.axis_index("ctx")
    me = lax.axis_index("tp")
    entered = greet(n_ctx, n)
    loads = [
        pltpu.make_async_copy(wq_hbm, wq, load_sem.at[0]),
        pltpu.make_async_copy(wkv_hbm, wkv, load_sem.at[1]),
    ]
    later = [
        pltpu.make_async_copy(maps_hbm, maps, load_sem.at[2]),
        pltpu.make_async_copy(sent.at[row], arrived.at[row], load_sem.at[3]),
        pltpu.make_async_copy(low_give.at[0], low_got.at[row], load_sem.at[4]),
    ]
    for load in loads + later[:2]:
        load.start()
    sums = SumTp(n, part, low_grad, *refs[:6])
    wide = dim.width // 2

    def product(r, block):
        at = pl.ds(pl.multiple_of(block * dim.width + r * wide, wide), wide)
        return nn(wq[at, :], gq_t[...]) + nn(wkv[at, :], gkv_t[...])

    scatter = ScatterTp(n, product, refs[6:])
    chosen = chooser(dim, n_ctx, tenant, store_row)

    def hand(k, source, target, send, arrive):
        return pltpu.make_async_remote_copy(
            src_ref=source.at[k],
            dst_ref=target.at[row],
            send_sem=send.at[k],
            recv_sem=arrive.at[k],
            device_id=(lax.rem(row + k, n_ctx), me),
            device_id_type=MESH,
        )

    def hand_all_up():
        for k in range(1, n_ctx):
            hand_up(k).start()

    def hand_up(k):
        peer = lax.rem(row + k, n_ctx)
        return pltpu.make_async_remote_copy(
            src_ref=sent.at[peer],
            dst_ref=arrived.at[row],
            send_sem=up_send.at[k],
            recv_sem=up_recv.at[k],
            device_id=(peer, me),
            device_id_type=MESH,
        )

    def lows(b):
        return jnp.concatenate(
            [
                low_grad[b * BLK : (b + 1) * BLK, :],
                low_grad[dim.rows + b * BLK : dim.rows + (b + 1) * BLK, :],
            ],
            axis=0,
        )

    def hand_low():
        sums.arrive()
        values = [lows(b) for b in range(dim.blocks)]
        for k in range(1, n_ctx):
            low_give[k] = chosen(k, values)
            hand(k, low_give, low_got, low_send, low_recv).start()
        low_give[0] = chosen(0, values)
        later[2].start()

    def finish(r):
        total = scatter.total(r).T
        cols = slice(r * wide, (r + 1) * wide)
        for b in range(dim.blocks):
            rows = slice(b * BLK, (b + 1) * BLK)
            first = low_grad[rows, :]
            second = low_grad[dim.rows + b * BLK : dim.rows + (b + 1) * BLK, :]

            def columns(at):
                return maps[b, :, at.start + cols.start : at.start + cols.stop]

            low = (
                nn(first[:, :RANK], columns(dim.dq))
                + nn(first[:, RANK:], columns(dim.dk))
                + nn(second[:, :RANK], columns(dim.dv))
            )
            o_ref[rows, cols] = (total[rows, :] + low).astype(BF16)

    gq_t[...] = gq[...].T
    gkv_t[...] = gkv[...].T
    entered()
    sums.start()
    for load in loads:
        load.wait()
    scatter.begin(hand_all_up)
    scatter.go_near(0)
    sums.middle()
    scatter.go_near(1)
    hand_low()
    later[0].wait()
    scatter.go_last(0)
    scatter.go_last(1)
    finish(0)
    finish(1)
    for k in range(1, n_ctx):
        hand(k, low_give, low_got, low_send, low_recv).wait()
        hand_up(k).wait()
    for copy in later[1:]:
        copy.wait()
    sums.drain()
    scatter.drain()


def tail(dim, tenant, store_row, part, grad_q, grad_kv, wq, wkv, maps, sent, collective_id):
    n = lax.axis_size("tp")
    n_ctx = lax.axis_size("ctx")
    low_shape = (n_ctx, 2 * BLK, HEAD)
    smem = pl.BlockSpec(memory_space=pltpu.SMEM)
    sems = pltpu.SemaphoreType.DMA
    return pl.pallas_call(
        functools.partial(tail_body, dim, n_ctx, n),
        out_shape=(
            jax.ShapeDtypeStruct((dim.rows, dim.width), BF16),
            jax.ShapeDtypeStruct(part.shape, BF16),
            jax.ShapeDtypeStruct(low_shape, BF16),
            jax.ShapeDtypeStruct(sent.shape, BF16),
        ),
        in_specs=[smem, smem] + [vmem_spec()] * 3 + [any_spec()] * 4,
        out_specs=(vmem_spec(),) * 2 + (any_spec(),) * 2,
        scratch_shapes=[
            pltpu.VMEM(wq.shape, BF16),
            pltpu.VMEM(wkv.shape, BF16),
            pltpu.VMEM(maps.shape, BF16),
            pltpu.VMEM(grad_q.shape[::-1], BF16),
            pltpu.VMEM(grad_kv.shape[::-1], BF16),
            pltpu.VMEM(low_shape, BF16),
            sems((5,)),
        ]
        + [sems((n_ctx,))] * 4
        + SumTp.scratch(n, part.shape, BF16)
        + ScatterTp.scratch(n, dim.width // 2, dim.rows, 2),
        compiler_params=pltpu.CompilerParams(
            collective_id=collective_id, has_side_effects=True, vmem_limit_bytes=60 << 20
        ),
        cost_estimate=cost(3e10, 1e8),
        name="tail",
    )(tenant, store_row, part, grad_q, grad_kv, wq, wkv, maps, sent)


def finalize_body(dim, xq, xkv, low, maps, ctab, stab, q_out, kv_out, delta_out):
    core = lax.rem(lax.axis_index("tp"), 2)
    is_value = core == 1
    for b in range(dim.blocks):
        rows = slice(b * BLK, (b + 1) * BLK)
        m = maps.at[b]
        first = low[0, rows, :]
        second = low[1, rows, :]
        low_q = first[:, :RANK]
        low_kv = jnp.where(is_value, second[:, :RANK], first[:, RANK:])
        low_o = second[:, RANK:]
        cosine = ctab[rows, :]
        sine = stab[rows, :]
        delta_out[rows, :] = nn(low_o, m[:, dim.od])
        turn = xq[rows, :] + nn(low_q, m[:, dim.qu])
        for head in range(dim.heads):
            cols = slice(head * HEAD, (head + 1) * HEAD)
            q = turn[:, cols]
            q_out[rows, cols] = (q * cosine + pltpu.roll(q, HEAD // 2, 1) * sine).astype(BF16)
        kv = xkv[rows, :] + nn(low_kv, m[:, dim.kvu])
        kv = kv.astype(BF16).astype(F32)
        turned = kv * cosine + pltpu.roll(kv, HEAD // 2, 1) * sine
        kv_out[rows, :] = jnp.where(is_value, kv, turned).astype(BF16)


def finalize(dim, xq, xkv, low, maps, ctab, stab):
    cols = dim.heads * HEAD
    return pl.pallas_call(
        functools.partial(finalize_body, dim),
        out_shape=(
            jax.ShapeDtypeStruct((dim.rows, cols), BF16),
            jax.ShapeDtypeStruct((dim.rows, HEAD), BF16),
            jax.ShapeDtypeStruct((dim.rows, cols), F32),
        ),
        in_specs=[vmem_spec()] * 6,
        out_specs=(vmem_spec(),) * 3,
        cost_estimate=cost(1e8, 4e6),
        name="finalize",
    )(xq, xkv, low, maps, ctab, stab)


def gather_kv_body(n, x_ref, o_ref, send_a, recv_a, send_b, recv_b):
    c = lax.axis_index("ctx")
    t = lax.axis_index("tp")
    core = lax.rem(t, 2)
    partner = t + 1 - 2 * core
    barrier = pltpu.get_barrier_semaphore()
    pl.semaphore_signal(barrier, inc=1, device_id=(c, partner), device_id_type=MESH)
    for k in range(1, n):
        pl.semaphore_signal(barrier, inc=1, device_id=(lax.rem(c + k, n), t), device_id_type=MESH)
    pl.semaphore_wait(barrier, n)
    copies = []
    for k in range(1, n):
        copy = pltpu.make_async_remote_copy(
            src_ref=x_ref,
            dst_ref=o_ref.at[core, c],
            send_sem=send_a.at[k],
            recv_sem=recv_a.at[k],
            device_id=(lax.rem(c + k, n), t),
            device_id_type=MESH,
        )
        copy.start()
        copies.append(copy)
    forwards = []
    copy = pltpu.make_async_remote_copy(
        src_ref=x_ref,
        dst_ref=o_ref.at[core, c],
        send_sem=send_b.at[0],
        recv_sem=recv_b.at[0],
        device_id=(c, partner),
        device_id_type=MESH,
    )
    copy.start()
    forwards.append(copy)
    o_ref[core, c] = x_ref[...]
    for k in range(1, n):
        source = lax.rem(c - k + n, n)
        copies[k - 1].wait_recv()
        copy = pltpu.make_async_remote_copy(
            src_ref=o_ref.at[core, source],
            dst_ref=o_ref.at[core, source],
            send_sem=send_b.at[k],
            recv_sem=recv_b.at[k],
            device_id=(c, partner),
            device_id_type=MESH,
        )
        copy.start()
        forwards.append(copy)
    for k in range(1, n):
        copies[k - 1].wait_send()
    for copy in forwards:
        copy.wait()


def gather_kv(kv, collective_id):
    n = lax.axis_size("ctx")
    rows = kv.shape[0]
    return pl.pallas_call(
        functools.partial(gather_kv_body, n),
        out_shape=jax.ShapeDtypeStruct((2, n, rows, HEAD), BF16),
        in_specs=[vmem_spec()],
        out_specs=vmem_spec(),
        scratch_shapes=[pltpu.SemaphoreType.DMA((n,))] * 4,
        compiler_params=pltpu.CompilerParams(collective_id=collective_id, has_side_effects=True),
        cost_estimate=cost(3e9, 3e7),
        name="gather_kv",
    )(kv)


def allowed_tile(j, rows, first_pos, start):
    key_pos = j * rows + lax.broadcasted_iota(jnp.int32, (rows, rows), 0)
    query_pos = first_pos + lax.broadcasted_iota(jnp.int32, (1, rows), 1)
    return (key_pos <= query_pos) & (key_pos >= start)


def attend_body(dim, meta, start_ref, q_ref, kv_ref, maps, o_ref, lse_ref, part, s_scr, acc):
    rows = dim.rows
    scale = HEAD ** (-0.5)
    lo = meta[0]
    hi = meta[1]
    first_pos = meta[2]
    start = start_ref[...]
    heads = range(dim.heads)

    def scores(j, peaks):
        kj = kv_ref[0, j]
        ok = allowed_tile(j, rows, first_pos, start)
        fresh = []
        for h in heads:
            s = nt(kj, q_ref[:, h * HEAD : (h + 1) * HEAD]) * scale
            s = jnp.where(ok, s, NEG)
            s_scr[h, j] = s
            fresh.append(jnp.maximum(peaks[h], jnp.max(s, axis=0, keepdims=True)))
        return tuple(fresh)

    peaks = lax.fori_loop(lo, hi, scores, tuple(jnp.full((1, rows), NEG, F32) for h in heads))
    acc[...] = jnp.zeros_like(acc)

    def mix(j, sums):
        vt = kv_ref[1, j].T
        fresh = []
        for h in heads:
            p = jnp.exp(s_scr[h, j] - peaks[h])
            fresh.append(sums[h] + jnp.sum(p, axis=0, keepdims=True))
            acc[h] += nn(vt, p.astype(BF16))
        return tuple(fresh)

    sums = lax.fori_loop(lo, hi, mix, tuple(jnp.zeros((1, rows), F32) for h in heads))
    for h in heads:
        o_ref[:, h * HEAD : (h + 1) * HEAD] = (acc[h] / sums[h]).T.astype(BF16)
        lse_ref[h] = peaks[h] + jnp.log(sums[h])
    for b in range(dim.blocks):
        at = slice(b * BLK, (b + 1) * BLK)
        part[at, :] = nt(o_ref[at, :], maps[b, :, dim.od])


def attend(dim, meta, start, q, kv, maps):
    n = kv.shape[1]
    rows = dim.rows
    return pl.pallas_call(
        functools.partial(attend_body, dim),
        out_shape=(
            jax.ShapeDtypeStruct(q.shape, BF16),
            jax.ShapeDtypeStruct((dim.heads, 1, rows), F32),
            jax.ShapeDtypeStruct((rows, RANK), F32),
        ),
        in_specs=[pl.BlockSpec(memory_space=pltpu.SMEM)] + [vmem_spec()] * 4,
        out_specs=(vmem_spec(),) * 3,
        scratch_shapes=[
            pltpu.VMEM((dim.heads, n, rows, rows), F32),
            pltpu.VMEM((dim.heads, HEAD, rows), F32),
        ],
        compiler_params=pltpu.CompilerParams(vmem_limit_bytes=40 << 20),
        cost_estimate=cost(4 * dim.heads * rows * rows * n * HEAD * 4, 3e7),
        name="attend",
    )(meta, start, q, kv, maps)


def back_body(
    dim,
    n_ctx,
    n_tp,
    tenant,
    store_row,
    start_ref,
    q_ref,
    o_ref,
    lse_ref,
    low_part,
    o_delta,
    ctab,
    stab,
    xs,
    kv_hbm,
    maps_hbm,
    cot_hbm,
    wo_hbm,
    out_ref,
    dq_ref,
    gkv_ref,
    low_out,
    x_got,
    x_give,
    kv_ref,
    maps,
    cot_ref,
    wo_ref,
    dkv_ref,
    acc,
    grad,
    do_ref,
    half,
    mine,
    arrived,
    load_sem,
    send_a,
    recv_a,
    send_b,
    recv_b,
    x_send,
    x_recv,
    *refs,
):
    c = lax.axis_index("ctx")
    t = lax.axis_index("tp")
    core = lax.rem(t, 2)
    partner = t + 1 - 2 * core
    rows = dim.rows
    scale = HEAD ** (-0.5)
    heads = range(dim.heads)
    entered = greet(n_ctx, n_tp)
    load_wo = pltpu.make_async_copy(wo_hbm, wo_ref, load_sem.at[0])
    load_cot = pltpu.make_async_copy(cot_hbm, cot_ref, load_sem.at[1])
    load_kv = pltpu.make_async_copy(kv_hbm, kv_ref, load_sem.at[2])
    load_maps = pltpu.make_async_copy(maps_hbm, maps, load_sem.at[3])
    for load in (load_wo, load_cot, load_kv, load_maps):
        load.start()
    sums = SumTp(n_tp, low_part, low_out, *refs[:6])
    wide = dim.width // 2

    def product(r, block):
        at = block * dim.width + r * wide
        return nn(o_ref[...], wo_ref[:, pl.ds(pl.multiple_of(at, wide), wide)])

    scatter = ScatterTp(n_tp, product, refs[6:])
    entered()
    sums.start()
    load_wo.wait()
    chosen = chooser(dim, n_ctx, tenant, store_row)
    keep_x = pltpu.make_async_copy(x_give.at[0], x_got.at[c], load_sem.at[4])

    def hand_x(k):
        return pltpu.make_async_remote_copy(
            src_ref=x_give.at[k],
            dst_ref=x_got.at[c],
            send_sem=x_send.at[k],
            recv_sem=x_recv.at[k],
            device_id=(lax.rem(c + k, n_ctx), t),
            device_id_type=MESH,
        )

    def hand_all_x():
        for k in range(n_ctx):
            x_give[k] = chosen(k, [xs[b] for b in range(dim.blocks)])
            if k == 0:
                keep_x.start()
            else:
                hand_x(k).start()

    scatter.begin(hand_all_x)
    sums.middle()

    for load in (load_cot, load_kv, load_maps):
        load.wait()
    grad[...] = o_delta[...]

    def features(g, carry):
        at = pl.ds(pl.multiple_of(g * dim.width, dim.width), dim.width)
        grad[...] += nt(cot_ref[g], wo_ref[:, at])
        return carry

    middle = n_tp // 2
    lax.fori_loop(0, middle, features, 0)
    for r in range(scatter.chunks):
        scatter.go_near(r)
    lax.fori_loop(middle, n_tp, features, 0)
    do_ref[...] = grad[...].astype(BF16)

    start = start_ref[...]
    acc[...] = jnp.zeros_like(acc)

    def clear(j, carry):
        dkv_ref[0, j] = jnp.zeros((rows, HEAD), BF16)
        dkv_ref[1, j] = jnp.zeros((rows, HEAD), BF16)
        return carry

    lax.fori_loop(c + 1, n_ctx, clear, 0)
    delta = []
    for h in heads:
        cols = slice(h * HEAD, (h + 1) * HEAD)
        both = do_ref[:, cols].astype(F32) * o_ref[:, cols].astype(F32)
        delta.append(jnp.sum(both.T, axis=0, keepdims=True))

    def step(j, carry):
        kj = kv_ref[0, j]
        vj = kv_ref[1, j]
        kt = kj.T
        ok = allowed_tile(j, rows, c * rows, start)
        dk = jnp.zeros((rows, HEAD), F32)
        dv = jnp.zeros((rows, HEAD), F32)
        for h in heads:
            qh = q_ref[:, h * HEAD : (h + 1) * HEAD]
            doh = do_ref[:, h * HEAD : (h + 1) * HEAD]
            s = jnp.where(ok, nt(kj, qh) * scale, NEG)
            p = jnp.exp(s - lse_ref[h])
            ds = (p * (nt(vj, doh) - delta[h])).astype(BF16)
            acc[h] += nn(kt, ds)
            dk += nn(ds, qh)
            dv += nn(p.astype(BF16), doh)
        dkv_ref[0, j] = (dk * scale).astype(BF16)
        dkv_ref[1, j] = dv.astype(BF16)
        return carry

    lax.fori_loop(0, c + 1, step, 0)

    order = list(range(1, n_ctx)) + [0]

    def swap(k):
        return pltpu.make_async_remote_copy(
            src_ref=dkv_ref.at[1 - core, lax.rem(c + k, n_ctx)],
            dst_ref=half.at[k],
            send_sem=send_a.at[k],
            recv_sem=recv_a.at[k],
            device_id=(c, partner),
            device_id_type=MESH,
        )

    def send(k):
        return pltpu.make_async_remote_copy(
            src_ref=mine.at[k],
            dst_ref=arrived.at[k],
            send_sem=send_b.at[k],
            recv_sem=recv_b.at[k],
            device_id=(lax.rem(c + k, n_ctx), t),
            device_id_type=MESH,
        )

    for k in order:
        swap(k).start()
    for h in heads:
        dq = (acc[h] * scale).T
        dq = dq * ctab[...] - pltpu.roll(dq, HEAD // 2, 1) * stab[...]
        dq_ref[:, h * HEAD : (h + 1) * HEAD] = dq.astype(BF16)
    for k in range(1, n_ctx):
        swap(k).wait_recv()
        mine[k] = (
            dkv_ref[core, lax.rem(c + k, n_ctx)].astype(F32) + half[k].astype(F32)
        ).astype(BF16)
        send(k).start()
    for r in range(scatter.chunks):
        scatter.go_last(r)
    sums.arrive()
    for r in range(scatter.chunks):
        total = scatter.total(r)
        cols = slice(r * wide, (r + 1) * wide)
        for b in range(dim.blocks):
            at = slice(b * BLK, (b + 1) * BLK)
            low = nn(
                low_out[at, :].astype(BF16),
                maps[b, :, dim.ou.start + cols.start : dim.ou.start + cols.stop],
            )
            out_ref[at, cols] = (total[at, :] + low).astype(BF16)
    swap(0).wait_recv()
    total = dkv_ref[core, c].astype(F32) + half[0].astype(F32)
    for k in range(1, n_ctx):
        send(k).wait_recv()
        total = total + arrived[k].astype(F32)
    turned = total * ctab[...] - pltpu.roll(total, HEAD // 2, 1) * stab[...]
    gkv_ref[...] = jnp.where(core == 1, total, turned).astype(BF16)
    for k in order:
        swap(k).wait_send()
    for k in range(1, n_ctx):
        send(k).wait_send()
        hand_x(k).wait()
    keep_x.wait()
    sums.drain()
    scatter.drain()


def back(dim, tenant, store_row, start, q, kv, out, lse, low_part, o_delta, ctab, stab, xs, maps, cot_all, wo, collective_id):
    n_ctx = lax.axis_size("ctx")
    n_tp = lax.axis_size("tp")
    rows = dim.rows
    sems = pltpu.SemaphoreType.DMA
    return pl.pallas_call(
        functools.partial(back_body, dim, n_ctx, n_tp),
        out_shape=(
            jax.ShapeDtypeStruct((rows, dim.width), BF16),
            jax.ShapeDtypeStruct(q.shape, BF16),
            jax.ShapeDtypeStruct((rows, HEAD), BF16),
            jax.ShapeDtypeStruct(low_part.shape, F32),
            jax.ShapeDtypeStruct((n_ctx,) + xs.shape[1:], BF16),
        ),
        in_specs=[pl.BlockSpec(memory_space=pltpu.SMEM)] * 2 + [vmem_spec()] * 9 + [any_spec()] * 4,
        out_specs=(vmem_spec(),) * 4 + (any_spec(),),
        scratch_shapes=[
            pltpu.VMEM((n_ctx,) + xs.shape[1:], BF16),
            pltpu.VMEM(kv.shape, BF16),
            pltpu.VMEM(maps.shape, BF16),
            pltpu.VMEM(cot_all.shape, BF16),
            pltpu.VMEM(wo.shape, BF16),
            pltpu.VMEM(kv.shape, BF16),
            pltpu.VMEM((dim.heads, HEAD, rows), F32),
            pltpu.VMEM((rows, dim.cols), F32),
            pltpu.VMEM((rows, dim.cols), BF16),
            pltpu.VMEM((n_ctx, rows, HEAD), BF16),
            pltpu.VMEM((n_ctx, rows, HEAD), BF16),
            pltpu.VMEM((n_ctx, rows, HEAD), BF16),
            sems((5,)),
        ]
        + [sems((n_ctx,))] * 6
        + SumTp.scratch(n_tp, low_part.shape, F32)
        + ScatterTp.scratch(n_tp, rows, dim.width // 2, 2),
        compiler_params=pltpu.CompilerParams(
            collective_id=collective_id, has_side_effects=True, vmem_limit_bytes=60 << 20
        ),
        cost_estimate=cost(3e10, 1e8),
        name="back",
    )(tenant, store_row, start, q, out, lse, low_part, o_delta, ctab, stab, xs, kv, maps, cot_all, wo)


def middle_body(
    dim, index_ref, cot, low_in, low_out_ref, attn, grad_q, grad_kv, maps, part, out
):
    core = lax.rem(lax.axis_index("tp"), 2)
    m = maps.at[0]
    low_q = nt(grad_q[...], m[:, dim.qu])
    low_kv = nt(grad_kv[...], m[:, dim.kvu])
    zero = jnp.zeros_like(low_kv)
    part[0] = jnp.concatenate([low_q, jnp.where(core == 0, low_kv, zero)], axis=1).astype(BF16)
    part[1] = jnp.concatenate([jnp.where(core == 1, low_kv, zero), zero], axis=1).astype(BF16)
    first_t = low_in[0].T
    second_t = low_in[1].T
    low_kv_t = jnp.where(core == 1, second_t[:RANK], first_t[RANK:])
    base = dim.ou.start

    def put(at, value):
        out[0, :, at.start - base : at.stop - base] = value.astype(BF16)

    put(dim.ou, nn(low_out_ref[...].T.astype(BF16), cot[...]))
    put(dim.qu, nn(first_t[:RANK], grad_q[...]))
    put(dim.kvu, nn(low_kv_t, grad_kv[...]))
    put(dim.od, nn(second_t[RANK:], attn[...]))


def middle(dim, index, owners, cot, low_in, low_out, attn, grad_q, grad_kv, maps):
    small = dim.total - dim.ou.start
    low_spec = pl.BlockSpec((2, BLK, HEAD), lambda b, idx: (0, b, 0))

    def rows_spec(width):
        return pl.BlockSpec((BLK, width), lambda b, idx: (b, 0))

    return pl.pallas_call(
        functools.partial(middle_body, dim),
        out_shape=(
            jax.ShapeDtypeStruct((2, dim.rows, HEAD), BF16),
            jax.ShapeDtypeStruct((owners, RANK, small), BF16),
        ),
        grid_spec=pltpu.PrefetchScalarGridSpec(
            num_scalar_prefetch=1,
            grid=(dim.blocks,),
            in_specs=[
                rows_spec(dim.width),
                low_spec,
                rows_spec(RANK),
                rows_spec(dim.cols),
                rows_spec(dim.cols),
                rows_spec(HEAD),
                pl.BlockSpec((1, RANK, dim.total), lambda b, idx: (b, 0, 0)),
            ],
            out_specs=(
                low_spec,
                pl.BlockSpec((1, RANK, small), lambda b, idx: (idx[b], 0, 0)),
            ),
        ),
        cost_estimate=cost(1e9, 6e6),
        name="middle",
    )(index, cot, low_in, low_out, attn, grad_q, grad_kv, maps)


def store_body(dim, row_ref, arrived, x_got, low_got, down, q_up, kv_up, o_down, o_up):
    for ref in (down, q_up, kv_up, o_down, o_up):
        ref[...] = jnp.zeros_like(ref)
    base = dim.ou.start

    def one(i, carry):
        row = row_ref[i]

        @pl.when(row >= 0)
        def _():
            def piece(at):
                return arrived[i, :, at.start - base : at.stop - base].astype(F32)

            x = x_got[i]
            down[row, 0 : 2 * RANK, :] += nn(low_got[i, :BLK, :].T, x)
            down[row, 2 * RANK :, :] += nn(low_got[i, BLK:, :].T[:RANK], x)
            q_up[row] += piece(dim.qu)
            kv_up[row] += piece(dim.kvu)
            o_down[row] += piece(dim.od)
            o_up[row] += piece(dim.ou)

        return carry

    lax.fori_loop(0, arrived.shape[0], one, 0)


def to_store(dim, rows, arrived, x_got, low_got, shapes):
    return pl.pallas_call(
        functools.partial(store_body, dim),
        out_shape=tuple(jax.ShapeDtypeStruct(s, F32) for s in shapes),
        in_specs=[pl.BlockSpec(memory_space=pltpu.SMEM)] + [vmem_spec()] * 3,
        out_specs=tuple(vmem_spec() for s in shapes),
        cost_estimate=cost(0, 6e6),
        name="to_store",
    )(rows, arrived, x_got, low_got)


def body(
    hidden_input,
    output_cotangent,
    query_projection,
    key_value_projection,
    output_projection,
    adapter_qkv_down_store,
    adapter_query_up,
    adapter_key_value_up,
    adapter_output_down,
    adapter_output_up,
    crop_token_length,
    tenant_per_block,
    tenant_store_row,
):
    ctx_count = lax.axis_size("ctx")
    ctx_index = lax.axis_index("ctx")
    tp_index = lax.axis_index("tp")
    rows_dev = hidden_input.shape[0]
    out_cols = output_cotangent.shape[1]
    tenants = adapter_qkv_down_store.shape[0]
    dim = Dims(rows_dev, out_cols, query_projection.shape[1] // HEAD)
    stores = (
        jnp.swapaxes(adapter_qkv_down_store, 1, 2),
        adapter_query_up,
        adapter_key_value_up,
        jnp.swapaxes(adapter_output_down, 1, 2),
        adapter_output_up,
    )

    tenant_ids = jnp.arange(tenant_store_row.shape[0], dtype=jnp.int32)
    rows_per_block = jnp.sum(
        jnp.where(tenant_per_block[:, None] == tenant_ids[None, :], tenant_store_row[None, :], 0),
        axis=1,
    )
    shard_rows = rows_per_block.reshape(ctx_count, dim.blocks)
    shard_owner = shard_rows // tenants
    served = shard_owner == ctx_index
    served_row = jnp.max(jnp.where(served, shard_rows - ctx_index * tenants, -1), axis=1)
    my_owner = lax.dynamic_index_in_dim(shard_owner, ctx_index, 0, keepdims=False)

    my_pos = ctx_index * rows_dev + jnp.arange(rows_dev, dtype=jnp.int32)
    crop_ends = jnp.cumsum(crop_token_length)
    row_start = jnp.max(
        jnp.where(crop_ends[:, None] <= my_pos[None, :], crop_ends[:, None], 0), axis=0
    ).astype(jnp.int32)
    first_pos = ctx_index * rows_dev
    first_start = jnp.max(jnp.where(crop_ends <= first_pos, crop_ends, 0))
    meta = jnp.stack([first_start // rows_dev, ctx_index + 1, first_pos]).astype(jnp.int32)
    start = row_start[None, :]
    half_dim = HEAD // 2
    exponent = jnp.arange(half_dim, dtype=F32) * (2.0 / HEAD)
    frequency = jnp.exp(-exponent * math.log(ROPE_BASE))
    angles = my_pos.astype(F32)[:, None] * jnp.concatenate([frequency, frequency])[None, :]
    sign = jnp.where(jnp.arange(HEAD) < half_dim, -1.0, 1.0).astype(F32)
    ctab = jnp.cos(angles)
    stab = jnp.sin(angles) * sign[None, :]

    maps, low_in, xq, xkv, cot_all, x_mine = front(
        dim,
        tenant_per_block,
        tenant_store_row,
        stores,
        output_cotangent,
        hidden_input,
        query_projection,
        key_value_projection,
        5,
    )
    low_in = low_in.reshape(2, rows_dev, HEAD)
    query, keyval, o_delta = finalize(dim, xq, xkv, low_in, maps, ctab, stab)
    kv_all = gather_kv(keyval, 1)
    attn, lse, low_part = attend(dim, meta, start, query, kv_all, maps)

    output, grad_q, grad_kv, low_out, x_got = back(
        dim,
        tenant_per_block,
        tenant_store_row,
        start,
        query,
        kv_all,
        attn,
        lse,
        low_part,
        o_delta,
        ctab,
        stab,
        x_mine,
        maps,
        cot_all,
        output_projection,
        2,
    )
    low_grad_part, sent = middle(
        dim, my_owner, ctx_count, output_cotangent, low_in, low_out, attn, grad_q, grad_kv, maps
    )
    hidden_input_gradient, unused, low_got, returned = tail(
        dim,
        tenant_per_block,
        tenant_store_row,
        low_grad_part.reshape(2 * rows_dev, HEAD),
        grad_q,
        grad_kv,
        query_projection,
        key_value_projection,
        maps,
        sent,
        3,
    )
    grads = to_store(dim, served_row, returned, x_got, low_got, [s.shape for s in stores])
    return (
        output,
        hidden_input_gradient,
        jnp.swapaxes(grads[0], 1, 2),
        grads[1],
        grads[2],
        jnp.swapaxes(grads[3], 1, 2),
        grads[4],
    )


def solution(mesh):
    in_specs = (
        P("ctx", None),
        P("ctx", "tp"),
        P(None, "tp"),
        P(None, "tp"),
        P("tp", None),
        P("ctx", "tp", None),
        P("ctx", None, "tp"),
        P("ctx", None, "tp"),
        P("ctx", "tp", None),
        P("ctx", None, "tp"),
        P(),
        P(),
        P(),
    )
    out_specs = (
        P("ctx", "tp"),
        P("ctx", "tp"),
        P("ctx", "tp", None),
        P("ctx", None, "tp"),
        P("ctx", None, "tp"),
        P("ctx", "tp", None),
        P("ctx", None, "tp"),
    )
    return jax.shard_map(body, mesh=mesh, in_specs=in_specs, out_specs=out_specs, check_vma=False)
```
